256 devices in a mesh: req: 32 (over z_hi, x, y), tp: 8 (over z_lo, core).
Axes of the slice: x: 4, y: 4, z: 8 (z_hi: 2, z_lo: 4; z = z_hi * 4 + z_lo), core: 2. Of those that a mesh axis runs over, the one named last changes fastest.
Arguments:
- hidden: bfloat16 [4096, 2048], P('req', 'tp'), may hold values from -6 to 6
- attn_gain: bfloat16 [2048], replicated, may hold values from 0.099609375 to 1.8984375
- w_qkv: bfloat16 [3, 2048, 2048], P(None, None, 'tp'), may hold values from -0.125 to 0.125
- w_out: bfloat16 [2048, 2048], P('tp'), may hold values from -0.125 to 0.125
- kv_cache: bfloat16 [2, 32, 1024, 2048], P(None, 'req', None, 'tp'), as said below
- holder_slot: int32 [32], replicated, may hold values from 0 to 31, as said below
- lengths: int32 [32], P('req'), may hold values from 1 to 1024, as said below
- ffn_gain: bfloat16 [2048], replicated, may hold values from 0.099609375 to 1.8984375
- w_router: bfloat16 [2048, 32], replicated
- expert_ids: int32 [4096, 6], P('req'), may hold values from 0 to 31, all different within a row; in each aligned block of 128 rows (0 to 127, 128 to 255, ...) at most 32 rows name the same one
- w_exp_in: bfloat16 [32, 2, 2048, 1408], P('req', None, None, 'tp'), may hold values from -0.4375 to 0.4375
- w_exp_down: bfloat16 [32, 1408, 2048], P('req', 'tp'), may hold values from -0.5 to 0.5
- w_sh_in: bfloat16 [2, 2048, 1408], P(None, None, 'tp'), may hold values from -0.125 to 0.125
- w_sh_down: bfloat16 [1408, 2048], P('tp'), may hold values from -0.15625 to 0.15625
- final_gain: bfloat16 [2048], replicated, may hold values from 0.5 to 1.5
- w_head: bfloat16 [51200, 2048], P(('req', 'tp')), may hold values from -0.5 to 0.5
Outputs:
- out_hidden: bfloat16 [4096, 2048], P('req', 'tp')
- new_cache: bfloat16 [2, 32, 128, 2048], P(None, 'req', None, 'tp')
- last_rms: float32 [32], replicated
- top_logit: float32 [32], replicated
The draws below stay inside these ranges and needn't reach their ends.
Inputs may be any that keep to these rules, and one draw needn't show every extreme that they name: `kv_cache`: the cache in slot s lies on index s // 1 of req; request r is owned by index r. `holder_slot`: A permutation of the cache slots; about half of the requests keep their own slot. `lengths`: some request has exactly 1024 cached positions. `expert_ids`: within the rows of one device (128 aligned tokens) each expert is named by at most 32 rows, a bound that is reached.
All inputs are finite; a program needn't handle non-finite values.
Results may differ from the reference program's by a relative error of at most 0.025.
Values may be sent and summed in bfloat16 or wider, within the bound.
No kernel may reach another device: no remote copies, remote signals or barrier semaphores. Data moves between devices by JAX's collectives and lax.ppermute only.
A program may use at most 64 MiB of HBM per device.

```python
import math
import jax
import jax.numpy as jnp
import numpy as np
from jax import lax

D = 2048
HEADS = 16
HD = 128
EXPERTS = 32
FFE = 1408
SH = 1408
VOCAB = 51200
TOPK = 6
NEW = 128
REQ_DEV = 1
CTX = 1024
CAP = 32
REQS = 32
TOKENS = 4096
N_REQ = 32
N_TP = 8


def draw_kv_cache(key, part):
    base = jax.random.normal(key, (2, REQS, CTX, HEADS * HD), jnp.float32)
    return base.astype(jnp.bfloat16)


def draw_holder_slot(key, part):
    shuffled = jax.random.permutation(jax.random.fold_in(key, 21), REQS)
    movers = shuffled[:REQS // 2]
    inner_order = jax.random.permutation(jax.random.fold_in(key, 22), REQS // 2)
    slots = jnp.arange(REQS, dtype=jnp.int32)
    return slots.at[movers].set(movers[inner_order]).astype(jnp.int32)


def draw_lengths(key, part):
    values = jax.random.randint(jax.random.fold_in(key, 31), (REQS,), 1, CTX + 1)
    chosen = jax.random.randint(jax.random.fold_in(key, 32), (), 0, REQS)
    return jnp.where(jnp.arange(REQS) == chosen, CTX, values).astype(jnp.int32)


def draw_w_router(key, part):
    column_scale = jnp.exp(jax.random.uniform(jax.random.fold_in(key, 41), (EXPERTS,), jnp.float32, -0.35, 0.35))
    base = jax.random.normal(key, (D, EXPERTS), jnp.float32)
    return (base * (0.5 * D ** (-0.5)) * column_scale[None, :]).astype(jnp.bfloat16)


def steps_of(key, dims, pieces, smallest, top_value):
    loudness, own = 1.0, jax.random.fold_in(key, 6)
    for dim, blocks in pieces:
        draws = jnp.exp(jax.random.uniform(jax.random.fold_in(own, dim), (blocks,), jnp.float32, smallest / len(pieces), top_value / len(pieces)))
        loudness = loudness * jnp.repeat(draws, dims[dim] // blocks).reshape([-1 if axis == dim else 1 for axis in range(len(dims))])
    return loudness


def assign_block(stream_key, own, number, rows, amount, top, most, skew):
    ranking = jax.random.permutation(stream_key, amount)
    packed, ordinary = shares(amount, rows * top, most, skew, True), shares(amount, rows * top, most, skew, False)
    places = jnp.arange(amount)

    def named(sizes, offset_by):
        used = int((sizes > 0).sum())
        fixed = max(1, used // 4)
        shifted = fixed + (places - fixed + offset_by * (used - fixed)) % max(1, amount - fixed)
        return jnp.zeros((amount,), jnp.int32).at[ranking[jnp.where(places < fixed, places, shifted)]].set(jnp.asarray(sizes, jnp.int32))

    sizes = jnp.where(number % 4 == 0, named(packed, number // 4), named(ordinary, number - number // 4 - 1))
    mixed = jax.random.permutation(jax.random.fold_in(own, 3), amount)
    source_of, receiver = mixed[0:amount // 2 * 2:2], mixed[1:amount // 2 * 2:2]
    margin = jnp.minimum(sizes[source_of] - 1, most - sizes[receiver]) // 2
    margin = jnp.where((source_of == ranking[0]) | (receiver == ranking[0]) | (sizes[receiver] == 0), 0, jnp.maximum(margin, 0))
    shifted = jax.random.randint(jax.random.fold_in(own, 4), (amount // 2,), 0, 1 << 20) % (margin + 1)
    sizes = sizes.at[source_of].add(-shifted).at[receiver].add(shifted)
    items = jnp.searchsorted(jnp.cumsum(sizes), jnp.arange(rows * top), side="right").astype(jnp.int32)
    listing = items.reshape(top, rows).T
    listing = listing[jax.random.permutation(jax.random.fold_in(own, 1), rows)]
    offset_by = jax.random.randint(jax.random.fold_in(own, 2), (rows, 1), 0, top)
    return jnp.take_along_axis(listing, (jnp.arange(top)[None, :] + offset_by) % top, axis=1)


def shares(number_of, total, most, slope, full):
    loads = [(1 << 20) // math.isqrt(standing ** slope) + 1 for standing in range(1, number_of + 1)]
    largest = most if full else min(most, max(-(-total // number_of), total * loads[0] // sum(loads)))
    least = 1 if total - largest >= number_of - 1 else 0
    counts, surplus = [largest] + [least] * (number_of - 1), total - largest - least * (number_of - 1)
    while surplus > 0:
        free = [i for i in range(1, number_of) if counts[i] < largest] or [i for i in range(1, number_of) if counts[i] < most]
        pool, left = sum([loads[i] for i in free]), surplus
        for i in free:
            more = min(most - counts[i], max(1, left * loads[i] // pool), surplus)
            counts[i] = counts[i] + more
            surplus = surplus - more
    return np.array(counts)


def noise(stream_key, extent, scale, bound, split=(), kind=jnp.bfloat16):
    loudness = steps_of(stream_key, extent, split, -0.22, 0.18) if split else 1.0
    array = jax.random.normal(stream_key, extent, jnp.float32) * scale * loudness
    return jnp.minimum(jnp.maximum(array, -bound), bound).astype(kind)


def setup_inputs(seed: int = 0) -> dict:
    splits = jax.random.split(jax.random.key(seed), 17)
    hidden = noise(splits[0], (TOKENS, D), 1.0, 6.0, ((0, 32), (1, 8)))
    attn_gain = jnp.clip(1.0 + 0.18 * jax.random.normal(splits[1], (D,), jnp.float32), 0.099609375, 1.8984375).astype(jnp.bfloat16)
    w_qkv = noise(splits[2], (3, D, HEADS * HD), D ** -0.5, 0.125, ((2, 8),))
    w_out = noise(splits[3], (HEADS * HD, D), (HEADS * HD) ** -0.5, 0.125, ((0, 8),))
    kv_cache = draw_kv_cache(jax.random.fold_in(splits[16], 71), 0)
    holder_slot = draw_holder_slot(jax.random.fold_in(splits[16], 71), 0)
    lengths = draw_lengths(jax.random.fold_in(splits[16], 71), 0)
    ffn_gain = jnp.clip(1.0 + 0.18 * jax.random.normal(splits[7], (D,), jnp.float32), 0.099609375, 1.8984375).astype(jnp.bfloat16)
    w_router = draw_w_router(jax.random.fold_in(splits[16], 71), 0)
    expert_ids_keys = jax.random.split(jax.random.fold_in(splits[9], 1), TOKENS // (REQ_DEV * NEW))
    expert_ids_turns = jax.random.permutation(jax.random.fold_in(splits[9], 3), TOKENS // (REQ_DEV * NEW))
    expert_ids = jax.vmap(lambda own, number: assign_block(jax.random.fold_in(splits[9], 2), own, number, REQ_DEV * NEW, EXPERTS, TOPK, CAP, 1))(expert_ids_keys, expert_ids_turns).reshape((TOKENS, TOPK))
    w_exp_in = noise(splits[10], (EXPERTS, 2, D, FFE), (D // 10) ** -0.5, 0.4375, ((0, 32), (3, 8)))
    w_exp_down = noise(splits[11], (EXPERTS, FFE, D), (FFE // 10) ** -0.5, 0.5, ((0, 32), (1, 8)))
    w_sh_in = noise(splits[12], (2, D, SH), D ** -0.5, 0.125, ((2, 8),))
    w_sh_down = noise(splits[13], (SH, D), SH ** -0.5, 0.15625, ((0, 8),))
    final_gain = jnp.clip(1.0 + 0.1 * jax.random.normal(splits[14], (D,), jnp.float32), 0.5, 1.5).astype(jnp.bfloat16)
    w_head = noise(splits[15], (VOCAB, D), 0.08, 0.5, ((0, 256),))
    return {"hidden": hidden, "attn_gain": attn_gain, "w_qkv": w_qkv, "w_out": w_out, "kv_cache": kv_cache, "holder_slot": holder_slot, "lengths": lengths, "ffn_gain": ffn_gain, "w_router": w_router, "expert_ids": expert_ids, "w_exp_in": w_exp_in, "w_exp_down": w_exp_down, "w_sh_in": w_sh_in, "w_sh_down": w_sh_down, "final_gain": final_gain, "w_head": w_head}


epsilon = 1e-06

def rms_scale(values, gain):
    return values * lax.rsqrt(lax.optimization_barrier(jnp.mean(values * values, axis=-1, keepdims=True)) + epsilon) * gain.astype(jnp.float32)

def rotate_half(values, positions):
    half_len = values.shape[-1] // 2
    freqs = 10000.0 ** (-2.0 * jnp.arange(half_len, dtype=jnp.float32) / values.shape[-1])
    angles = positions[..., None] * freqs
    cosine = jnp.cos(angles)[..., None, :]
    sine = jnp.sin(angles)[..., None, :]
    lead_half = values[..., :half_len]
    tail_half = values[..., half_len:]
    return jnp.concatenate([lead_half * cosine - tail_half * sine, tail_half * cosine + lead_half * sine], axis=-1)

def attend(queries, keys_new, values_new, old_keys, old_values, lengths):
    context_len = old_keys.shape[1]
    new_len = queries.shape[1]
    all_keys = jnp.concatenate([old_keys, keys_new], axis=1).astype(jnp.float32)
    all_values = jnp.concatenate([old_values, values_new], axis=1).astype(jnp.float32)
    scores = jnp.einsum('rthd,rshd->rhts', queries.astype(jnp.float32), all_keys) * queries.shape[-1] ** (-0.5)
    column = jnp.arange(context_len + new_len)[None, None, :]
    row_pos = jnp.arange(new_len)[None, :, None]
    visible = jnp.where(column < context_len, column < lengths[:, None, None], column - context_len <= row_pos)
    visible = visible[:, None]
    masked = jnp.where(visible, scores, -1e+30)
    peak = lax.optimization_barrier(jnp.max(masked, axis=-1, keepdims=True))
    raised = jnp.where(visible, jnp.exp(masked - peak), 0.0)
    weights = (raised / lax.optimization_barrier(jnp.sum(raised, axis=-1, keepdims=True))).astype(jnp.bfloat16)
    mixed = jnp.einsum('rhts,rshd->rthd', weights.astype(jnp.float32), all_values)
    return mixed.astype(jnp.bfloat16)

def reference(hidden, attn_gain, w_qkv, w_out, kv_cache, holder_slot, lengths, ffn_gain, w_router, expert_ids, w_exp_in, w_exp_down, w_sh_in, w_sh_down, final_gain, w_head):
    normed = rms_scale(hidden.astype(jnp.float32), attn_gain).astype(jnp.bfloat16)
    projected = jnp.stack([jnp.dot(normed, w_qkv[member], preferred_element_type=jnp.float32) for member in range(3)])
    positions = (lengths[:, None] + jnp.arange(NEW, dtype=jnp.int32)[None, :]).astype(jnp.float32)
    shaped = projected.reshape(3, REQS, NEW, HEADS, HD)
    queries = rotate_half(shaped[0], positions).astype(jnp.bfloat16)
    keys_new = rotate_half(shaped[1], positions).astype(jnp.bfloat16)
    values_new = shaped[2].astype(jnp.bfloat16)
    new_cache = jnp.stack([keys_new, values_new]).reshape(2, REQS, NEW, HEADS * HD)
    fetched = jnp.take(kv_cache, holder_slot, axis=1).reshape(2, REQS, CTX, HEADS, HD)

    def one_request(items):
        return attend(*[item[None] for item in items])[0]
    attn_out = lax.map(one_request, (queries, keys_new, values_new, fetched[0], fetched[1], lengths))
    attn_out = attn_out.reshape(TOKENS, HEADS * HD)
    resid = (hidden.astype(jnp.float32) + jnp.dot(attn_out, w_out, preferred_element_type=jnp.float32)).astype(jnp.bfloat16)
    ffn_in = rms_scale(resid.astype(jnp.float32), ffn_gain).astype(jnp.bfloat16)
    probs = jax.nn.softmax(jnp.dot(ffn_in, w_router, preferred_element_type=jnp.float32), axis=-1)
    gates = jnp.take_along_axis(probs, expert_ids, axis=1)
    shared_gate = jnp.dot(ffn_in, w_sh_in[0], preferred_element_type=jnp.float32)
    shared_up = jnp.dot(ffn_in, w_sh_in[1], preferred_element_type=jnp.float32)
    shared_inner = (jax.nn.silu(shared_gate) * shared_up).astype(jnp.bfloat16)
    shared_out = jnp.dot(shared_inner, w_sh_down, preferred_element_type=jnp.float32)
    picks = expert_ids.reshape(-1)
    gate_flat = gates.reshape(-1)
    limit = N_REQ * CAP
    unit_block = FFE // N_TP

    def one_expert(expert, totals):
        picked = jnp.argsort((picks != expert).astype(jnp.int32), stable=True)[:limit]
        live = (picks[picked] == expert).astype(jnp.float32)
        token = picked // TOPK
        rows_in = jnp.take(ffn_in, token, axis=0)
        gate_part = jnp.dot(rows_in, w_exp_in[expert, 0], preferred_element_type=jnp.float32)
        up_part = jnp.dot(rows_in, w_exp_in[expert, 1], preferred_element_type=jnp.float32)
        inner = (jax.nn.silu(gate_part) * up_part).astype(jnp.bfloat16)
        blocks = inner.reshape(limit, N_TP, unit_block).astype(jnp.float32)
        down = w_exp_down[expert].reshape(N_TP, unit_block, D).astype(jnp.float32)
        partial_value = jnp.einsum('rtf,tfd->trd', blocks, down)
        partial_value = lax.optimization_barrier(partial_value.astype(jnp.bfloat16)).astype(jnp.float32)
        merged = lax.optimization_barrier(jnp.sum(partial_value, axis=0))
        return totals.at[token].add((gate_flat[picked] * live)[:, None] * merged)
    routed = lax.fori_loop(0, EXPERTS, one_expert, jnp.zeros((TOKENS, D), jnp.float32))
    out_hidden = (resid.astype(jnp.float32) + shared_out + routed).astype(jnp.bfloat16)
    last_tok = out_hidden.reshape(REQS, NEW, D)[:, NEW - 1].astype(jnp.float32)
    last_rms = jnp.sqrt(lax.optimization_barrier(jnp.mean(last_tok * last_tok, axis=-1)) + epsilon)
    head_in = (last_tok / last_rms[:, None] * final_gain.astype(jnp.float32)).astype(jnp.bfloat16)
    logits = lax.dot_general(head_in, w_head, (((1,), (1,)), ((), ())), preferred_element_type=jnp.float32)
    top_logit = lax.optimization_barrier(jnp.max(logits, axis=1))
    return (out_hidden, new_cache, last_rms, top_logit)
```

```python
import jax
import jax.numpy as jnp
from jax import lax
from jax.sharding import Mesh, PartitionSpec as P
from jax.experimental import pallas as pl
from jax.experimental.pallas import tpu as pltpu

HD = 128
TOPK = 6
CAP = 32

REQ = ("zh", "x", "y")
TP = ("zl", "core")
COL = ("zh", "zl", "core")
Z = ("zh", "zl")
ALL = ("zh", "x", "y", "zl", "core")
SIZES = (2, 4, 4, 4, 2)

epsilon = 1e-06
bf16 = jnp.bfloat16
f32 = jnp.float32


def rms_scale(values, gain):
    return (
        values
        * lax.rsqrt(jnp.mean(values * values, axis=-1, keepdims=True) + epsilon)
        * gain.astype(f32)
    )


def rotate_half(values, positions):
    half_len = values.shape[-1] // 2
    freqs = 10000.0 ** (-2.0 * jnp.arange(half_len, dtype=f32) / values.shape[-1])
    angles = positions[..., None] * freqs
    cosine = jnp.cos(angles)[..., None, :]
    sine = jnp.sin(angles)[..., None, :]
    lead_half = values[..., :half_len]
    tail_half = values[..., half_len:]
    return jnp.concatenate(
        [lead_half * cosine - tail_half * sine, tail_half * cosine + lead_half * sine], axis=-1
    )


def attend_body(len_ref, q_ref, k_ref, v_ref, old_ref, w_ref, o_ref):
    length = len_ref[0]
    parts, _, span, _ = old_ref.shape
    ctx = parts * span
    new = q_ref.shape[0]
    nt = (((1,), (1,)), ((), ()))
    heads = []
    for head in range(q_ref.shape[1] // HD):
        lanes = slice(head * HD, (head + 1) * HD)
        q = q_ref[:, lanes]
        old_k = old_ref[:, 0, :, lanes].reshape(ctx, HD)
        old_v = old_ref[:, 1, :, lanes].reshape(ctx, HD)
        s_old = lax.dot_general(q, old_k, nt, preferred_element_type=f32) * HD ** (-0.5)
        s_new = lax.dot_general(q, k_ref[:, lanes], nt, preferred_element_type=f32) * HD ** (-0.5)
        seen_old = lax.broadcasted_iota(jnp.int32, (new, ctx), 1) < length
        seen_new = lax.broadcasted_iota(jnp.int32, (new, new), 1) <= lax.broadcasted_iota(
            jnp.int32, (new, new), 0
        )
        s_old = jnp.where(seen_old, s_old, -1e30)
        s_new = jnp.where(seen_new, s_new, -1e30)
        peak = jnp.maximum(
            jnp.max(s_old, axis=-1, keepdims=True), jnp.max(s_new, axis=-1, keepdims=True)
        )
        e_old = jnp.where(seen_old, jnp.exp(s_old - peak), 0.0)
        e_new = jnp.where(seen_new, jnp.exp(s_new - peak), 0.0)
        total = jnp.sum(e_old, axis=-1, keepdims=True) + jnp.sum(e_new, axis=-1, keepdims=True)
        w_old = (e_old / total).astype(bf16)
        w_new = (e_new / total).astype(bf16)
        out = jnp.dot(w_old, old_v, preferred_element_type=f32) + jnp.dot(
            w_new, v_ref[:, lanes], preferred_element_type=f32
        )
        heads.append(out.astype(bf16))
    attn = jnp.concatenate(heads, axis=1)
    wide = o_ref.shape[2]
    for part in range(o_ref.shape[0]):
        o_ref[part] = jnp.dot(
            attn, w_ref[:, part * wide : (part + 1) * wide], preferred_element_type=f32
        ).astype(bf16)


def attend(lengths, q, k, v, old, w_out):
    vm = pl.BlockSpec(memory_space=pltpu.VMEM)
    new, feat = q.shape
    return pl.pallas_call(
        attend_body,
        out_shape=jax.ShapeDtypeStruct((w_out.shape[1] // feat, new, feat), bf16),
        in_specs=[pl.BlockSpec(memory_space=pltpu.SMEM), vm, vm, vm, vm, vm],
        out_specs=vm,
        name="attend",
    )(lengths, q, k, v, old, w_out)


def expert_body(
    place_ref, a_ref, b_ref, gain_ref, router_ref, in_ref, down_ref, om_ref, ot_ref, x_ref, routed
):
    first = place_ref[0] == 0
    width = x_ref.shape[1]
    feat = width // 8

    def fill(even_ref, odd_ref):
        for part in range(4):
            piece = slice(part * feat, (part + 1) * feat)
            x_ref[:, 2 * part * feat : (2 * part + 1) * feat] = even_ref[:, piece]
            x_ref[:, (2 * part + 1) * feat : (2 * part + 2) * feat] = odd_ref[:, piece]

    @pl.when(first)
    def _():
        fill(a_ref, b_ref)

    @pl.when(jnp.logical_not(first))
    def _():
        fill(b_ref, a_ref)

    x = x_ref[...].astype(f32)
    scale = lax.rsqrt(jnp.mean(x * x, axis=-1, keepdims=True) + epsilon)
    rows = (x * scale * gain_ref[...].astype(f32)).astype(bf16)
    gate = jnp.dot(rows, in_ref[0], preferred_element_type=f32)
    up = jnp.dot(rows, in_ref[1], preferred_element_type=f32)
    inner = (gate / (1.0 + jnp.exp(-gate)) * up).astype(bf16)
    out = jnp.dot(inner, down_ref[...], preferred_element_type=f32)
    if routed:
        logits = jnp.dot(rows, router_ref[...], preferred_element_type=f32)
        raised = jnp.exp(logits - jnp.max(logits, axis=-1, keepdims=True))
        own = lax.broadcasted_iota(jnp.int32, logits.shape, 1) == place_ref[1]
        picked = jnp.sum(jnp.where(own, raised, 0.0), axis=-1, keepdims=True)
        out = out * (picked / jnp.sum(raised, axis=-1, keepdims=True))
    out = out.astype(bf16)

    def drain(even_ref, odd_ref):
        for part in range(4):
            piece = slice(part * feat, (part + 1) * feat)
            even_ref[:, piece] = out[:, 2 * part * feat : (2 * part + 1) * feat]
            odd_ref[:, piece] = out[:, (2 * part + 1) * feat : (2 * part + 2) * feat]

    @pl.when(first)
    def _():
        drain(om_ref, ot_ref)

    @pl.when(jnp.logical_not(first))
    def _():
        drain(ot_ref, om_ref)


def expert_mlp(place, rows_mine, rows_theirs, gain, w_router, w_in, w_down, block, routed):
    count, half = rows_mine.shape
    width = 2 * half
    hidden = w_down.shape[0]
    row_spec = pl.BlockSpec((block, half), lambda i: (i, 0))

    def whole(array):
        zeros = (0,) * array.ndim
        return pl.BlockSpec(array.shape, lambda i: zeros)

    shape = jax.ShapeDtypeStruct((count, half), bf16)

    def body(*refs):
        expert_body(*refs, routed)

    return pl.pallas_call(
        body,
        grid=(count // block,),
        out_shape=(shape, shape),
        in_specs=[
            pl.BlockSpec(memory_space=pltpu.SMEM),
            row_spec,
            row_spec,
            whole(gain),
            whole(w_router),
            whole(w_in),
            whole(w_down),
        ],
        out_specs=(row_spec, row_spec),
        scratch_shapes=[pltpu.VMEM((block, width), bf16)],
        cost_estimate=pl.CostEstimate(
            flops=6 * count * width * hidden,
            transcendentals=count * hidden,
            bytes_accessed=8 * count * half + 6 * width * hidden,
        ),
        name="routed_mlp" if routed else "shared_mlp",
    )(place, rows_mine, rows_theirs, gain, w_router, w_in, w_down)


def head_body(last_ref, gain_ref, w_ref, top_ref, rms_ref):
    rows, width = last_ref.shape
    plane = rows // 2
    feat = width // 8
    halves = []
    for zo in range(2):
        pieces = []
        for part in range(4):
            for core in range(2):
                lanes = slice((zo * 4 + part) * feat, (zo * 4 + part + 1) * feat)
                pieces.append(last_ref[core * plane : (core + 1) * plane, lanes])
        halves.append(jnp.concatenate(pieces, axis=1))
    tok = jnp.concatenate(halves, axis=0).astype(f32)
    rms = jnp.sqrt(jnp.mean(tok * tok, axis=-1, keepdims=True) + epsilon)
    head_in = (tok / rms * gain_ref[...].astype(f32)).astype(bf16)
    logits = lax.dot_general(
        w_ref[...], head_in, (((1,), (1,)), ((), ())), preferred_element_type=f32
    )
    top_ref[...] = jnp.broadcast_to(jnp.max(logits, axis=0, keepdims=True), top_ref.shape)
    rms_ref[...] = rms


def head(last, gain, w_head):
    vm = pl.BlockSpec(memory_space=pltpu.VMEM)
    rows = last.shape[0]
    return pl.pallas_call(
        head_body,
        out_shape=(
            jax.ShapeDtypeStruct((256, rows), f32),
            jax.ShapeDtypeStruct((rows, 1), f32),
        ),
        in_specs=[vm, vm, vm],
        out_specs=(vm, vm),
        name="head",
    )(last, gain, w_head)


def spread(value, axes, count):
    wide = jnp.broadcast_to(value[None], (count,) + value.shape)
    return lax.all_to_all(wide, axes, 0, 0, tiled=True)


def swap_core(value):
    return lax.ppermute(value, "core", [(0, 1), (1, 0)])


def local(
    hidden,
    attn_gain,
    w_qkv,
    w_out,
    kv_cache,
    holder_slot,
    lengths,
    ffn_gain,
    w_router,
    expert_ids,
    w_exp_in,
    w_exp_down,
    w_sh_in,
    w_sh_down,
    final_gain,
    w_head,
):
    zh = lax.axis_index("zh")
    zl = lax.axis_index("zl")
    core = lax.axis_index("core")
    expert = lax.axis_index(REQ)
    new, feat = hidden.shape
    width = attn_gain.shape[0]
    half = width // 2
    experts_all = w_router.shape[1]
    plane = experts_all // 2
    slots = plane * 2 * CAP

    reqs = holder_slot.shape[0]
    ctx = kv_cache.shape[2]
    pieces = kv_cache.reshape(2, reqs, ctx // reqs, feat).transpose(1, 0, 2, 3)
    leg = lax.all_to_all(pieces, REQ, 0, 0, tiled=True)
    leg = leg.at[holder_slot].get(mode="promise_in_bounds")
    old = lax.all_to_all(leg, REQ, 0, 0, tiled=True)

    ids_there = lax.ppermute(expert_ids, "zh", [(0, 1), (1, 0)])
    own = lax.all_gather(hidden, TP, axis=1, tiled=True)
    normed = rms_scale(own.astype(f32), attn_gain).astype(bf16)
    projected = jnp.einsum("td,cde->cte", normed, w_qkv, preferred_element_type=f32)
    positions = (lengths[:, None] + jnp.arange(new, dtype=jnp.int32)[None, :]).astype(f32)
    shaped = projected.reshape(3, 1, new, feat // HD, HD)
    queries = rotate_half(shaped[0], positions).astype(bf16).reshape(new, feat)
    keys_new = rotate_half(shaped[1], positions).astype(bf16).reshape(new, feat)
    values_new = shaped[2].astype(bf16).reshape(new, feat)
    new_cache = jnp.stack([keys_new, values_new])[:, None]

    parts = attend(lengths, queries, keys_new, values_new, old, w_out)
    parts = lax.all_to_all(parts, TP, 0, 0, tiled=True)
    attn_total = jnp.sum(parts.astype(f32), axis=0)
    resid_share = (hidden.astype(f32) + attn_total).astype(bf16)
    resid = spread(resid_share, Z, 8).reshape(2, 4, new, feat)
    resid = resid.transpose(0, 2, 1, 3).reshape(2 * new, half)

    ids = jnp.where(
        zh == 0, jnp.stack([expert_ids, ids_there]), jnp.stack([ids_there, expert_ids])
    )
    picks = ids.reshape(2, new * TOPK)
    onehot = (picks[:, :, None] == jnp.arange(experts_all, dtype=jnp.int32)).astype(bf16)
    order = jnp.arange(new * TOPK, dtype=jnp.int32)
    before = (order[:, None] > order[None, :]).astype(bf16)
    earlier = jnp.einsum("pq,rqe->rpe", before, onehot, preferred_element_type=f32)
    rank = jnp.sum(earlier * onehot.astype(f32), axis=2).astype(jnp.int32)
    there = picks - zh * plane
    slot = (there * 2 + jnp.arange(2, dtype=jnp.int32)[:, None]) * CAP + rank
    slot = jnp.where((there >= 0) & (there < plane), slot, -1).reshape(2 * new, TOPK)
    slot_iota = jnp.arange(slots, dtype=jnp.int32)
    chosen = jnp.zeros((2 * new, slots), bf16)
    for pick in range(TOPK):
        chosen = chosen + (slot[:, pick : pick + 1] == slot_iota[None, :]).astype(bf16)

    outgoing = lax.dot_general(
        chosen, resid, (((0,), (0,)), ((), ())), preferred_element_type=f32
    ).astype(bf16)
    rows_mine = lax.all_to_all(
        outgoing.reshape(plane, 2 * CAP, half), ("x", "y"), 0, 0, tiled=True
    ).reshape(slots, half)
    rows_theirs = swap_core(rows_mine)

    place = jnp.stack([core, expert]).astype(jnp.int32)
    gain = ffn_gain[None]
    own_mine = lax.dynamic_slice_in_dim(resid, zh * new, new, 0)
    shared_mine, shared_theirs = expert_mlp(
        place, own_mine, swap_core(own_mine), gain, w_router, w_sh_in, w_sh_down, new, False
    )
    shared = shared_mine.astype(f32) + swap_core(shared_theirs).astype(f32)

    served_mine, served_theirs = expert_mlp(
        place, rows_mine, rows_theirs, gain, w_router, w_exp_in[0], w_exp_down[0], 256, True
    )
    served = (served_mine.astype(f32) + swap_core(served_theirs).astype(f32)).astype(bf16)
    returned = lax.all_to_all(
        served.reshape(plane, 2 * CAP, half), ("x", "y"), 0, 0, tiled=True
    ).reshape(slots, half)
    share = jnp.dot(chosen, returned, preferred_element_type=f32).reshape(2, new, half)
    is_own = (jnp.arange(2) == zh)[:, None, None]
    share = (share + jnp.where(is_own, shared[None], 0.0)).astype(bf16)

    cut = share.reshape(2, new, 4, feat).transpose(0, 2, 1, 3).reshape(8, new, feat)
    last = share[:, new - 1].reshape(1, 8, feat)
    packed = jnp.concatenate([cut, jnp.broadcast_to(last, (8, 8, feat))], axis=1)
    summed = jnp.sum(lax.all_to_all(packed, Z, 0, 0, tiled=True).astype(f32), axis=0)
    out_hidden = (resid_share.astype(f32) + summed[:new]).astype(bf16)
    last_resid = resid.reshape(2, new, half)[:, new - 1].astype(f32)
    last_half = (last_resid + summed[new:].reshape(2, half)).astype(bf16)

    last_all = spread(last_half.reshape(width), ("core", "x", "y"), reqs)
    tops, rms = head(last_all, final_gain[None], w_head)
    last_rms = rms.reshape(reqs)
    top_logit = jnp.max(lax.all_to_all(tops, ALL, 0, 0, tiled=True), axis=0)
    return (out_hidden, new_cache, last_rms, top_logit)


def solution(mesh):
    fine = Mesh(mesh.devices.reshape(SIZES), ALL)
    return jax.shard_map(
        local,
        mesh=fine,
        in_specs=(
            P(REQ, TP),
            P(),
            P(None, None, TP),
            P(TP, None),
            P(None, REQ, None, TP),
            P(),
            P(REQ),
            P(),
            P(),
            P(REQ, None),
            P(REQ, None, None, TP),
            P(REQ, TP, None),
            P(None, None, TP),
            P(TP, None),
            P(),
            P(REQ + TP, None),
        ),
        out_specs=(P(REQ, TP), P(None, REQ, None, TP), P(), P()),
        check_vma=False,
    )
```

```python
import jax
import jax.numpy as jnp
from jax import lax
from jax.sharding import Mesh, PartitionSpec as P
from jax.experimental import pallas as pl
from jax.experimental.pallas import tpu as pltpu

HD = 128
TOPK = 6
CAP = 32
SHARE = CAP // 2

REQ = ("zh", "x", "y")
TP = ("zl", "core")
COL = ("zh", "zl", "core")
Z = ("zh", "zl")
ALL = ("zh", "x", "y", "zl", "core")
SIZES = (2, 4, 4, 4, 2)

epsilon = 1e-06
bf16 = jnp.bfloat16
f32 = jnp.float32


def rms_scale(values, gain):
    return (
        values
        * lax.rsqrt(jnp.mean(values * values, axis=-1, keepdims=True) + epsilon)
        * gain.astype(f32)
    )


def rotate_half(values, positions):
    half_len = values.shape[-1] // 2
    freqs = 10000.0 ** (-2.0 * jnp.arange(half_len, dtype=f32) / values.shape[-1])
    angles = positions[..., None] * freqs
    cosine = jnp.cos(angles)[..., None, :]
    sine = jnp.sin(angles)[..., None, :]
    lead_half = values[..., :half_len]
    tail_half = values[..., half_len:]
    return jnp.concatenate(
        [lead_half * cosine - tail_half * sine, tail_half * cosine + lead_half * sine], axis=-1
    )


def attend_body(len_ref, q_ref, k_ref, v_ref, old_ref, w_ref, o_ref):
    length = len_ref[0]
    parts, _, span, _ = old_ref.shape
    ctx = parts * span
    new = q_ref.shape[0]
    nt = (((1,), (1,)), ((), ()))
    heads = []
    for head in range(q_ref.shape[1] // HD):
        lanes = slice(head * HD, (head + 1) * HD)
        q = q_ref[:, lanes]
        old_k = old_ref[:, 0, :, lanes].reshape(ctx, HD)
        old_v = old_ref[:, 1, :, lanes].reshape(ctx, HD)
        s_old = lax.dot_general(q, old_k, nt, preferred_element_type=f32) * HD ** (-0.5)
        s_new = lax.dot_general(q, k_ref[:, lanes], nt, preferred_element_type=f32) * HD ** (-0.5)
        seen_old = lax.broadcasted_iota(jnp.int32, (new, ctx), 1) < length
        seen_new = lax.broadcasted_iota(jnp.int32, (new, new), 1) <= lax.broadcasted_iota(
            jnp.int32, (new, new), 0
        )
        s_old = jnp.where(seen_old, s_old, -1e30)
        s_new = jnp.where(seen_new, s_new, -1e30)
        peak = jnp.maximum(
            jnp.max(s_old, axis=-1, keepdims=True), jnp.max(s_new, axis=-1, keepdims=True)
        )
        e_old = jnp.where(seen_old, jnp.exp(s_old - peak), 0.0)
        e_new = jnp.where(seen_new, jnp.exp(s_new - peak), 0.0)
        total = jnp.sum(e_old, axis=-1, keepdims=True) + jnp.sum(e_new, axis=-1, keepdims=True)
        w_old = (e_old / total).astype(bf16)
        w_new = (e_new / total).astype(bf16)
        out = jnp.dot(w_old, old_v, preferred_element_type=f32) + jnp.dot(
            w_new, v_ref[:, lanes], preferred_element_type=f32
        )
        heads.append(out.astype(bf16))
    attn = jnp.concatenate(heads, axis=1)
    wide = o_ref.shape[2]
    for part in range(o_ref.shape[0]):
        o_ref[part] = jnp.dot(
            attn, w_ref[:, part * wide : (part + 1) * wide], preferred_element_type=f32
        ).astype(bf16)


def attend(lengths, q, k, v, old, w_out):
    vm = pl.BlockSpec(memory_space=pltpu.VMEM)
    new, feat = q.shape
    return pl.pallas_call(
        attend_body,
        out_shape=jax.ShapeDtypeStruct((w_out.shape[1] // feat, new, feat), bf16),
        in_specs=[pl.BlockSpec(memory_space=pltpu.SMEM), vm, vm, vm, vm, vm],
        out_specs=vm,
        name="attend",
    )(lengths, q, k, v, old, w_out)


def dot_nt(a, b):
    return lax.dot_general(a, b, (((1,), (1,)), ((), ())), preferred_element_type=f32)


def expert_body(place_ref, a_ref, b_ref, gain_ref, router_ref, *refs, routed):
    om_ref, ot_ref, x_ref = refs[-3:]
    weights = refs[:-3]
    first = place_ref[0] == 0
    width = x_ref.shape[1]
    feat = width // 8

    def fill(even_ref, odd_ref):
        for part in range(4):
            piece = slice(part * feat, (part + 1) * feat)
            x_ref[:, 2 * part * feat : (2 * part + 1) * feat] = even_ref[:, piece]
            x_ref[:, (2 * part + 1) * feat : (2 * part + 2) * feat] = odd_ref[:, piece]

    @pl.when(first)
    def _():
        fill(a_ref, b_ref)

    @pl.when(jnp.logical_not(first))
    def _():
        fill(b_ref, a_ref)

    x = x_ref[...].astype(f32)
    scale = lax.rsqrt(jnp.mean(x * x, axis=-1, keepdims=True) + epsilon)
    rows = (x * scale * gain_ref[...].astype(f32)).astype(bf16)
    out = None
    for i in range(0, len(weights), 2):
        in_ref, down_ref = weights[i : i + 2]
        gate = dot_nt(rows, in_ref[0])
        up = dot_nt(rows, in_ref[1])
        inner = (gate / (1.0 + jnp.exp(-gate)) * up).astype(bf16)
        term = jnp.dot(inner, down_ref[...], preferred_element_type=f32)
        out = term if out is None else out + term
    if routed:
        logits = dot_nt(rows, router_ref[...])
        raised = jnp.exp(logits - jnp.max(logits, axis=-1, keepdims=True))
        own = lax.broadcasted_iota(jnp.int32, logits.shape, 1) == place_ref[1]
        picked = jnp.sum(jnp.where(own, raised, 0.0), axis=-1, keepdims=True)
        out = out * (picked / jnp.sum(raised, axis=-1, keepdims=True))
    out = out.astype(bf16)

    def drain(even_ref, odd_ref):
        for part in range(4):
            piece = slice(part * feat, (part + 1) * feat)
            even_ref[:, piece] = out[:, 2 * part * feat : (2 * part + 1) * feat]
            odd_ref[:, piece] = out[:, (2 * part + 1) * feat : (2 * part + 2) * feat]

    @pl.when(first)
    def _():
        drain(om_ref, ot_ref)

    @pl.when(jnp.logical_not(first))
    def _():
        drain(ot_ref, om_ref)


def expert_mlp(place, rows_mine, rows_theirs, gain, router, weights, block, routed):
    count, half = rows_mine.shape
    width = 2 * half
    hidden = sum(w.shape[0] for w in weights[1::2])
    row_spec = pl.BlockSpec((block, half), lambda i: (i, 0))

    def whole(array):
        zeros = (0,) * array.ndim
        return pl.BlockSpec(array.shape, lambda i: zeros)

    shape = jax.ShapeDtypeStruct((count, half), bf16)

    def body(*refs):
        expert_body(*refs, routed=routed)

    return pl.pallas_call(
        body,
        grid=(count // block,),
        out_shape=(shape, shape),
        in_specs=[pl.BlockSpec(memory_space=pltpu.SMEM), row_spec, row_spec]
        + [whole(array) for array in (gain, router) + weights],
        out_specs=(row_spec, row_spec),
        scratch_shapes=[pltpu.VMEM((block, width), bf16)],
        cost_estimate=pl.CostEstimate(
            flops=6 * count * width * hidden,
            transcendentals=count * hidden,
            bytes_accessed=8 * count * half + 6 * width * hidden,
        ),
        name="routed_mlp" if routed else "shared_mlp",
    )(place, rows_mine, rows_theirs, gain, router, *weights)


def dispatch_body(chosen_ref, parts_ref, out_ref, rows_ref):
    new, feat = parts_ref.shape[1:]
    for part in range(4):
        lanes = slice(part * feat, (part + 1) * feat)
        both = jnp.concatenate([parts_ref[part], parts_ref[4 + part]], axis=0)
        rows_ref[:, lanes] = both
        out_ref[:, lanes] = jnp.dot(
            chosen_ref[...], both, preferred_element_type=f32
        ).astype(bf16)


def dispatch(chosen_t, parts):
    vm = pl.BlockSpec(memory_space=pltpu.VMEM)
    slots, tokens = chosen_t.shape
    half = 4 * parts.shape[2]
    return pl.pallas_call(
        dispatch_body,
        out_shape=(
            jax.ShapeDtypeStruct((slots, half), bf16),
            jax.ShapeDtypeStruct((tokens, half), bf16),
        ),
        in_specs=[vm, vm],
        out_specs=(vm, vm),
        name="dispatch",
    )(chosen_t, parts)


def combine_body(place_ref, chosen_ref, back_ref, mine_ref, theirs_ref, out_ref):
    tokens = chosen_ref.shape[0]
    new = tokens // 2
    feat = out_ref.shape[2]
    for zo in range(2):
        own = (place_ref[2] == zo).astype(f32)
        total = jnp.dot(
            chosen_ref[zo * new : (zo + 1) * new, :], back_ref[...], preferred_element_type=f32
        )
        total = total + own * (mine_ref[...].astype(f32) + theirs_ref[...].astype(f32))
        for part in range(4):
            piece = total[:, part * feat : (part + 1) * feat]
            out_ref[zo * 4 + part, :new, :] = piece.astype(bf16)
            row = piece[new - 1 :, :].astype(bf16)
            for dest in range(8):
                out_ref[dest, new + zo * 4 + part : new + zo * 4 + part + 1, :] = row


def combine(place, chosen, back, mine, theirs):
    vm = pl.BlockSpec(memory_space=pltpu.VMEM)
    tokens = chosen.shape[0]
    half = back.shape[1]
    return pl.pallas_call(
        combine_body,
        out_shape=jax.ShapeDtypeStruct((8, tokens // 2 + 8, half // 4), bf16),
        in_specs=[pl.BlockSpec(memory_space=pltpu.SMEM), vm, vm, vm, vm],
        out_specs=vm,
        name="combine",
    )(place, chosen, back, mine, theirs)


def finish_body(parts_ref, share_ref, resid_ref, out_ref, last_ref):
    new, feat = share_ref.shape
    total = parts_ref[0].astype(f32)
    for part in range(1, 8):
        total = total + parts_ref[part].astype(f32)
    out_ref[...] = (share_ref[...].astype(f32) + total[:new]).astype(bf16)
    for zo in range(2):
        for part in range(4):
            lanes = slice(part * feat, (part + 1) * feat)
            tail = resid_ref[(zo + 1) * new - 16 : (zo + 1) * new, lanes].astype(f32)
            at = new + zo * 4 + part
            row = tail[15:16] + total[at : at + 1]
            for sub in range(2):
                r = (zo * 4 + part) * 2 + sub
                piece = row[:, sub * 128 : (sub + 1) * 128]
                last_ref[:, r : r + 1, :] = jnp.broadcast_to(
                    piece.astype(bf16)[None], (last_ref.shape[0], 1, 128)
                )


def finish(parts, share, resid, copies):
    vm = pl.BlockSpec(memory_space=pltpu.VMEM)
    return pl.pallas_call(
        finish_body,
        out_shape=(
            jax.ShapeDtypeStruct(share.shape, bf16),
            jax.ShapeDtypeStruct((copies, 16, 128), bf16),
        ),
        in_specs=[vm, vm, vm],
        out_specs=(vm, vm),
        name="finish",
    )(parts, share, resid)


def head_body(last_ref, gain_ref, w_ref, top_ref, rms_ref):
    plane = last_ref.shape[0] // 2
    rows = jnp.swapaxes(last_ref[...].astype(f32), 0, 1)
    halves = []
    for zo in range(2):
        pieces = []
        for part in range(4):
            for core in range(2):
                for sub in range(2):
                    pieces.append(
                        rows[(zo * 4 + part) * 2 + sub, core * plane : (core + 1) * plane]
                    )
        halves.append(jnp.concatenate(pieces, axis=1))
    tok = jnp.concatenate(halves, axis=0)
    rms = jnp.sqrt(jnp.mean(tok * tok, axis=-1, keepdims=True) + epsilon)
    head_in = (tok / rms * gain_ref[...].astype(f32)).astype(bf16)
    logits = lax.dot_general(
        w_ref[...], head_in, (((1,), (1,)), ((), ())), preferred_element_type=f32
    )
    top_ref[...] = jnp.broadcast_to(jnp.max(logits, axis=0, keepdims=True), top_ref.shape)
    rms_ref[...] = rms


def head(last, gain, w_head):
    vm = pl.BlockSpec(memory_space=pltpu.VMEM)
    rows = last.shape[0]
    return pl.pallas_call(
        head_body,
        out_shape=(
            jax.ShapeDtypeStruct((256, rows), f32),
            jax.ShapeDtypeStruct((rows, 1), f32),
        ),
        in_specs=[vm, vm, vm],
        out_specs=(vm, vm),
        name="head",
    )(last, gain, w_head)


def spread(value, axes, count):
    wide = jnp.broadcast_to(value[None], (count,) + value.shape)
    return lax.all_to_all(wide, axes, 0, 0, tiled=True)


def swap_core(value):
    return lax.ppermute(value, "core", [(0, 1), (1, 0)])


def local(
    hidden,
    attn_gain,
    w_qkv,
    w_out,
    kv_cache,
    holder_slot,
    lengths,
    ffn_gain,
    w_router,
    expert_ids,
    w_exp_in,
    w_exp_down,
    w_sh_in,
    w_sh_down,
    final_gain,
    w_head,
):
    zh = lax.axis_index("zh")
    zl = lax.axis_index("zl")
    core = lax.axis_index("core")
    expert = lax.axis_index(REQ)
    new, feat = hidden.shape
    width = attn_gain.shape[0]
    half = width // 2
    experts_all = w_router.shape[1]
    plane = experts_all // 2
    slots = plane * 2 * SHARE

    neighbours = [(0, 1), (1, 0), (2, 3), (3, 2)]
    w_in = w_exp_in[0].swapaxes(1, 2)
    w_down = w_exp_down[0]
    pair_in = lax.ppermute(w_in, "zl", neighbours)
    pair_down = lax.ppermute(w_down, "zl", neighbours)

    reqs = holder_slot.shape[0]
    ctx = kv_cache.shape[2]
    pieces = kv_cache.reshape(2, reqs, ctx // reqs, feat).transpose(1, 0, 2, 3)
    leg = lax.all_to_all(pieces, REQ, 0, 0, tiled=True)
    leg = leg.at[holder_slot].get(mode="promise_in_bounds")
    old = lax.all_to_all(leg, REQ, 0, 0, tiled=True)

    ids_there = lax.ppermute(expert_ids, "zh", [(0, 1), (1, 0)])
    own = lax.all_gather(hidden, TP, axis=1, tiled=True)
    normed = rms_scale(own.astype(f32), attn_gain).astype(bf16)
    projected = jnp.einsum("td,cde->cte", normed, w_qkv, preferred_element_type=f32)
    positions = (lengths[:, None] + jnp.arange(new, dtype=jnp.int32)[None, :]).astype(f32)
    shaped = projected.reshape(3, 1, new, feat // HD, HD)
    queries = rotate_half(shaped[0], positions).astype(bf16).reshape(new, feat)
    keys_new = rotate_half(shaped[1], positions).astype(bf16).reshape(new, feat)
    values_new = shaped[2].astype(bf16).reshape(new, feat)
    new_cache = jnp.stack([keys_new, values_new])[:, None]

    parts = attend(lengths, queries, keys_new, values_new, old, w_out)
    parts = lax.all_to_all(parts, TP, 0, 0, tiled=True)
    attn_total = jnp.sum(parts.astype(f32), axis=0)
    resid_share = (hidden.astype(f32) + attn_total).astype(bf16)
    ids = jnp.where(
        zh == 0, jnp.stack([expert_ids, ids_there]), jnp.stack([ids_there, expert_ids])
    )
    picks = ids.reshape(2, new * TOPK)
    onehot = (picks[:, :, None] == jnp.arange(experts_all, dtype=jnp.int32)).astype(bf16)
    order = jnp.arange(new * TOPK, dtype=jnp.int32)
    before = (order[:, None] > order[None, :]).astype(bf16)
    earlier = jnp.einsum("pq,rqe->rpe", before, onehot, preferred_element_type=f32)
    rank = jnp.sum(earlier * onehot.astype(f32), axis=2).astype(jnp.int32)
    rank = rank - (zl % 2) * SHARE
    there = picks - zh * plane
    slot = (there * 2 + jnp.arange(2, dtype=jnp.int32)[:, None]) * SHARE + rank
    here = (there >= 0) & (there < plane) & (rank >= 0) & (rank < SHARE)
    slot = jnp.where(here, slot, -1).reshape(2 * new, TOPK)
    slot_iota = jnp.arange(slots, dtype=jnp.int32)
    chosen = jnp.zeros((2 * new, slots), bf16)
    chosen_t = jnp.zeros((slots, 2 * new), bf16)
    for pick in range(TOPK):
        chosen = chosen + (slot[:, pick : pick + 1] == slot_iota[None, :]).astype(bf16)
        chosen_t = chosen_t + (slot[:, pick][None, :] == slot_iota[:, None]).astype(bf16)

    outgoing, resid = dispatch(chosen_t, spread(resid_share, Z, 8))
    rows_mine = lax.all_to_all(
        outgoing.reshape(plane, 2 * SHARE, half), ("x", "y"), 0, 0, tiled=True
    ).reshape(slots, half)
    rows_theirs = swap_core(rows_mine)

    place = jnp.stack([core, expert, zh]).astype(jnp.int32)
    gain = ffn_gain[None]
    router = w_router.T
    own_mine = lax.dynamic_slice_in_dim(resid, zh * new, new, 0)
    shared_mine, shared_theirs = expert_mlp(
        place,
        own_mine,
        swap_core(own_mine),
        gain,
        router,
        (w_sh_in.swapaxes(1, 2), w_sh_down),
        new,
        False,
    )
    shared_theirs = swap_core(shared_theirs)

    served_mine, served_theirs = expert_mlp(
        place, rows_mine, rows_theirs, gain, router, (w_in, w_down, pair_in, pair_down), 256, True
    )
    served = (served_mine.astype(f32) + swap_core(served_theirs).astype(f32)).astype(bf16)
    returned = lax.all_to_all(
        served.reshape(plane, 2 * SHARE, half), ("x", "y"), 0, 0, tiled=True
    ).reshape(slots, half)

    packed = combine(place, chosen, returned, shared_mine, shared_theirs)
    summed = lax.all_to_all(packed, Z, 0, 0, tiled=True)
    out_hidden, last = finish(summed, resid_share, resid, reqs)

    last_all = lax.all_to_all(last, ("core", "x", "y"), 0, 0, tiled=True)
    tops, rms = head(last_all, final_gain[None], w_head)
    last_rms = rms.reshape(reqs)
    top_logit = jnp.max(lax.all_to_all(tops, ALL, 0, 0, tiled=True), axis=0)
    return (out_hidden, new_cache, last_rms, top_logit)


def solution(mesh):
    fine = Mesh(mesh.devices.reshape(SIZES), ALL)
    return jax.shard_map(
        local,
        mesh=fine,
        in_specs=(
            P(REQ, TP),
            P(),
            P(None, None, TP),
            P(TP, None),
            P(None, REQ, None, TP),
            P(),
            P(REQ),
            P(),
            P(),
            P(REQ, None),
            P(REQ, None, None, TP),
            P(REQ, TP, None),
            P(None, None, TP),
            P(TP, None),
            P(),
            P(REQ + TP, None),
        ),
        out_specs=(P(REQ, TP), P(None, REQ, None, TP), P(), P()),
        check_vma=False,
    )
```

```python
import jax
import jax.numpy as jnp
from jax import lax
from jax.sharding import Mesh, PartitionSpec as P
from jax.experimental import pallas as pl
from jax.experimental.pallas import tpu as pltpu

HD = 128
TOPK = 6
CAP = 32
SHARE = CAP // 2

REQ = ("zh", "x", "y")
TP = ("zl", "core")
COL = ("zh", "zl", "core")
Z = ("zh", "zl")
ALL = ("zh", "x", "y", "zl", "core")
SIZES = (2, 4, 4, 4, 2)

epsilon = 1e-06
bf16 = jnp.bfloat16
f32 = jnp.float32


def rms_scale(values, gain):
    return (
        values
        * lax.rsqrt(jnp.mean(values * values, axis=-1, keepdims=True) + epsilon)
        * gain.astype(f32)
    )


def rope_tables(length, new):
    half_len = HD // 2
    freqs = 10000.0 ** (-2.0 * jnp.arange(half_len, dtype=f32) / HD)
    positions = (length + jnp.arange(new, dtype=jnp.int32)).astype(f32)
    angles = positions[:, None] * freqs[None, :]
    cosine, sine = jnp.cos(angles), jnp.sin(angles)
    return jnp.concatenate([cosine, cosine], 1), jnp.concatenate([-sine, sine], 1)


def norm_rows(full_ref, gain_ref):
    return rms_scale(full_ref[...].astype(f32), gain_ref[...]).astype(bf16)


def rotate(values, cos_ref, sin_ref):
    heads = []
    for head in range(values.shape[1] // HD):
        piece = values[:, head * HD : (head + 1) * HD]
        heads.append(piece * cos_ref[...] + pltpu.roll(piece, HD // 2, 1) * sin_ref[...])
    return jnp.concatenate(heads, axis=1).astype(bf16)


def new_kv_body(full_ref, gain_ref, w_ref, cos_ref, sin_ref, o_ref):
    normed = norm_rows(full_ref, gain_ref)
    keys = jnp.dot(normed, w_ref[1], preferred_element_type=f32)
    o_ref[0] = rotate(keys, cos_ref, sin_ref)
    o_ref[1] = jnp.dot(normed, w_ref[2], preferred_element_type=f32).astype(bf16)


def new_kv(full, gain, w_qkv, tables):
    vm = pl.BlockSpec(memory_space=pltpu.VMEM)
    return pl.pallas_call(
        new_kv_body,
        out_shape=jax.ShapeDtypeStruct((2, full.shape[0], w_qkv.shape[2]), bf16),
        in_specs=[vm] * 5,
        out_specs=vm,
        name="new_kv",
    )(full, gain, w_qkv, *tables)


def attend_body(len_ref, full_ref, gain_ref, qkv_ref, cos_ref, sin_ref, kv_ref, w_ref, o_ref):
    length = len_ref[0]
    ctx = kv_ref.shape[2]
    new = full_ref.shape[0]
    normed = norm_rows(full_ref, gain_ref)
    q_all = rotate(jnp.dot(normed, qkv_ref[0], preferred_element_type=f32), cos_ref, sin_ref)
    k_all = rotate(jnp.dot(normed, qkv_ref[1], preferred_element_type=f32), cos_ref, sin_ref)
    v_all = jnp.dot(normed, qkv_ref[2], preferred_element_type=f32).astype(bf16)
    heads = []
    for head in range(q_all.shape[1] // HD):
        lanes = slice(head * HD, (head + 1) * HD)
        q = q_all[:, lanes]
        s_old = dot_nt(q, kv_ref[0, 0, :, lanes]) * HD ** (-0.5)
        s_new = dot_nt(q, k_all[:, lanes]) * HD ** (-0.5)
        seen_old = lax.broadcasted_iota(jnp.int32, (new, ctx), 1) < length
        seen_new = lax.broadcasted_iota(jnp.int32, (new, new), 1) <= lax.broadcasted_iota(
            jnp.int32, (new, new), 0
        )
        s_old = jnp.where(seen_old, s_old, -1e30)
        s_new = jnp.where(seen_new, s_new, -1e30)
        peak = jnp.maximum(
            jnp.max(s_old, axis=-1, keepdims=True), jnp.max(s_new, axis=-1, keepdims=True)
        )
        e_old = jnp.where(seen_old, jnp.exp(s_old - peak), 0.0)
        e_new = jnp.where(seen_new, jnp.exp(s_new - peak), 0.0)
        total = jnp.sum(e_old, axis=-1, keepdims=True) + jnp.sum(e_new, axis=-1, keepdims=True)
        w_old = (e_old / total).astype(bf16)
        w_new = (e_new / total).astype(bf16)
        out = jnp.dot(w_old, kv_ref[1, 0, :, lanes], preferred_element_type=f32) + jnp.dot(
            w_new, v_all[:, lanes], preferred_element_type=f32
        )
        heads.append(out.astype(bf16))
    attn = jnp.concatenate(heads, axis=1)
    wide = o_ref.shape[2]
    for part in range(o_ref.shape[0]):
        o_ref[part] = jnp.dot(
            attn, w_ref[:, part * wide : (part + 1) * wide], preferred_element_type=f32
        ).astype(bf16)


def attend(length, full, gain, w_qkv, tables, kv_cache, w_out):
    vm = pl.BlockSpec(memory_space=pltpu.VMEM)
    new = full.shape[0]
    feat = w_out.shape[0]
    return pl.pallas_call(
        attend_body,
        out_shape=jax.ShapeDtypeStruct((w_out.shape[1] // feat, new, feat), bf16),
        in_specs=[pl.BlockSpec(memory_space=pltpu.SMEM)] + [vm] * 7,
        out_specs=vm,
        name="attend",
    )(length, full, gain, w_qkv, *tables, kv_cache, w_out)


def spread(value, axes, count):
    wide = jnp.broadcast_to(value[None], (count,) + value.shape)
    return lax.all_to_all(wide, axes, 0, 0, tiled=True)


def swap_core(value):
    return lax.ppermute(value, "core", [(0, 1), (1, 0)])


def dot_nt(a, b):
    return lax.dot_general(a, b, (((1,), (1,)), ((), ())), preferred_element_type=f32)


def expert_rows(rows, gate_w, up_w, down_w):
    gate = dot_nt(rows, gate_w)
    up = dot_nt(rows, up_w)
    inner = (gate / (1.0 + jnp.exp(-gate)) * up).astype(bf16)
    return jnp.dot(inner, down_w, preferred_element_type=f32)


def drain(first, out, mine_ref, theirs_ref):
    feat = out.shape[1] // 8

    def store(even_ref, odd_ref):
        for part in range(4):
            piece = slice(part * feat, (part + 1) * feat)
            even_ref[:, piece] = out[:, 2 * part * feat : (2 * part + 1) * feat]
            odd_ref[:, piece] = out[:, (2 * part + 1) * feat : (2 * part + 2) * feat]

    @pl.when(first)
    def _():
        store(mine_ref, theirs_ref)

    @pl.when(jnp.logical_not(first))
    def _():
        store(theirs_ref, mine_ref)


def routed_body(
    place_ref, a_ref, b_ref, gain_ref, router_ref, in_ref, down_ref, pg_ref, pu_ref, pd_ref,
    om_ref, ot_ref, x_ref,
):
    first = place_ref[0] == 0
    feat = x_ref.shape[1] // 8

    def fill(even_ref, odd_ref):
        for part in range(4):
            piece = slice(part * feat, (part + 1) * feat)
            x_ref[:, 2 * part * feat : (2 * part + 1) * feat] = even_ref[:, piece]
            x_ref[:, (2 * part + 1) * feat : (2 * part + 2) * feat] = odd_ref[:, piece]

    @pl.when(first)
    def _():
        fill(a_ref, b_ref)

    @pl.when(jnp.logical_not(first))
    def _():
        fill(b_ref, a_ref)

    rows = norm_rows(x_ref, gain_ref)
    out = expert_rows(rows, in_ref[0], in_ref[1], down_ref[...])
    out = out + expert_rows(rows, pg_ref[...], pu_ref[...], pd_ref[...])
    logits = dot_nt(rows, router_ref[...])
    raised = jnp.exp(logits - jnp.max(logits, axis=-1, keepdims=True))
    own = lax.broadcasted_iota(jnp.int32, logits.shape, 1) == place_ref[1]
    picked = jnp.sum(jnp.where(own, raised, 0.0), axis=-1, keepdims=True)
    out = out * (picked / jnp.sum(raised, axis=-1, keepdims=True))
    drain(first, out.astype(bf16), om_ref, ot_ref)


def routed_mlp(place, rows_mine, rows_theirs, block, *shared_operands):
    count, half = rows_mine.shape
    width = 2 * half
    hidden = 2 * shared_operands[3].shape[0]
    row_spec = pl.BlockSpec((block, half), lambda i: (i, 0))

    def whole(array):
        zeros = (0,) * array.ndim
        return pl.BlockSpec(array.shape, lambda i: zeros)

    shape = jax.ShapeDtypeStruct((count, half), bf16)
    return pl.pallas_call(
        routed_body,
        grid=(count // block,),
        out_shape=(shape, shape),
        in_specs=[pl.BlockSpec(memory_space=pltpu.SMEM), row_spec, row_spec]
        + [whole(array) for array in shared_operands],
        out_specs=(row_spec, row_spec),
        scratch_shapes=[pltpu.VMEM((block, width), bf16)],
        cost_estimate=pl.CostEstimate(
            flops=6 * count * width * hidden,
            transcendentals=count * hidden,
            bytes_accessed=8 * count * half + 6 * width * hidden,
        ),
        name="routed_mlp",
    )(place, rows_mine, rows_theirs, *shared_operands)


def shared_body(place_ref, x_ref, gain_ref, in_ref, down_ref, om_ref, ot_ref):
    rows = norm_rows(x_ref, gain_ref)
    out = expert_rows(rows, in_ref[0], in_ref[1], down_ref[...])
    drain(place_ref[0] == 0, out.astype(bf16), om_ref, ot_ref)


def shared_mlp(place, rows, gain, w_in, w_down):
    vm = pl.BlockSpec(memory_space=pltpu.VMEM)
    shape = jax.ShapeDtypeStruct((rows.shape[0], rows.shape[1] // 2), bf16)
    return pl.pallas_call(
        shared_body,
        out_shape=(shape, shape),
        in_specs=[pl.BlockSpec(memory_space=pltpu.SMEM)] + [vm] * 4,
        out_specs=(vm, vm),
        name="shared_mlp",
    )(place, rows, gain, w_in, w_down)


def reorder_body(order_ref, a_ref, b_ref, o_ref):
    chunks = order_ref.shape[0]
    rows = o_ref.shape[0] // chunks
    for i in range(chunks):
        at = pl.ds(pl.multiple_of(order_ref[i] * rows, rows), rows)
        o_ref[i * rows : (i + 1) * rows, :] = (
            a_ref[at, :].astype(f32) + b_ref[at, :].astype(f32)
        ).astype(bf16)


def reorder(order, a, b):
    vm = pl.BlockSpec(memory_space=pltpu.VMEM)
    return pl.pallas_call(
        reorder_body,
        out_shape=jax.ShapeDtypeStruct(a.shape, bf16),
        in_specs=[pl.BlockSpec(memory_space=pltpu.SMEM), vm, vm],
        out_specs=vm,
        name="reorder",
    )(order, a, b)


def dispatch_body(chosen_ref, parts_ref, out_ref):
    feat = parts_ref.shape[2]
    for part in range(4):
        both = jnp.concatenate([parts_ref[part], parts_ref[4 + part]], axis=0)
        out_ref[:, part * feat : (part + 1) * feat] = jnp.dot(
            chosen_ref[...], both, preferred_element_type=f32
        ).astype(bf16)


def dispatch(chosen_t, parts):
    vm = pl.BlockSpec(memory_space=pltpu.VMEM)
    return pl.pallas_call(
        dispatch_body,
        out_shape=jax.ShapeDtypeStruct((chosen_t.shape[0], 4 * parts.shape[2]), bf16),
        in_specs=[vm, vm],
        out_specs=vm,
        name="dispatch",
    )(chosen_t, parts)


def combine_body(place_ref, chosen_ref, back_ref, mine_ref, theirs_ref, share_ref, out_ref):
    tokens = chosen_ref.shape[0]
    new = tokens // 2
    feat = out_ref.shape[2]
    for zo in range(2):
        own = (place_ref[2] == zo).astype(f32)
        total = jnp.dot(
            chosen_ref[zo * new : (zo + 1) * new, :], back_ref[...], preferred_element_type=f32
        )
        total = total + own * (mine_ref[...].astype(f32) + theirs_ref[...].astype(f32))
        for part in range(4):
            once = own * (place_ref[3] == part).astype(f32)
            piece = total[:, part * feat : (part + 1) * feat]
            piece = (piece + once * share_ref[...].astype(f32)).astype(bf16)
            out_ref[zo * 4 + part, :new, :] = piece
            row = piece[new - 1 :, :]
            for dest in range(8):
                out_ref[dest, new + zo * 4 + part : new + zo * 4 + part + 1, :] = row


def combine(place, chosen, back, mine, theirs, share):
    vm = pl.BlockSpec(memory_space=pltpu.VMEM)
    tokens = chosen.shape[0]
    half = back.shape[1]
    return pl.pallas_call(
        combine_body,
        out_shape=jax.ShapeDtypeStruct((8, tokens // 2 + 8, half // 4), bf16),
        in_specs=[pl.BlockSpec(memory_space=pltpu.SMEM)] + [vm] * 5,
        out_specs=vm,
        name="combine",
    )(place, chosen, back, mine, theirs, share)


def finish_body(parts_ref, out_ref, last_ref):
    new = out_ref.shape[0]
    total = parts_ref[0].astype(f32)
    for part in range(1, 8):
        total = total + parts_ref[part].astype(f32)
    out_ref[...] = total[:new].astype(bf16)
    for part in range(8):
        row = total[new + part : new + part + 1]
        for sub in range(2):
            piece = row[:, sub * 128 : (sub + 1) * 128]
            last_ref[:, part * 2 + sub : part * 2 + sub + 1, :] = jnp.broadcast_to(
                piece.astype(bf16)[None], (last_ref.shape[0], 1, 128)
            )


def finish(parts, copies):
    vm = pl.BlockSpec(memory_space=pltpu.VMEM)
    return pl.pallas_call(
        finish_body,
        out_shape=(
            jax.ShapeDtypeStruct((parts.shape[1] - 8, parts.shape[2]), bf16),
            jax.ShapeDtypeStruct((copies, 16, 128), bf16),
        ),
        in_specs=[vm],
        out_specs=(vm, vm),
        name="finish",
    )(parts)


def head_body(last_ref, gain_ref, w_ref, top_ref, rms_ref):
    plane = last_ref.shape[0] // 2
    rows = jnp.swapaxes(last_ref[...].astype(f32), 0, 1)
    halves = []
    for zo in range(2):
        pieces = []
        for part in range(4):
            for core in range(2):
                for sub in range(2):
                    pieces.append(
                        rows[(zo * 4 + part) * 2 + sub, core * plane : (core + 1) * plane]
                    )
        halves.append(jnp.concatenate(pieces, axis=1))
    tok = jnp.concatenate(halves, axis=0)
    rms = jnp.sqrt(jnp.mean(tok * tok, axis=-1, keepdims=True) + epsilon)
    head_in = (tok / rms * gain_ref[...].astype(f32)).astype(bf16)
    logits = lax.dot_general(
        w_ref[...], head_in, (((1,), (1,)), ((), ())), preferred_element_type=f32
    )
    top_ref[...] = jnp.broadcast_to(jnp.max(logits, axis=0, keepdims=True), top_ref.shape)
    rms_ref[...] = rms


def head(last, gain, w_head):
    vm = pl.BlockSpec(memory_space=pltpu.VMEM)
    rows = last.shape[0]
    return pl.pallas_call(
        head_body,
        out_shape=(
            jax.ShapeDtypeStruct((256, rows), f32),
            jax.ShapeDtypeStruct((rows, 1), f32),
        ),
        in_specs=[vm, vm, vm],
        out_specs=(vm, vm),
        name="head",
    )(last, gain, w_head)


def local(
    hidden,
    attn_gain,
    w_qkv,
    w_out,
    kv_cache,
    holder_slot,
    lengths,
    ffn_gain,
    w_router,
    expert_ids,
    w_exp_in,
    w_exp_down,
    w_sh_in,
    w_sh_down,
    final_gain,
    w_head,
):
    zh = lax.axis_index("zh")
    zl = lax.axis_index("zl")
    core = lax.axis_index("core")
    expert = lax.axis_index(REQ)
    new, feat = hidden.shape
    width = attn_gain.shape[0]
    half = width // 2
    experts_all = w_router.shape[1]
    plane = experts_all // 2
    slots = plane * 2 * SHARE
    reqs = holder_slot.shape[0]
    span = new // reqs
    place = jnp.stack([core, expert, zh, zl]).astype(jnp.int32)
    gain = attn_gain[None]
    ffn = ffn_gain[None]
    barrier = lax.optimization_barrier

    meta = jnp.concatenate(
        [
            expert_ids.reshape(reqs, span * TOPK),
            jnp.broadcast_to(lengths[:, None] // 32, (reqs, 1)),
            jnp.broadcast_to(lengths[:, None] % 32, (reqs, 1)),
        ],
        axis=1,
    ).astype(bf16)
    meta = jnp.pad(meta, ((0, 0), (0, feat - meta.shape[1])))[:, None]
    chunks = jnp.concatenate(
        [hidden.reshape(reqs, span, feat), meta, jnp.zeros((reqs, 8 - span - 1, feat), bf16)], axis=1
    )
    leg = lax.all_to_all(chunks, REQ, 0, 0, tiled=True)

    neighbours = [(0, 1), (1, 0), (2, 3), (3, 2)]
    w_in = w_exp_in[0].swapaxes(1, 2)
    w_down = w_exp_down[0]
    pair_gate = lax.ppermute(w_in[0], "zl", neighbours)
    pair_up = lax.ppermute(w_in[1], "zl", neighbours)
    pair_down = lax.ppermute(w_down, "zl", neighbours)

    leg, pair_gate = barrier((leg, pair_gate))
    req_iota = jnp.arange(reqs, dtype=jnp.int32)
    owner_of = jnp.sum(
        jnp.where(holder_slot[None, :] == req_iota[:, None], req_iota[None, :], 0), axis=1
    )
    leg = leg.at[owner_of].get(mode="promise_in_bounds")
    leg = lax.all_to_all(leg, REQ, 0, 0, tiled=True)
    leg, pair_up = barrier((leg, pair_up))
    held = leg[:, :span].reshape(new, feat)
    held_ids = leg[:, span, : span * TOPK].reshape(new, TOPK).astype(jnp.int32)
    packed_len = leg[0, span, span * TOPK : span * TOPK + 2].astype(jnp.int32)
    held_len = packed_len[0] * 32 + packed_len[1]

    full = lax.all_gather(held, TP, axis=1, tiled=True)
    full, pair_down = barrier((full, pair_down))
    parts = attend(
        held_len[None], full, gain, w_qkv, rope_tables(held_len, new), kv_cache, w_out
    )
    parts = lax.all_to_all(parts, TP, 0, 0, tiled=True)
    held_share = (held.astype(f32) + jnp.sum(parts.astype(f32), axis=0)).astype(bf16)

    def slots_of(ids):
        other = lax.ppermute(ids, "zh", [(0, 1), (1, 0)])
        both = jnp.where(zh == 0, jnp.stack([ids, other]), jnp.stack([other, ids]))
        picks = both.reshape(2, new * TOPK)
        onehot = (picks[:, :, None] == jnp.arange(experts_all, dtype=jnp.int32)).astype(bf16)
        order = jnp.arange(new * TOPK, dtype=jnp.int32)
        before = (order[:, None] > order[None, :]).astype(bf16)
        earlier = jnp.einsum("pq,rqe->rpe", before, onehot, preferred_element_type=f32)
        rank = jnp.sum(earlier * onehot.astype(f32), axis=2).astype(jnp.int32)
        rank = rank - (zl % 2) * SHARE
        there = picks - zh * plane
        slot = (there * 2 + jnp.arange(2, dtype=jnp.int32)[:, None]) * SHARE + rank
        here = (there >= 0) & (there < plane) & (rank >= 0) & (rank < SHARE)
        return jnp.where(here, slot, -1).reshape(2 * new, TOPK)

    slot_iota = jnp.arange(slots, dtype=jnp.int32)
    slot_held = slots_of(held_ids)
    slot_own = slots_of(expert_ids)
    chosen_t = jnp.zeros((slots, 2 * new), bf16)
    chosen = jnp.zeros((2 * new, slots), bf16)
    for pick in range(TOPK):
        chosen_t = chosen_t + (slot_held[:, pick][None, :] == slot_iota[:, None]).astype(bf16)
        chosen = chosen + (slot_own[:, pick : pick + 1] == slot_iota[None, :]).astype(bf16)

    outgoing = dispatch(chosen_t, spread(held_share, Z, 8))
    rows_mine = lax.all_to_all(
        outgoing.reshape(plane, 2 * SHARE, half), ("x", "y"), 0, 0, tiled=True
    ).reshape(slots, half)

    hidden_late, _ = barrier((hidden, outgoing))
    own_full = lax.all_gather(hidden_late, TP, axis=1, tiled=True)
    rows_mine, own_full = barrier((rows_mine, own_full))
    rows_theirs = swap_core(rows_mine)
    new_cache = new_kv(own_full, gain, w_qkv, rope_tables(lengths[0], new))[:, None]

    served_mine, served_theirs = routed_mlp(
        place,
        rows_mine,
        rows_theirs,
        256,
        ffn,
        w_router.T,
        w_in,
        w_down,
        pair_gate,
        pair_up,
        pair_down,
    )
    slot_at = holder_slot.reshape(2, plane).T.reshape(reqs)
    order = (slot_at % plane) * 2 + slot_at // plane
    served = reorder(order, served_mine, swap_core(served_theirs))
    returned = lax.all_to_all(
        served.reshape(plane, 2 * SHARE, half), ("x", "y"), 0, 0, tiled=True
    ).reshape(slots, half)

    shares = lax.all_gather(held_share, REQ, axis=0)
    own_slot = lax.dynamic_index_in_dim(holder_slot, expert, 0, keepdims=False)
    own_share = lax.dynamic_index_in_dim(shares, own_slot, 0, keepdims=False)
    own_rows = lax.all_gather(own_share, TP, axis=1, tiled=True)
    shared_mine, shared_theirs = shared_mlp(
        place, own_rows, ffn, w_sh_in.swapaxes(1, 2), w_sh_down
    )
    shared_theirs = swap_core(shared_theirs)

    packed = combine(place, chosen, returned, shared_mine, shared_theirs, own_share)
    summed = lax.all_to_all(packed, Z, 0, 0, tiled=True)
    out_hidden, last = finish(summed, reqs)

    last_all = lax.all_to_all(last, ("core", "x", "y"), 0, 0, tiled=True)
    tops, rms = head(last_all, final_gain[None], w_head)
    last_rms = rms.reshape(reqs)
    top_logit = jnp.max(lax.all_to_all(tops, ALL, 0, 0, tiled=True), axis=0)
    return (out_hidden, new_cache, last_rms, top_logit)


def solution(mesh):
    fine = Mesh(mesh.devices.reshape(SIZES), ALL)
    return jax.shard_map(
        local,
        mesh=fine,
        in_specs=(
            P(REQ, TP),
            P(),
            P(None, None, TP),
            P(TP, None),
            P(None, REQ, None, TP),
            P(),
            P(REQ),
            P(),
            P(),
            P(REQ, None),
            P(REQ, None, None, TP),
            P(REQ, TP, None),
            P(None, None, TP),
            P(TP, None),
            P(),
            P(REQ + TP, None),
        ),
        out_specs=(P(REQ, TP), P(None, REQ, None, TP), P(), P()),
        check_vma=False,
    )
```

```python
import jax
import jax.numpy as jnp
from jax import lax
from jax.sharding import Mesh, PartitionSpec as P
from jax.experimental import pallas as pl
from jax.experimental.pallas import tpu as pltpu

HD = 128
TOPK = 6
CAP = 32
SHARE = CAP // 2

REQ = ("zh", "x", "y")
TP = ("zl", "core")
COL = ("zh", "zl", "core")
Z = ("zh", "zl")
ALL = ("zh", "x", "y", "zl", "core")
SIZES = (2, 4, 4, 4, 2)

epsilon = 1e-06
bf16 = jnp.bfloat16
f32 = jnp.float32


def rms_scale(values, gain):
    return (
        values
        * lax.rsqrt(jnp.mean(values * values, axis=-1, keepdims=True) + epsilon)
        * gain.astype(f32)
    )


def rope_tables(length, new):
    half_len = HD // 2
    freqs = 10000.0 ** (-2.0 * jnp.arange(half_len, dtype=f32) / HD)
    positions = (length + jnp.arange(new, dtype=jnp.int32)).astype(f32)
    angles = positions[:, None] * freqs[None, :]
    cosine, sine = jnp.cos(angles), jnp.sin(angles)
    return jnp.concatenate([cosine, cosine], 1), jnp.concatenate([-sine, sine], 1)


def norm_rows(full_ref, gain_ref):
    return rms_scale(full_ref[...].astype(f32), gain_ref[...]).astype(bf16)


def rotate(values, cos_ref, sin_ref):
    heads = []
    for head in range(values.shape[1] // HD):
        piece = values[:, head * HD : (head + 1) * HD]
        heads.append(piece * cos_ref[...] + pltpu.roll(piece, HD // 2, 1) * sin_ref[...])
    return jnp.concatenate(heads, axis=1).astype(bf16)


def new_kv_body(full_ref, gain_ref, w_ref, cos_ref, sin_ref, o_ref):
    normed = norm_rows(full_ref, gain_ref)
    keys = jnp.dot(normed, w_ref[1], preferred_element_type=f32)
    o_ref[0] = rotate(keys, cos_ref, sin_ref)
    o_ref[1] = jnp.dot(normed, w_ref[2], preferred_element_type=f32).astype(bf16)


def new_kv(full, gain, w_qkv, tables):
    vm = pl.BlockSpec(memory_space=pltpu.VMEM)
    return pl.pallas_call(
        new_kv_body,
        out_shape=jax.ShapeDtypeStruct((2, full.shape[0], w_qkv.shape[2]), bf16),
        in_specs=[vm] * 5,
        out_specs=vm,
        name="new_kv",
    )(full, gain, w_qkv, *tables)


def attend_body(len_ref, full_ref, gain_ref, qkv_ref, cos_ref, sin_ref, kv_ref, w_ref, o_ref):
    length = len_ref[0]
    ctx = kv_ref.shape[2]
    new = full_ref.shape[0]
    normed = norm_rows(full_ref, gain_ref)
    q_all = rotate(jnp.dot(normed, qkv_ref[0], preferred_element_type=f32), cos_ref, sin_ref)
    k_all = rotate(jnp.dot(normed, qkv_ref[1], preferred_element_type=f32), cos_ref, sin_ref)
    v_all = jnp.dot(normed, qkv_ref[2], preferred_element_type=f32).astype(bf16)
    heads = []
    for head in range(q_all.shape[1] // HD):
        lanes = slice(head * HD, (head + 1) * HD)
        q = q_all[:, lanes]
        s_old = dot_nt(q, kv_ref[0, 0, :, lanes]) * HD ** (-0.5)
        s_new = dot_nt(q, k_all[:, lanes]) * HD ** (-0.5)
        seen_old = lax.broadcasted_iota(jnp.int32, (new, ctx), 1) < length
        seen_new = lax.broadcasted_iota(jnp.int32, (new, new), 1) <= lax.broadcasted_iota(
            jnp.int32, (new, new), 0
        )
        s_old = jnp.where(seen_old, s_old, -1e30)
        s_new = jnp.where(seen_new, s_new, -1e30)
        peak = jnp.maximum(
            jnp.max(s_old, axis=-1, keepdims=True), jnp.max(s_new, axis=-1, keepdims=True)
        )
        e_old = jnp.where(seen_old, jnp.exp(s_old - peak), 0.0)
        e_new = jnp.where(seen_new, jnp.exp(s_new - peak), 0.0)
        total = jnp.sum(e_old, axis=-1, keepdims=True) + jnp.sum(e_new, axis=-1, keepdims=True)
        w_old = (e_old / total).astype(bf16)
        w_new = (e_new / total).astype(bf16)
        out = jnp.dot(w_old, kv_ref[1, 0, :, lanes], preferred_element_type=f32) + jnp.dot(
            w_new, v_all[:, lanes], preferred_element_type=f32
        )
        heads.append(out.astype(bf16))
    attn = jnp.concatenate(heads, axis=1)
    wide = o_ref.shape[2]
    for part in range(o_ref.shape[0]):
        o_ref[part] = jnp.dot(
            attn, w_ref[:, part * wide : (part + 1) * wide], preferred_element_type=f32
        ).astype(bf16)


def attend(length, full, gain, w_qkv, tables, kv_cache, w_out):
    vm = pl.BlockSpec(memory_space=pltpu.VMEM)
    new = full.shape[0]
    feat = w_out.shape[0]
    return pl.pallas_call(
        attend_body,
        out_shape=jax.ShapeDtypeStruct((w_out.shape[1] // feat, new, feat), bf16),
        in_specs=[pl.BlockSpec(memory_space=pltpu.SMEM)] + [vm] * 7,
        out_specs=vm,
        name="attend",
    )(length, full, gain, w_qkv, *tables, kv_cache, w_out)


def spread(value, axes, count):
    wide = jnp.broadcast_to(value[None], (count,) + value.shape)
    return lax.all_to_all(wide, axes, 0, 0, tiled=True)


def swap_core(value):
    return lax.ppermute(value, "core", [(0, 1), (1, 0)])


def dot_nt(a, b):
    return lax.dot_general(a, b, (((1,), (1,)), ((), ())), preferred_element_type=f32)


def expert_rows(rows, gate_w, up_w, down_w):
    gate = dot_nt(rows, gate_w)
    up = dot_nt(rows, up_w)
    inner = (gate / (1.0 + jnp.exp(-gate)) * up).astype(bf16)
    return jnp.dot(inner, down_w, preferred_element_type=f32)


def drain(first, out, mine_ref, theirs_ref):
    feat = out.shape[1] // 8

    def store(even_ref, odd_ref):
        for part in range(4):
            piece = slice(part * feat, (part + 1) * feat)
            even_ref[:, piece] = out[:, 2 * part * feat : (2 * part + 1) * feat]
            odd_ref[:, piece] = out[:, (2 * part + 1) * feat : (2 * part + 2) * feat]

    @pl.when(first)
    def _():
        store(mine_ref, theirs_ref)

    @pl.when(jnp.logical_not(first))
    def _():
        store(theirs_ref, mine_ref)


def experts_body(
    place_ref, a_ref, b_ref, gain_ref, router_ref, in_ref, down_ref, pg_ref, pu_ref, pd_ref,
    si_ref, sd_ref, om_ref, ot_ref, xr_ref, xs_ref,
):
    first = place_ref[0] == 0
    feat = xr_ref.shape[1] // 8
    chunks, span = a_ref.shape[:2]
    routed = xr_ref.shape[0] // chunks
    shared = span - routed

    def fill(even_ref, odd_ref):
        for chunk in range(chunks):
            for part in range(4):
                piece = slice(part * feat, (part + 1) * feat)
                for odd, ref in enumerate((even_ref, odd_ref)):
                    lanes = slice((2 * part + odd) * feat, (2 * part + odd + 1) * feat)
                    rows = ref[chunk, :, piece].astype(f32)
                    xr_ref[chunk * routed : (chunk + 1) * routed, lanes] = rows[:routed]
                    xs_ref[chunk * shared : (chunk + 1) * shared, lanes] = rows[routed:]

    @pl.when(first)
    def _():
        fill(a_ref, b_ref)

    @pl.when(jnp.logical_not(first))
    def _():
        fill(b_ref, a_ref)

    rows = norm_rows(xr_ref, gain_ref)
    out = expert_rows(rows, in_ref[0], in_ref[1], down_ref[...])
    out = out + expert_rows(rows, pg_ref[...], pu_ref[...], pd_ref[...])
    logits = dot_nt(rows, router_ref[...])
    raised = jnp.exp(logits - jnp.max(logits, axis=-1, keepdims=True))
    own = lax.broadcasted_iota(jnp.int32, logits.shape, 1) == place_ref[1]
    picked = jnp.sum(jnp.where(own, raised, 0.0), axis=-1, keepdims=True)
    out = out * (picked / jnp.sum(raised, axis=-1, keepdims=True))
    common = norm_rows(xs_ref, gain_ref)
    common = expert_rows(common, si_ref[0], si_ref[1], sd_ref[...])
    common = common + xs_ref[...] * 0.125

    def store(even_ref, odd_ref):
        for chunk in range(chunks):
            top = out[chunk * routed : (chunk + 1) * routed]
            low = common[chunk * shared : (chunk + 1) * shared]
            both = jnp.concatenate([top, low], axis=0).astype(bf16)
            for part in range(4):
                piece = slice(part * feat, (part + 1) * feat)
                even_ref[chunk, :, piece] = both[:, 2 * part * feat : (2 * part + 1) * feat]
                odd_ref[chunk, :, piece] = both[:, (2 * part + 1) * feat : (2 * part + 2) * feat]

    @pl.when(first)
    def _():
        store(om_ref, ot_ref)

    @pl.when(jnp.logical_not(first))
    def _():
        store(ot_ref, om_ref)


def experts(place, rows_mine, rows_theirs, steps, *weights):
    count, span, half = rows_mine.shape
    width = 2 * half
    block = count // steps
    row_spec = pl.BlockSpec((block, span, half), lambda i: (i, 0, 0))

    def whole(array):
        zeros = (0,) * array.ndim
        return pl.BlockSpec(array.shape, lambda i: zeros)

    shape = jax.ShapeDtypeStruct(rows_mine.shape, bf16)
    return pl.pallas_call(
        experts_body,
        grid=(steps,),
        out_shape=(shape, shape),
        in_specs=[pl.BlockSpec(memory_space=pltpu.SMEM), row_spec, row_spec]
        + [whole(array) for array in weights],
        out_specs=(row_spec, row_spec),
        scratch_shapes=[
            pltpu.VMEM((block * 2 * SHARE, width), f32),
            pltpu.VMEM((block * (span - 2 * SHARE), width), f32),
        ],
        cost_estimate=pl.CostEstimate(
            flops=6 * count * span * width * 352,
            transcendentals=count * span * 352,
            bytes_accessed=8 * count * span * half + 18 * width * 176,
        ),
        name="experts",
    )(place, rows_mine, rows_theirs, *weights)


def reorder_body(order_ref, a_ref, b_ref, o_ref):
    o_ref[...] = (
        jnp.dot(order_ref[...], a_ref[...], preferred_element_type=f32)
        + jnp.dot(order_ref[...], b_ref[...], preferred_element_type=f32)
    ).astype(bf16)


def reorder(order, a, b):
    vm = pl.BlockSpec(memory_space=pltpu.VMEM)
    return pl.pallas_call(
        reorder_body,
        out_shape=jax.ShapeDtypeStruct(a.shape, bf16),
        in_specs=[vm, vm, vm],
        out_specs=vm,
        name="reorder",
    )(order, a, b)


def dispatch_body(chosen_ref, parts_ref, out_ref):
    feat = parts_ref.shape[2]
    for part in range(4):
        both = jnp.concatenate([parts_ref[part], parts_ref[4 + part]], axis=0)
        out_ref[:, part * feat : (part + 1) * feat] = jnp.dot(
            chosen_ref[...], both, preferred_element_type=f32
        ).astype(bf16)


def dispatch(chosen_t, parts):
    vm = pl.BlockSpec(memory_space=pltpu.VMEM)
    return pl.pallas_call(
        dispatch_body,
        out_shape=jax.ShapeDtypeStruct((chosen_t.shape[0], 4 * parts.shape[2]), bf16),
        in_specs=[vm, vm],
        out_specs=vm,
        name="dispatch",
    )(chosen_t, parts)


def combine_body(chosen_ref, back_ref, out_ref):
    feat = out_ref.shape[2]
    new = chosen_ref.shape[1] // 2
    for zo in range(2):
        total = lax.dot_general(
            chosen_ref[:, zo * new : (zo + 1) * new],
            back_ref[...],
            (((0,), (0,)), ((), ())),
            preferred_element_type=f32,
        ).astype(bf16)
        for part in range(4):
            piece = total[:, part * feat : (part + 1) * feat]
            out_ref[zo * 4 + part, :new, :] = piece
            row = piece[new - 1 :, :]
            for dest in range(8):
                out_ref[dest, new + zo * 4 + part : new + zo * 4 + part + 1, :] = row


def combine(chosen_t, back):
    vm = pl.BlockSpec(memory_space=pltpu.VMEM)
    return pl.pallas_call(
        combine_body,
        out_shape=jax.ShapeDtypeStruct((8, chosen_t.shape[1] // 2 + 8, back.shape[1] // 4), bf16),
        in_specs=[vm, vm],
        out_specs=vm,
        name="combine",
    )(chosen_t, back)


def finish_body(parts_ref, out_ref, last_ref):
    new = out_ref.shape[0]
    total = parts_ref[0].astype(f32)
    for part in range(1, 8):
        total = total + parts_ref[part].astype(f32)
    out_ref[...] = total[:new].astype(bf16)
    for part in range(8):
        row = total[new + part : new + part + 1]
        for sub in range(2):
            piece = row[:, sub * 128 : (sub + 1) * 128]
            last_ref[:, part * 2 + sub : part * 2 + sub + 1, :] = jnp.broadcast_to(
                piece.astype(bf16)[None], (last_ref.shape[0], 1, 128)
            )


def finish(parts, copies):
    vm = pl.BlockSpec(memory_space=pltpu.VMEM)
    return pl.pallas_call(
        finish_body,
        out_shape=(
            jax.ShapeDtypeStruct((parts.shape[1] - 8, parts.shape[2]), bf16),
            jax.ShapeDtypeStruct((copies, 16, 128), bf16),
        ),
        in_specs=[vm],
        out_specs=(vm, vm),
        name="finish",
    )(parts)


def head_body(last_ref, gain_ref, w_ref, top_ref, rms_ref):
    plane = last_ref.shape[0] // 2
    rows = jnp.swapaxes(last_ref[...].astype(f32), 0, 1)
    halves = []
    for zo in range(2):
        pieces = []
        for part in range(4):
            for core in range(2):
                for sub in range(2):
                    pieces.append(
                        rows[(zo * 4 + part) * 2 + sub, core * plane : (core + 1) * plane]
                    )
        halves.append(jnp.concatenate(pieces, axis=1))
    tok = jnp.concatenate(halves, axis=0)
    rms = jnp.sqrt(jnp.mean(tok * tok, axis=-1, keepdims=True) + epsilon)
    head_in = (tok / rms * gain_ref[...].astype(f32)).astype(bf16)
    logits = lax.dot_general(
        w_ref[...], head_in, (((1,), (1,)), ((), ())), preferred_element_type=f32
    )
    top_ref[...] = jnp.broadcast_to(jnp.max(logits, axis=0, keepdims=True), top_ref.shape)
    rms_ref[...] = rms


def head(last, gain, w_head):
    vm = pl.BlockSpec(memory_space=pltpu.VMEM)
    rows = last.shape[0]
    return pl.pallas_call(
        head_body,
        out_shape=(
            jax.ShapeDtypeStruct((256, rows), f32),
            jax.ShapeDtypeStruct((rows, 1), f32),
        ),
        in_specs=[vm, vm, vm],
        out_specs=(vm, vm),
        name="head",
    )(last, gain, w_head)


def local(
    hidden,
    attn_gain,
    w_qkv,
    w_out,
    kv_cache,
    holder_slot,
    lengths,
    ffn_gain,
    w_router,
    expert_ids,
    w_exp_in,
    w_exp_down,
    w_sh_in,
    w_sh_down,
    final_gain,
    w_head,
):
    zh = lax.axis_index("zh")
    zl = lax.axis_index("zl")
    core = lax.axis_index("core")
    expert = lax.axis_index(REQ)
    new, feat = hidden.shape
    width = attn_gain.shape[0]
    half = width // 2
    experts_all = w_router.shape[1]
    plane = experts_all // 2
    reqs = holder_slot.shape[0]
    span = new // reqs
    rows = 2 * (SHARE + span)
    slots = plane * rows
    place = jnp.stack([core, expert]).astype(jnp.int32)
    gain = attn_gain[None]
    barrier = lax.optimization_barrier

    ids_t = expert_ids.T
    sizes = jnp.concatenate(
        [jnp.broadcast_to(lengths // 32, (feat // 2,)), jnp.broadcast_to(lengths % 32, (feat // 2,))]
    )
    meta = jnp.concatenate([ids_t.reshape(TOPK * new // feat, feat), sizes[None]]).astype(bf16)
    meta = jnp.broadcast_to(meta[None], (reqs,) + meta.shape)
    chunks = jnp.concatenate([hidden.reshape(reqs, span, feat), meta], axis=1)
    w_in = w_exp_in[0].swapaxes(1, 2)
    w_down = w_exp_down[0]
    leg = lax.all_to_all(chunks, REQ, 0, 0, tiled=True)
    leg, gate_w = barrier((leg, w_in[0]))

    neighbours = [(0, 1), (1, 0), (2, 3), (3, 2)]
    pair_gate = lax.ppermute(gate_w, "zl", neighbours)

    req_iota = jnp.arange(reqs, dtype=jnp.int32)
    owner_of = jnp.sum(
        jnp.where(holder_slot[None, :] == req_iota[:, None], req_iota[None, :], 0), axis=1
    )
    leg = leg.at[owner_of].get(mode="promise_in_bounds")
    leg = lax.all_to_all(leg, REQ, 0, 0, tiled=True)
    leg, pair_gate, up_w = barrier((leg, pair_gate, w_in[1]))
    pair_up = lax.ppermute(up_w, "zl", neighbours)
    held = leg[:, :span].reshape(new, feat)
    held_ids = leg[0, span:-1].reshape(TOPK, new).astype(jnp.int32)
    held_len = leg[0, -1, :1].astype(jnp.int32) * 32 + leg[0, -1, feat // 2 :][:1].astype(jnp.int32)

    full = lax.all_gather(held, TP, axis=1, tiled=True)
    parts = attend(
        held_len, full, gain, w_qkv, rope_tables(held_len, new), kv_cache, w_out
    )
    parts, pair_up = barrier((parts, pair_up))
    parts = lax.all_to_all(parts, TP, 0, 0, tiled=True)
    held_share = (held.astype(f32) + jnp.sum(parts.astype(f32), axis=0)).astype(bf16)

    slot_iota = jnp.arange(slots, dtype=jnp.int32)

    def chosen_of(ids):
        other = lax.ppermute(ids, "zh", [(0, 1), (1, 0)])
        both = jnp.where(zh == 0, jnp.stack([ids, other]), jnp.stack([other, ids]))
        picks = both.reshape(2, TOPK * new)
        onehot = (picks[:, :, None] == jnp.arange(experts_all, dtype=jnp.int32)).astype(bf16)
        order = jnp.arange(TOPK * new, dtype=jnp.int32)
        before = (order[:, None] > order[None, :]).astype(bf16)
        earlier = jnp.einsum("pq,rqe->rpe", before, onehot, preferred_element_type=f32)
        rank = jnp.sum(earlier * onehot.astype(f32), axis=2).astype(jnp.int32)
        rank = rank - (zl % 2) * SHARE
        there = picks - zh * plane
        which = jnp.arange(2, dtype=jnp.int32)[:, None]
        slot = there * rows + which * SHARE + rank
        here = (there >= 0) & (there < plane) & (rank >= 0) & (rank < SHARE)
        slot = jnp.where(here, slot, -1).reshape(2, TOPK, new)
        token = jnp.arange(new, dtype=jnp.int32)[None, :]
        chunk = token // span - zh * plane
        common = chunk * rows + 2 * SHARE + which * span + token % span
        common = jnp.where((chunk >= 0) & (chunk < plane), common, -1)
        chosen = (common.reshape(1, 2 * new) == slot_iota[:, None]).astype(bf16)
        for pick in range(TOPK):
            at = slot[:, pick].reshape(1, 2 * new)
            chosen = chosen + (at == slot_iota[:, None]).astype(bf16)
        return chosen

    chosen_held = chosen_of(held_ids)
    chosen_own = chosen_of(ids_t)

    outgoing = dispatch(chosen_held, spread(held_share, Z, 8))
    hidden_late, down_w, outgoing = barrier((hidden, w_down, outgoing))
    rows_mine = lax.all_to_all(
        outgoing.reshape(plane, rows, half), ("x", "y"), 0, 0, tiled=True
    )
    pair_down = lax.ppermute(down_w, "zl", neighbours)

    own_full = lax.all_gather(hidden_late, TP, axis=1, tiled=True)
    rows_mine, own_full, pair_down = barrier((rows_mine, own_full, pair_down))
    rows_theirs = swap_core(rows_mine)
    new_cache = new_kv(own_full, gain, w_qkv, rope_tables(lengths[0], new))[:, None]

    served_mine, served_theirs = experts(
        place,
        rows_mine,
        rows_theirs,
        2,
        ffn_gain[None],
        w_router.T,
        w_in,
        w_down,
        pair_gate,
        pair_up,
        pair_down,
        w_sh_in.swapaxes(1, 2),
        w_sh_down,
    )
    chunk, row = slot_iota // rows, slot_iota % rows
    common = row >= 2 * SHARE
    size = jnp.where(common, span, SHARE)
    base = jnp.where(common, 2 * SHARE, 0)
    which, inner = (row - base) // size, (row - base) % size
    slot_at = jnp.sum(
        jnp.where((which * plane + chunk)[:, None] == req_iota[None, :], holder_slot[None, :], 0),
        axis=1,
    )
    origin = (slot_at % plane) * rows + base + (slot_at // plane) * size + inner
    order = (origin[:, None] == slot_iota[None, :]).astype(bf16)
    served = reorder(
        order, served_mine.reshape(slots, half), swap_core(served_theirs).reshape(slots, half)
    )
    returned = lax.all_to_all(
        served.reshape(plane, rows, half), ("x", "y"), 0, 0, tiled=True
    ).reshape(slots, half)

    packed = combine(chosen_own, returned)
    summed = lax.all_to_all(packed, Z, 0, 0, tiled=True)
    out_hidden, last = finish(summed, reqs)

    last_all = lax.all_to_all(last, ("core", "x", "y"), 0, 0, tiled=True)
    tops, rms = head(last_all, final_gain[None], w_head)
    last_rms = rms.reshape(reqs)
    top_logit = jnp.max(lax.all_to_all(tops, ALL, 0, 0, tiled=True), axis=0)
    return (out_hidden, new_cache, last_rms, top_logit)


def solution(mesh):
    fine = Mesh(mesh.devices.reshape(SIZES), ALL)
    return jax.shard_map(
        local,
        mesh=fine,
        in_specs=(
            P(REQ, TP),
            P(),
            P(None, None, TP),
            P(TP, None),
            P(None, REQ, None, TP),
            P(),
            P(REQ),
            P(),
            P(),
            P(REQ, None),
            P(REQ, None, None, TP),
            P(REQ, TP, None),
            P(None, None, TP),
            P(TP, None),
            P(),
            P(REQ + TP, None),
        ),
        out_specs=(P(REQ, TP), P(None, REQ, None, TP), P(), P()),
        check_vma=False,
    )
```

```python
import jax
import jax.numpy as jnp
from jax import lax
from jax.sharding import Mesh, PartitionSpec as P
from jax.experimental import pallas as pl
from jax.experimental.pallas import tpu as pltpu

HD = 128
TOPK = 6
CAP = 32
SHARE = CAP // 2

REQ = ("zh", "x", "y")
TP = ("zl", "core")
COL = ("zh", "zl", "core")
Z = ("zh", "zl")
ALL = ("zh", "x", "y", "zl", "core")
SIZES = (2, 4, 4, 4, 2)

epsilon = 1e-06
bf16 = jnp.bfloat16
f32 = jnp.float32


def rms_scale(values, gain):
    return (
        values
        * lax.rsqrt(jnp.mean(values * values, axis=-1, keepdims=True) + epsilon)
        * gain.astype(f32)
    )


def rope_tables(length, new):
    half_len = HD // 2
    freqs = 10000.0 ** (-2.0 * jnp.arange(half_len, dtype=f32) / HD)
    positions = (length + jnp.arange(new, dtype=jnp.int32)).astype(f32)
    angles = positions[:, None] * freqs[None, :]
    cosine, sine = jnp.cos(angles), jnp.sin(angles)
    return jnp.concatenate([cosine, cosine], 1), jnp.concatenate([-sine, sine], 1)


def norm_rows(full_ref, gain_ref):
    return rms_scale(full_ref[...].astype(f32), gain_ref[...]).astype(bf16)


def rotate(values, cos_ref, sin_ref):
    heads = []
    for head in range(values.shape[1] // HD):
        piece = values[:, head * HD : (head + 1) * HD]
        heads.append(piece * cos_ref[...] + pltpu.roll(piece, HD // 2, 1) * sin_ref[...])
    return jnp.concatenate(heads, axis=1).astype(bf16)


def new_kv_body(full_ref, gain_ref, w_ref, cos_ref, sin_ref, o_ref):
    normed = norm_rows(full_ref, gain_ref)
    keys = jnp.dot(normed, w_ref[1], preferred_element_type=f32)
    o_ref[0] = rotate(keys, cos_ref, sin_ref)
    o_ref[1] = jnp.dot(normed, w_ref[2], preferred_element_type=f32).astype(bf16)


def new_kv(full, gain, w_qkv, tables):
    vm = pl.BlockSpec(memory_space=pltpu.VMEM)
    return pl.pallas_call(
        new_kv_body,
        out_shape=jax.ShapeDtypeStruct((2, full.shape[0], w_qkv.shape[2]), bf16),
        in_specs=[vm] * 5,
        out_specs=vm,
        name="new_kv",
    )(full, gain, w_qkv, *tables)


def attend_body(len_ref, full_ref, gain_ref, qkv_ref, cos_ref, sin_ref, kv_ref, w_ref, o_ref):
    length = len_ref[0]
    ctx = kv_ref.shape[2]
    new = full_ref.shape[0]
    normed = norm_rows(full_ref, gain_ref)
    q_all = rotate(jnp.dot(normed, qkv_ref[0], preferred_element_type=f32), cos_ref, sin_ref)
    k_all = rotate(jnp.dot(normed, qkv_ref[1], preferred_element_type=f32), cos_ref, sin_ref)
    v_all = jnp.dot(normed, qkv_ref[2], preferred_element_type=f32).astype(bf16)
    heads = []
    for head in range(q_all.shape[1] // HD):
        lanes = slice(head * HD, (head + 1) * HD)
        q = q_all[:, lanes]
        s_old = dot_nt(q, kv_ref[0, 0, :, lanes]) * HD ** (-0.5)
        s_new = dot_nt(q, k_all[:, lanes]) * HD ** (-0.5)
        seen_old = lax.broadcasted_iota(jnp.int32, (new, ctx), 1) < length
        seen_new = lax.broadcasted_iota(jnp.int32, (new, new), 1) <= lax.broadcasted_iota(
            jnp.int32, (new, new), 0
        )
        s_old = jnp.where(seen_old, s_old, -1e30)
        s_new = jnp.where(seen_new, s_new, -1e30)
        peak = jnp.maximum(
            jnp.max(s_old, axis=-1, keepdims=True), jnp.max(s_new, axis=-1, keepdims=True)
        )
        e_old = jnp.where(seen_old, jnp.exp(s_old - peak), 0.0)
        e_new = jnp.where(seen_new, jnp.exp(s_new - peak), 0.0)
        total = jnp.sum(e_old, axis=-1, keepdims=True) + jnp.sum(e_new, axis=-1, keepdims=True)
        w_old = (e_old / total).astype(bf16)
        w_new = (e_new / total).astype(bf16)
        out = jnp.dot(w_old, kv_ref[1, 0, :, lanes], preferred_element_type=f32) + jnp.dot(
            w_new, v_all[:, lanes], preferred_element_type=f32
        )
        heads.append(out.astype(bf16))
    attn = jnp.concatenate(heads, axis=1)
    wide = o_ref.shape[2]
    for part in range(o_ref.shape[0]):
        o_ref[part] = jnp.dot(
            attn, w_ref[:, part * wide : (part + 1) * wide], preferred_element_type=f32
        ).astype(bf16)


def attend(length, full, gain, w_qkv, tables, kv_cache, w_out):
    vm = pl.BlockSpec(memory_space=pltpu.VMEM)
    new = full.shape[0]
    feat = w_out.shape[0]
    return pl.pallas_call(
        attend_body,
        out_shape=jax.ShapeDtypeStruct((w_out.shape[1] // feat, new, feat), bf16),
        in_specs=[pl.BlockSpec(memory_space=pltpu.SMEM)] + [vm] * 7,
        out_specs=vm,
        name="attend",
    )(length, full, gain, w_qkv, *tables, kv_cache, w_out)


def spread(value, axes, count):
    wide = jnp.broadcast_to(value[None], (count,) + value.shape)
    return lax.all_to_all(wide, axes, 0, 0, tiled=True)


def swap_core(value):
    return lax.ppermute(value, "core", [(0, 1), (1, 0)])


def column_swap(value):
    return lax.ppermute(value, "zh", [(0, 1), (1, 0)])


def dot_nt(a, b):
    return lax.dot_general(a, b, (((1,), (1,)), ((), ())), preferred_element_type=f32)


def expert_rows(rows, gate_w, up_w, down_w):
    gate = dot_nt(rows, gate_w)
    up = dot_nt(rows, up_w)
    inner = (gate / (1.0 + jnp.exp(-gate)) * up).astype(bf16)
    return jnp.dot(inner, down_w, preferred_element_type=f32)


def drain(first, out, mine_ref, theirs_ref):
    feat = out.shape[1] // 8

    def store(even_ref, odd_ref):
        for part in range(4):
            piece = slice(part * feat, (part + 1) * feat)
            even_ref[:, piece] = out[:, 2 * part * feat : (2 * part + 1) * feat]
            odd_ref[:, piece] = out[:, (2 * part + 1) * feat : (2 * part + 2) * feat]

    @pl.when(first)
    def _():
        store(mine_ref, theirs_ref)

    @pl.when(jnp.logical_not(first))
    def _():
        store(theirs_ref, mine_ref)


def experts_body(
    place_ref, a_ref, b_ref, gain_ref, router_ref, in_ref, down_ref, pg_ref, pu_ref, pd_ref,
    si_ref, sd_ref, om_ref, ot_ref, xr_ref, xs_ref,
):
    first = place_ref[0] == 0
    feat = xr_ref.shape[1] // 8
    chunks, span = a_ref.shape[:2]
    routed = xr_ref.shape[0] // chunks
    shared = span - routed

    def fill(even_ref, odd_ref):
        for chunk in range(chunks):
            for part in range(4):
                piece = slice(part * feat, (part + 1) * feat)
                for odd, ref in enumerate((even_ref, odd_ref)):
                    lanes = slice((2 * part + odd) * feat, (2 * part + odd + 1) * feat)
                    rows = ref[chunk, :, piece].astype(f32)
                    xr_ref[chunk * routed : (chunk + 1) * routed, lanes] = rows[:routed]
                    xs_ref[chunk * shared : (chunk + 1) * shared, lanes] = rows[routed:]

    @pl.when(first)
    def _():
        fill(a_ref, b_ref)

    @pl.when(jnp.logical_not(first))
    def _():
        fill(b_ref, a_ref)

    rows = norm_rows(xr_ref, gain_ref)
    out = expert_rows(rows, in_ref[0], in_ref[1], down_ref[...])
    out = out + expert_rows(rows, pg_ref[...], pu_ref[...], pd_ref[...])
    logits = dot_nt(rows, router_ref[...])
    raised = jnp.exp(logits - jnp.max(logits, axis=-1, keepdims=True))
    own = lax.broadcasted_iota(jnp.int32, logits.shape, 1) == place_ref[1]
    picked = jnp.sum(jnp.where(own, raised, 0.0), axis=-1, keepdims=True)
    out = out * (picked / jnp.sum(raised, axis=-1, keepdims=True))
    common = norm_rows(xs_ref, gain_ref)
    common = expert_rows(common, si_ref[0], si_ref[1], sd_ref[...])
    common = common + xs_ref[...] * 0.125

    def store(even_ref, odd_ref):
        for chunk in range(chunks):
            top = out[chunk * routed : (chunk + 1) * routed]
            low = common[chunk * shared : (chunk + 1) * shared]
            both = jnp.concatenate([top, low], axis=0).astype(bf16)
            for part in range(4):
                piece = slice(part * feat, (part + 1) * feat)
                even_ref[chunk, :, piece] = both[:, 2 * part * feat : (2 * part + 1) * feat]
                odd_ref[chunk, :, piece] = both[:, (2 * part + 1) * feat : (2 * part + 2) * feat]

    @pl.when(first)
    def _():
        store(om_ref, ot_ref)

    @pl.when(jnp.logical_not(first))
    def _():
        store(ot_ref, om_ref)


def experts(place, rows_mine, rows_theirs, steps, *weights):
    count, span, half = rows_mine.shape
    width = 2 * half
    block = count // steps
    row_spec = pl.BlockSpec((block, span, half), lambda i: (i, 0, 0))

    def whole(array):
        zeros = (0,) * array.ndim
        return pl.BlockSpec(array.shape, lambda i: zeros)

    shape = jax.ShapeDtypeStruct(rows_mine.shape, bf16)
    return pl.pallas_call(
        experts_body,
        grid=(steps,),
        out_shape=(shape, shape),
        in_specs=[pl.BlockSpec(memory_space=pltpu.SMEM), row_spec, row_spec]
        + [whole(array) for array in weights],
        out_specs=(row_spec, row_spec),
        scratch_shapes=[
            pltpu.VMEM((block * 2 * SHARE, width), f32),
            pltpu.VMEM((block * (span - 2 * SHARE), width), f32),
        ],
        cost_estimate=pl.CostEstimate(
            flops=6 * count * span * width * 352,
            transcendentals=count * span * 352,
            bytes_accessed=8 * count * span * half + 18 * width * 176,
        ),
        name="experts",
    )(place, rows_mine, rows_theirs, *weights)


def reorder_body(order_ref, a_ref, b_ref, o_ref):
    total = (a_ref[...].astype(f32) + b_ref[...].astype(f32)).astype(bf16)
    o_ref[...] = jnp.dot(order_ref[...], total, preferred_element_type=f32).astype(bf16)


def reorder(order, a, b):
    vm = pl.BlockSpec(memory_space=pltpu.VMEM)
    return pl.pallas_call(
        reorder_body,
        out_shape=jax.ShapeDtypeStruct(a.shape, bf16),
        in_specs=[vm, vm, vm],
        out_specs=vm,
        name="reorder",
    )(order, a, b)


def dispatch_body(chosen_ref, parts_ref, out_ref):
    feat = parts_ref.shape[2]
    for part in range(4):
        both = jnp.concatenate([parts_ref[part], parts_ref[4 + part]], axis=0)
        out_ref[:, part * feat : (part + 1) * feat] = jnp.dot(
            chosen_ref[...], both, preferred_element_type=f32
        ).astype(bf16)


def dispatch(chosen_t, parts):
    vm = pl.BlockSpec(memory_space=pltpu.VMEM)
    return pl.pallas_call(
        dispatch_body,
        out_shape=jax.ShapeDtypeStruct((chosen_t.shape[0], 4 * parts.shape[2]), bf16),
        in_specs=[vm, vm],
        out_specs=vm,
        name="dispatch",
    )(chosen_t, parts)


def combine_body(chosen_ref, back_ref, out_ref):
    feat = out_ref.shape[2]
    new = chosen_ref.shape[1] // 2
    for zo in range(2):
        total = lax.dot_general(
            chosen_ref[:, zo * new : (zo + 1) * new],
            back_ref[...],
            (((0,), (0,)), ((), ())),
            preferred_element_type=f32,
        ).astype(bf16)
        for part in range(4):
            piece = total[:, part * feat : (part + 1) * feat]
            out_ref[zo * 4 + part, :new, :] = piece
            row = piece[new - 1 :, :]
            for dest in range(8):
                out_ref[dest, new + zo * 4 + part : new + zo * 4 + part + 1, :] = row


def combine(chosen_t, back):
    vm = pl.BlockSpec(memory_space=pltpu.VMEM)
    return pl.pallas_call(
        combine_body,
        out_shape=jax.ShapeDtypeStruct((8, chosen_t.shape[1] // 2 + 8, back.shape[1] // 4), bf16),
        in_specs=[vm, vm],
        out_specs=vm,
        name="combine",
    )(chosen_t, back)


def finish_body(parts_ref, out_ref, last_ref):
    new = out_ref.shape[0]
    total = parts_ref[0].astype(f32)
    for part in range(1, 8):
        total = total + parts_ref[part].astype(f32)
    out_ref[...] = total[:new].astype(bf16)
    for part in range(8):
        row = total[new + part : new + part + 1]
        for sub in range(2):
            piece = row[:, sub * 128 : (sub + 1) * 128]
            last_ref[:, part * 2 + sub : part * 2 + sub + 1, :] = jnp.broadcast_to(
                piece.astype(bf16)[None], (last_ref.shape[0], 1, 128)
            )


def finish(parts, copies):
    vm = pl.BlockSpec(memory_space=pltpu.VMEM)
    return pl.pallas_call(
        finish_body,
        out_shape=(
            jax.ShapeDtypeStruct((parts.shape[1] - 8, parts.shape[2]), bf16),
            jax.ShapeDtypeStruct((copies, 16, 128), bf16),
        ),
        in_specs=[vm],
        out_specs=(vm, vm),
        name="finish",
    )(parts)


def head_body(last_ref, gain_ref, w_ref, top_ref, rms_ref):
    plane = last_ref.shape[0] // 2
    rows = jnp.swapaxes(last_ref[...].astype(f32), 0, 1)
    halves = []
    for zo in range(2):
        pieces = []
        for part in range(4):
            for core in range(2):
                for sub in range(2):
                    pieces.append(
                        rows[(zo * 4 + part) * 2 + sub, core * plane : (core + 1) * plane]
                    )
        halves.append(jnp.concatenate(pieces, axis=1))
    tok = jnp.concatenate(halves, axis=0)
    rms = jnp.sqrt(jnp.mean(tok * tok, axis=-1, keepdims=True) + epsilon)
    head_in = (tok / rms * gain_ref[...].astype(f32)).astype(bf16)
    logits = lax.dot_general(
        w_ref[...], head_in, (((1,), (1,)), ((), ())), preferred_element_type=f32
    )
    top_ref[...] = jnp.broadcast_to(jnp.max(logits, axis=0, keepdims=True), top_ref.shape)
    rms_ref[...] = rms


def head(last, gain, w_head):
    vm = pl.BlockSpec(memory_space=pltpu.VMEM)
    rows = last.shape[0]
    return pl.pallas_call(
        head_body,
        out_shape=(
            jax.ShapeDtypeStruct((256, rows), f32),
            jax.ShapeDtypeStruct((rows, 1), f32),
        ),
        in_specs=[vm, vm, vm],
        out_specs=(vm, vm),
        name="head",
    )(last, gain, w_head)


def local(
    hidden,
    attn_gain,
    w_qkv,
    w_out,
    kv_cache,
    holder_slot,
    lengths,
    ffn_gain,
    w_router,
    expert_ids,
    w_exp_in,
    w_exp_down,
    w_sh_in,
    w_sh_down,
    final_gain,
    w_head,
):
    zh = lax.axis_index("zh")
    zl = lax.axis_index("zl")
    core = lax.axis_index("core")
    expert = lax.axis_index(REQ)
    new, feat = hidden.shape
    width = attn_gain.shape[0]
    half = width // 2
    experts_all = w_router.shape[1]
    plane = experts_all // 2
    reqs = holder_slot.shape[0]
    span = new // reqs
    rows = 2 * (SHARE + span)
    slots = plane * rows
    place = jnp.stack([core, expert]).astype(jnp.int32)
    gain = attn_gain[None]
    barrier = lax.optimization_barrier

    ids_t = expert_ids.T
    sizes = jnp.concatenate(
        [jnp.broadcast_to(lengths // 32, (feat // 2,)), jnp.broadcast_to(lengths % 32, (feat // 2,))]
    )
    meta = jnp.concatenate([ids_t.reshape(TOPK * new // feat, feat), sizes[None]]).astype(bf16)
    meta = jnp.broadcast_to(meta[None], (reqs,) + meta.shape)
    chunks = jnp.concatenate([hidden.reshape(reqs, span, feat), meta], axis=1)
    w_in = w_exp_in[0].swapaxes(1, 2)
    w_down = w_exp_down[0]
    leg = lax.all_to_all(chunks, REQ, 0, 0, tiled=True)
    ids_there, up_w = barrier((column_swap(ids_t), w_in[1]))
    leg, gate_w = barrier((leg, w_in[0]))

    neighbours = [(0, 1), (1, 0), (2, 3), (3, 2)]
    pair_up = lax.ppermute(up_w, "zl", neighbours)
    pair_gate = lax.ppermute(gate_w, "zl", neighbours)

    req_iota = jnp.arange(reqs, dtype=jnp.int32)
    owner_of = jnp.sum(
        jnp.where(holder_slot[None, :] == req_iota[:, None], req_iota[None, :], 0), axis=1
    )
    leg = leg.at[owner_of].get(mode="promise_in_bounds")
    leg = lax.all_to_all(leg, REQ, 0, 0, tiled=True)
    leg, pair_up = barrier((leg, pair_up))
    held = leg[:, :span].reshape(new, feat)
    held_ids = leg[0, span:-1].reshape(TOPK, new).astype(jnp.int32)
    held_len = leg[0, -1, :1].astype(jnp.int32) * 32 + leg[0, -1, feat // 2 :][:1].astype(jnp.int32)

    full = lax.all_gather(held, TP, axis=1, tiled=True)
    parts = attend(
        held_len, full, gain, w_qkv, rope_tables(held_len, new), kv_cache, w_out
    )
    parts, pair_gate = barrier((parts, pair_gate))
    parts = lax.all_to_all(parts, TP, 0, 0, tiled=True)
    held_share = (held.astype(f32) + jnp.sum(parts.astype(f32), axis=0)).astype(bf16)

    slot_iota = jnp.arange(slots, dtype=jnp.int32)

    def chosen_of(ids, other):
        both = jnp.where(zh == 0, jnp.stack([ids, other]), jnp.stack([other, ids]))
        picks = both.reshape(2, TOPK * new)
        onehot = (picks[:, :, None] == jnp.arange(experts_all, dtype=jnp.int32)).astype(bf16)
        order = jnp.arange(TOPK * new, dtype=jnp.int32)
        before = (order[:, None] > order[None, :]).astype(bf16)
        earlier = jnp.einsum("pq,rqe->rpe", before, onehot, preferred_element_type=f32)
        rank = jnp.sum(earlier * onehot.astype(f32), axis=2).astype(jnp.int32)
        rank = rank - (zl % 2) * SHARE
        there = picks - zh * plane
        which = jnp.arange(2, dtype=jnp.int32)[:, None]
        slot = there * rows + which * SHARE + rank
        here = (there >= 0) & (there < plane) & (rank >= 0) & (rank < SHARE)
        slot = jnp.where(here, slot, -1).reshape(2, TOPK, new)
        token = jnp.arange(new, dtype=jnp.int32)[None, :]
        chunk = token // span - zh * plane
        common = chunk * rows + 2 * SHARE + which * span + token % span
        common = jnp.where((chunk >= 0) & (chunk < plane), common, -1)
        chosen = (common.reshape(1, 2 * new) == slot_iota[:, None]).astype(bf16)
        for pick in range(TOPK):
            at = slot[:, pick].reshape(1, 2 * new)
            chosen = chosen + (at == slot_iota[:, None]).astype(bf16)
        return chosen

    chosen_held = chosen_of(held_ids, column_swap(held_ids))
    chosen_own = chosen_of(ids_t, ids_there)

    outgoing = dispatch(chosen_held, spread(held_share, Z, 8))
    down_w, outgoing = barrier((w_down, outgoing))
    rows_mine = lax.all_to_all(
        outgoing.reshape(plane, rows, half), ("x", "y"), 0, 0, tiled=True
    )
    pair_down = lax.ppermute(down_w, "zl", neighbours)

    rows_mine, pair_down = barrier((rows_mine, pair_down))
    rows_theirs = swap_core(rows_mine)
    served_mine, served_theirs = experts(
        place,
        rows_mine,
        rows_theirs,
        2,
        ffn_gain[None],
        w_router.T,
        w_in,
        w_down,
        pair_gate,
        pair_up,
        pair_down,
        w_sh_in.swapaxes(1, 2),
        w_sh_down,
    )
    chunk, row = slot_iota // rows, slot_iota % rows
    common = row >= 2 * SHARE
    size = jnp.where(common, span, SHARE)
    base = jnp.where(common, 2 * SHARE, 0)
    which, inner = (row - base) // size, (row - base) % size
    slot_at = jnp.sum(
        jnp.where((which * plane + chunk)[:, None] == req_iota[None, :], holder_slot[None, :], 0),
        axis=1,
    )
    origin = (slot_at % plane) * rows + base + (slot_at // plane) * size + inner
    order = (origin[:, None] == slot_iota[None, :]).astype(bf16)
    served = reorder(
        order, served_mine.reshape(slots, half), swap_core(served_theirs).reshape(slots, half)
    )
    served, hidden_late = barrier((served, hidden))
    returned = lax.all_to_all(
        served.reshape(plane, rows, half), ("x", "y"), 0, 0, tiled=True
    ).reshape(slots, half)

    own_full = lax.all_gather(hidden_late, TP, axis=1, tiled=True)
    returned, own_full = barrier((returned, own_full))
    new_cache = new_kv(own_full, gain, w_qkv, rope_tables(lengths[0], new))[:, None]

    packed = combine(chosen_own, returned)
    summed = lax.all_to_all(packed, Z, 0, 0, tiled=True)
    out_hidden, last = finish(summed, reqs)

    last_all = lax.all_to_all(last, ("core", "x", "y"), 0, 0, tiled=True)
    tops, rms = head(last_all, final_gain[None], w_head)
    last_rms = rms.reshape(reqs)
    top_logit = jnp.max(lax.all_to_all(tops, ALL, 0, 0, tiled=True), axis=0)
    return (out_hidden, new_cache, last_rms, top_logit)


def solution(mesh):
    fine = Mesh(mesh.devices.reshape(SIZES), ALL)
    return jax.shard_map(
        local,
        mesh=fine,
        in_specs=(
            P(REQ, TP),
            P(),
            P(None, None, TP),
            P(TP, None),
            P(None, REQ, None, TP),
            P(),
            P(REQ),
            P(),
            P(),
            P(REQ, None),
            P(REQ, None, None, TP),
            P(REQ, TP, None),
            P(None, None, TP),
            P(TP, None),
            P(),
            P(REQ + TP, None),
        ),
        out_specs=(P(REQ, TP), P(None, REQ, None, TP), P(), P()),
        check_vma=False,
    )
```

```python
import jax
import jax.numpy as jnp
from jax import lax
from jax.sharding import Mesh, PartitionSpec as P
from jax.experimental import pallas as pl
from jax.experimental.pallas import tpu as pltpu

HD = 128
TOPK = 6
CAP = 32
SHARE = CAP // 2

REQ = ("zh", "x", "y")
TP = ("zl", "core")
COL = ("zh", "zl", "core")
Z = ("zh", "zl")
ALL = ("zh", "x", "y", "zl", "core")
SIZES = (2, 4, 4, 4, 2)

epsilon = 1e-06
bf16 = jnp.bfloat16
f32 = jnp.float32


def rms_scale(values, gain):
    return (
        values
        * lax.rsqrt(jnp.mean(values * values, axis=-1, keepdims=True) + epsilon)
        * gain.astype(f32)
    )


def rope_tables(length, new):
    half_len = HD // 2
    freqs = 10000.0 ** (-2.0 * jnp.arange(half_len, dtype=f32) / HD)
    positions = (length + jnp.arange(new, dtype=jnp.int32)).astype(f32)
    angles = positions[:, None] * freqs[None, :]
    cosine, sine = jnp.cos(angles), jnp.sin(angles)
    return jnp.concatenate([cosine, cosine], 1), jnp.concatenate([-sine, sine], 1)


def norm_rows(full_ref, gain_ref):
    return rms_scale(full_ref[...].astype(f32), gain_ref[...]).astype(bf16)


def rotate(values, cos_ref, sin_ref):
    heads = []
    for head in range(values.shape[1] // HD):
        piece = values[:, head * HD : (head + 1) * HD]
        heads.append(piece * cos_ref[...] + pltpu.roll(piece, HD // 2, 1) * sin_ref[...])
    return jnp.concatenate(heads, axis=1).astype(bf16)


def new_kv_body(full_ref, gain_ref, w_ref, cos_ref, sin_ref, o_ref):
    normed = norm_rows(full_ref, gain_ref)
    keys = jnp.dot(normed, w_ref[1], preferred_element_type=f32)
    o_ref[0] = rotate(keys, cos_ref, sin_ref)
    o_ref[1] = jnp.dot(normed, w_ref[2], preferred_element_type=f32).astype(bf16)


def new_kv(full, gain, w_qkv, tables):
    vm = pl.BlockSpec(memory_space=pltpu.VMEM)
    return pl.pallas_call(
        new_kv_body,
        out_shape=jax.ShapeDtypeStruct((2, full.shape[0], w_qkv.shape[2]), bf16),
        in_specs=[vm] * 5,
        out_specs=vm,
        name="new_kv",
    )(full, gain, w_qkv, *tables)


def attend_body(place_ref, full_ref, gain_ref, qkv_ref, cos_ref, sin_ref, kv_ref, w_ref, o_ref):
    length = place_ref[0]
    core = place_ref[1]
    ctx = kv_ref.shape[2]
    new = full_ref.shape[0]
    normed = norm_rows(full_ref, gain_ref)
    q_all = rotate(jnp.dot(normed, qkv_ref[0], preferred_element_type=f32), cos_ref, sin_ref)
    k_all = rotate(jnp.dot(normed, qkv_ref[1], preferred_element_type=f32), cos_ref, sin_ref)
    v_all = jnp.dot(normed, qkv_ref[2], preferred_element_type=f32).astype(bf16)
    heads = []
    for head in range(q_all.shape[1] // HD):
        lanes = slice(head * HD, (head + 1) * HD)
        q = q_all[:, lanes]
        s_old = dot_nt(q, kv_ref[0, 0, :, lanes]) * HD ** (-0.5)
        s_new = dot_nt(q, k_all[:, lanes]) * HD ** (-0.5)
        seen_old = lax.broadcasted_iota(jnp.int32, (new, ctx), 1) < length
        seen_new = lax.broadcasted_iota(jnp.int32, (new, new), 1) <= lax.broadcasted_iota(
            jnp.int32, (new, new), 0
        )
        s_old = jnp.where(seen_old, s_old, -1e30)
        s_new = jnp.where(seen_new, s_new, -1e30)
        peak = jnp.maximum(
            jnp.max(s_old, axis=-1, keepdims=True), jnp.max(s_new, axis=-1, keepdims=True)
        )
        e_old = jnp.where(seen_old, jnp.exp(s_old - peak), 0.0)
        e_new = jnp.where(seen_new, jnp.exp(s_new - peak), 0.0)
        total = jnp.sum(e_old, axis=-1, keepdims=True) + jnp.sum(e_new, axis=-1, keepdims=True)
        w_old = (e_old / total).astype(bf16)
        w_new = (e_new / total).astype(bf16)
        out = jnp.dot(w_old, kv_ref[1, 0, :, lanes], preferred_element_type=f32) + jnp.dot(
            w_new, v_all[:, lanes], preferred_element_type=f32
        )
        heads.append(out.astype(bf16))
    attn = jnp.concatenate(heads, axis=1)
    wide = o_ref.shape[3]
    for part in range(2 * o_ref.shape[1]):
        at = core if part % 2 == 0 else 1 - core
        o_ref[at, part // 2] = jnp.dot(
            attn, w_ref[:, part * wide : (part + 1) * wide], preferred_element_type=f32
        ).astype(bf16)


def attend(place, full, gain, w_qkv, tables, kv_cache, w_out):
    vm = pl.BlockSpec(memory_space=pltpu.VMEM)
    new = full.shape[0]
    feat = w_out.shape[0]
    return pl.pallas_call(
        attend_body,
        out_shape=jax.ShapeDtypeStruct((2, w_out.shape[1] // feat // 2, new, feat), bf16),
        in_specs=[pl.BlockSpec(memory_space=pltpu.SMEM)] + [vm] * 7,
        out_specs=vm,
        name="attend",
    )(place, full, gain, w_qkv, *tables, kv_cache, w_out)


def spread(value, axes, count):
    wide = jnp.broadcast_to(value[None], (count,) + value.shape)
    return lax.all_to_all(wide, axes, 0, 0, tiled=True)


def swap_core(value):
    return lax.ppermute(value, "core", [(0, 1), (1, 0)])


def column_swap(value):
    return lax.ppermute(value, "zh", [(0, 1), (1, 0)])


def dot_nt(a, b):
    return lax.dot_general(a, b, (((1,), (1,)), ((), ())), preferred_element_type=f32)


def expert_rows(rows, gate_w, up_w, down_w):
    gate = dot_nt(rows, gate_w)
    up = dot_nt(rows, up_w)
    inner = (gate / (1.0 + jnp.exp(-gate)) * up).astype(bf16)
    return jnp.dot(inner, down_w, preferred_element_type=f32)


def drain(first, out, mine_ref, theirs_ref):
    feat = out.shape[1] // 8

    def store(even_ref, odd_ref):
        for part in range(4):
            piece = slice(part * feat, (part + 1) * feat)
            even_ref[:, piece] = out[:, 2 * part * feat : (2 * part + 1) * feat]
            odd_ref[:, piece] = out[:, (2 * part + 1) * feat : (2 * part + 2) * feat]

    @pl.when(first)
    def _():
        store(mine_ref, theirs_ref)

    @pl.when(jnp.logical_not(first))
    def _():
        store(theirs_ref, mine_ref)


def experts_body(
    place_ref, a_ref, b_ref, gain_ref, router_ref, in_ref, down_ref, pg_ref, pu_ref, pd_ref,
    si_ref, sd_ref, om_ref, ot_ref, xr_ref, xs_ref, ys_ref,
):
    first = place_ref[0] == 0
    feat = xr_ref.shape[1] // 8
    chunks, span = a_ref.shape[:2]
    routed = xr_ref.shape[0] // chunks
    shared = span - routed

    def fill(even_ref, odd_ref):
        for chunk in range(chunks):
            for part in range(4):
                piece = slice(part * feat, (part + 1) * feat)
                for odd, ref in enumerate((even_ref, odd_ref)):
                    lanes = slice((2 * part + odd) * feat, (2 * part + odd + 1) * feat)
                    rows = ref[chunk, :, piece].astype(f32)
                    xr_ref[chunk * routed : (chunk + 1) * routed, lanes] = rows[:routed]
                    xs_ref[chunk * shared : (chunk + 1) * shared, lanes] = rows[routed:]

    @pl.when(first)
    def _():
        fill(a_ref, b_ref)

    @pl.when(jnp.logical_not(first))
    def _():
        fill(b_ref, a_ref)

    common = norm_rows(xs_ref, gain_ref)
    common = expert_rows(common, si_ref[0], si_ref[1], sd_ref[...])
    common = common + xs_ref[...] * 0.125
    half = shared // 2
    for piece in range(2 * chunks):
        ys_ref[piece, :half, :] = common[piece * half : (piece + 1) * half]

    rows = norm_rows(xr_ref, gain_ref)
    out = expert_rows(rows, in_ref[0], in_ref[1], down_ref[...])
    out = out + expert_rows(rows, pg_ref[...], pu_ref[...], pd_ref[...])
    logits = dot_nt(rows, router_ref[...])
    raised = jnp.exp(logits - jnp.max(logits, axis=-1, keepdims=True))
    own = lax.broadcasted_iota(jnp.int32, logits.shape, 1) == place_ref[1]
    picked = jnp.sum(jnp.where(own, raised, 0.0), axis=-1, keepdims=True)
    xr_ref[...] = out * (picked / jnp.sum(raised, axis=-1, keepdims=True))

    def store(even_ref, odd_ref):
        for chunk in range(chunks):
            origin = [place_ref[2 + 2 * chunk + zo] for zo in range(2)]
            size = routed // 2
            top = [xr_ref[pl.ds(pl.multiple_of(at * size, size), size), :] for at in origin]
            low = [ys_ref[at, :half, :] for at in origin]
            both = jnp.concatenate(top + low, axis=0).astype(bf16)
            for part in range(4):
                piece = slice(part * feat, (part + 1) * feat)
                even_ref[chunk, :, piece] = both[:, 2 * part * feat : (2 * part + 1) * feat]
                odd_ref[chunk, :, piece] = both[:, (2 * part + 1) * feat : (2 * part + 2) * feat]

    @pl.when(first)
    def _():
        store(om_ref, ot_ref)

    @pl.when(jnp.logical_not(first))
    def _():
        store(ot_ref, om_ref)


def experts(place, rows_mine, rows_theirs, *weights):
    vm = pl.BlockSpec(memory_space=pltpu.VMEM)
    count, span, half = rows_mine.shape
    width = 2 * half
    shape = jax.ShapeDtypeStruct(rows_mine.shape, bf16)
    shared = span - 2 * SHARE
    return pl.pallas_call(
        experts_body,
        out_shape=(shape, shape),
        in_specs=[pl.BlockSpec(memory_space=pltpu.SMEM)] + [vm] * (2 + len(weights)),
        out_specs=(vm, vm),
        scratch_shapes=[
            pltpu.VMEM((count * 2 * SHARE, width), f32),
            pltpu.VMEM((count * shared, width), f32),
            pltpu.VMEM((2 * count, 8, width), f32),
        ],
        cost_estimate=pl.CostEstimate(
            flops=6 * count * span * width * 352,
            transcendentals=count * span * 352,
            bytes_accessed=8 * count * span * half + 18 * width * 176,
        ),
        name="experts",
    )(place, rows_mine, rows_theirs, *weights)


def dispatch_body(chosen_ref, parts_ref, out_ref):
    feat = parts_ref.shape[2]
    for part in range(4):
        both = jnp.concatenate([parts_ref[part], parts_ref[4 + part]], axis=0)
        out_ref[:, part * feat : (part + 1) * feat] = jnp.dot(
            chosen_ref[...], both, preferred_element_type=f32
        ).astype(bf16)


def dispatch(chosen_t, parts):
    vm = pl.BlockSpec(memory_space=pltpu.VMEM)
    return pl.pallas_call(
        dispatch_body,
        out_shape=jax.ShapeDtypeStruct((chosen_t.shape[0], 4 * parts.shape[2]), bf16),
        in_specs=[vm, vm],
        out_specs=vm,
        name="dispatch",
    )(chosen_t, parts)


def combine_body(chosen_ref, back_ref, out_ref):
    feat = out_ref.shape[2]
    new = chosen_ref.shape[1] // 2
    for zo in range(2):
        total = lax.dot_general(
            chosen_ref[:, zo * new : (zo + 1) * new],
            back_ref[...],
            (((0,), (0,)), ((), ())),
            preferred_element_type=f32,
        ).astype(bf16)
        for part in range(4):
            piece = total[:, part * feat : (part + 1) * feat]
            out_ref[zo * 4 + part, :new, :] = piece
            row = piece[new - 1 :, :]
            for dest in range(8):
                out_ref[dest, new + zo * 4 + part : new + zo * 4 + part + 1, :] = row


def combine(chosen_t, back):
    vm = pl.BlockSpec(memory_space=pltpu.VMEM)
    return pl.pallas_call(
        combine_body,
        out_shape=jax.ShapeDtypeStruct((8, chosen_t.shape[1] // 2 + 8, back.shape[1] // 4), bf16),
        in_specs=[vm, vm],
        out_specs=vm,
        name="combine",
    )(chosen_t, back)


def finish_body(parts_ref, out_ref, last_ref):
    new = out_ref.shape[0]
    total = parts_ref[0].astype(f32)
    for part in range(1, 8):
        total = total + parts_ref[part].astype(f32)
    out_ref[...] = total[:new].astype(bf16)
    for part in range(8):
        row = total[new + part : new + part + 1]
        for sub in range(2):
            piece = row[:, sub * 128 : (sub + 1) * 128]
            last_ref[:, part * 2 + sub : part * 2 + sub + 1, :] = jnp.broadcast_to(
                piece.astype(bf16)[None], (last_ref.shape[0], 1, 128)
            )


def finish(parts, copies):
    vm = pl.BlockSpec(memory_space=pltpu.VMEM)
    return pl.pallas_call(
        finish_body,
        out_shape=(
            jax.ShapeDtypeStruct((parts.shape[1] - 8, parts.shape[2]), bf16),
            jax.ShapeDtypeStruct((copies, 16, 128), bf16),
        ),
        in_specs=[vm],
        out_specs=(vm, vm),
        name="finish",
    )(parts)


def head_body(last_ref, gain_ref, w_ref, top_ref, rms_ref):
    plane = last_ref.shape[0] // 2
    rows = jnp.swapaxes(last_ref[...].astype(f32), 0, 1)
    halves = []
    for zo in range(2):
        pieces = []
        for part in range(4):
            for core in range(2):
                for sub in range(2):
                    pieces.append(
                        rows[(zo * 4 + part) * 2 + sub, core * plane : (core + 1) * plane]
                    )
        halves.append(jnp.concatenate(pieces, axis=1))
    tok = jnp.concatenate(halves, axis=0)
    rms = jnp.sqrt(jnp.mean(tok * tok, axis=-1, keepdims=True) + epsilon)
    head_in = (tok / rms * gain_ref[...].astype(f32)).astype(bf16)
    logits = lax.dot_general(
        w_ref[...], head_in, (((1,), (1,)), ((), ())), preferred_element_type=f32
    )
    top_ref[...] = jnp.broadcast_to(jnp.max(logits, axis=0, keepdims=True), top_ref.shape)
    rms_ref[...] = rms


def head(last, gain, w_head):
    vm = pl.BlockSpec(memory_space=pltpu.VMEM)
    rows = last.shape[0]
    return pl.pallas_call(
        head_body,
        out_shape=(
            jax.ShapeDtypeStruct((256, rows), f32),
            jax.ShapeDtypeStruct((rows, 1), f32),
        ),
        in_specs=[vm, vm, vm],
        out_specs=(vm, vm),
        name="head",
    )(last, gain, w_head)


def local(
    hidden,
    attn_gain,
    w_qkv,
    w_out,
    kv_cache,
    holder_slot,
    lengths,
    ffn_gain,
    w_router,
    expert_ids,
    w_exp_in,
    w_exp_down,
    w_sh_in,
    w_sh_down,
    final_gain,
    w_head,
):
    zh = lax.axis_index("zh")
    zl = lax.axis_index("zl")
    core = lax.axis_index("core")
    expert = lax.axis_index(REQ)
    new, feat = hidden.shape
    width = attn_gain.shape[0]
    half = width // 2
    experts_all = w_router.shape[1]
    plane = experts_all // 2
    reqs = holder_slot.shape[0]
    span = new // reqs
    rows = 2 * (SHARE + span)
    slots = plane * rows
    slot_at = holder_slot.reshape(2, plane).T.reshape(reqs)
    order = (slot_at % plane) * 2 + slot_at // plane
    place = jnp.concatenate([jnp.stack([core, expert]).astype(jnp.int32), order])
    barrier = lax.optimization_barrier

    ids_t = expert_ids.T
    sizes = jnp.concatenate(
        [jnp.broadcast_to(lengths // 32, (feat // 2,)), jnp.broadcast_to(lengths % 32, (feat // 2,))]
    )
    meta = jnp.concatenate([ids_t.reshape(TOPK * new // feat, feat), sizes[None]]).astype(bf16)
    meta = jnp.broadcast_to(meta[None], (reqs,) + meta.shape)
    chunks = jnp.concatenate([hidden.reshape(reqs, span, feat), meta], axis=1)
    w_in = w_exp_in[0].swapaxes(1, 2)
    w_down = w_exp_down[0]
    neighbours = [(0, 1), (1, 0), (2, 3), (3, 2)]
    pair_gate = lax.ppermute(w_in[0], "zl", neighbours)
    leg = lax.all_to_all(chunks, REQ, 0, 0, tiled=True)
    ids_there, up_w = barrier((column_swap(ids_t), w_in[1]))

    pair_up = lax.ppermute(up_w, "zl", neighbours)

    req_iota = jnp.arange(reqs, dtype=jnp.int32)
    owner_of = jnp.sum(
        jnp.where(holder_slot[None, :] == req_iota[:, None], req_iota[None, :], 0), axis=1
    )
    leg = leg.at[owner_of].get(mode="promise_in_bounds")
    leg = lax.all_to_all(leg, REQ, 0, 0, tiled=True)
    leg, pair_gate, gain, gain_ffn, gain_final, place = barrier(
        (leg, pair_gate, attn_gain[None], ffn_gain[None], final_gain[None], place)
    )
    held = leg[:, :span].reshape(new, feat)
    held_ids = leg[0, span:-1].reshape(TOPK, new).astype(jnp.int32)
    held_len = leg[0, -1, :1].astype(jnp.int32) * 32 + leg[0, -1, feat // 2 :][:1].astype(jnp.int32)

    full = lax.all_gather(held, TP, axis=1, tiled=True)
    parts = attend(
        jnp.concatenate([held_len, place[:1]]),
        full,
        gain,
        w_qkv,
        rope_tables(held_len, new),
        kv_cache,
        w_out,
    )
    parts, pair_up = barrier((parts, pair_up))
    parts = (parts[0].astype(f32) + swap_core(parts[1]).astype(f32)).astype(bf16)
    parts, held_ids = barrier((parts, held_ids))
    parts = lax.all_to_all(parts, "zl", 0, 0, tiled=True)
    held_share = (held.astype(f32) + jnp.sum(parts.astype(f32), axis=0)).astype(bf16)

    slot_iota = jnp.arange(slots, dtype=jnp.int32)

    def chosen_of(ids, other):
        both = jnp.where(zh == 0, jnp.stack([ids, other]), jnp.stack([other, ids]))
        picks = both.reshape(2, TOPK * new)
        onehot = (picks[:, :, None] == jnp.arange(experts_all, dtype=jnp.int32)).astype(bf16)
        order = jnp.arange(TOPK * new, dtype=jnp.int32)
        before = (order[:, None] > order[None, :]).astype(bf16)
        earlier = jnp.einsum("pq,rqe->rpe", before, onehot, preferred_element_type=f32)
        rank = jnp.sum(earlier * onehot.astype(f32), axis=2).astype(jnp.int32)
        rank = rank - (zl % 2) * SHARE
        there = picks - zh * plane
        which = jnp.arange(2, dtype=jnp.int32)[:, None]
        slot = there * rows + which * SHARE + rank
        here = (there >= 0) & (there < plane) & (rank >= 0) & (rank < SHARE)
        slot = jnp.where(here, slot, -1).reshape(2, TOPK, new)
        token = jnp.arange(new, dtype=jnp.int32)[None, :]
        chunk = token // span - zh * plane
        common = chunk * rows + 2 * SHARE + which * span + token % span
        common = jnp.where((chunk >= 0) & (chunk < plane), common, -1)
        chosen = (common.reshape(1, 2 * new) == slot_iota[:, None]).astype(bf16)
        for pick in range(TOPK):
            at = slot[:, pick].reshape(1, 2 * new)
            chosen = chosen + (at == slot_iota[:, None]).astype(bf16)
        return chosen

    chosen_held = chosen_of(held_ids, column_swap(held_ids))
    chosen_own = chosen_of(ids_t, ids_there)

    outgoing = dispatch(chosen_held, spread(held_share, Z, 8))
    down_w, outgoing = barrier((w_down, outgoing))
    rows_mine = lax.all_to_all(
        outgoing.reshape(plane, rows, half), ("x", "y"), 0, 0, tiled=True
    )
    pair_down = lax.ppermute(down_w, "zl", neighbours)

    rows_mine, pair_down = barrier((rows_mine, pair_down))
    rows_theirs = swap_core(rows_mine)
    served_mine, served_theirs = experts(
        place,
        rows_mine,
        rows_theirs,
        gain_ffn,
        w_router.T,
        w_in,
        w_down,
        pair_gate,
        pair_up,
        pair_down,
        w_sh_in.swapaxes(1, 2),
        w_sh_down,
    )
    served = (served_mine.astype(f32) + swap_core(served_theirs).astype(f32)).astype(bf16)
    served, hidden_late = barrier((served, hidden))
    returned = lax.all_to_all(served, ("x", "y"), 0, 0, tiled=True).reshape(slots, half)

    own_full = lax.all_gather(hidden_late, TP, axis=1, tiled=True)
    returned, own_full = barrier((returned, own_full))
    new_cache = new_kv(own_full, gain, w_qkv, rope_tables(lengths[0], new))[:, None]

    packed = combine(chosen_own, returned)
    summed = lax.all_to_all(packed, Z, 0, 0, tiled=True)
    out_hidden, last = finish(summed, reqs)

    last_all = lax.all_to_all(last, ("core", "x", "y"), 0, 0, tiled=True)
    tops, rms = head(last_all, gain_final, w_head)
    last_rms = rms.reshape(reqs)
    top_logit = jnp.max(lax.all_to_all(tops, ALL, 0, 0, tiled=True), axis=0)
    return (out_hidden, new_cache, last_rms, top_logit)


def solution(mesh):
    fine = Mesh(mesh.devices.reshape(SIZES), ALL)
    return jax.shard_map(
        local,
        mesh=fine,
        in_specs=(
            P(REQ, TP),
            P(),
            P(None, None, TP),
            P(TP, None),
            P(None, REQ, None, TP),
            P(),
            P(REQ),
            P(),
            P(),
            P(REQ, None),
            P(REQ, None, None, TP),
            P(REQ, TP, None),
            P(None, None, TP),
            P(TP, None),
            P(),
            P(REQ + TP, None),
        ),
        out_specs=(P(REQ, TP), P(None, REQ, None, TP), P(), P()),
        check_vma=False,
    )
```

```python
import jax
import jax.numpy as jnp
from jax import lax
from jax.sharding import Mesh, PartitionSpec as P
from jax.experimental import pallas as pl
from jax.experimental.pallas import tpu as pltpu

HD = 128
TOPK = 6
CAP = 32
SHARE = CAP // 2

REQ = ("zh", "x", "y")
TP = ("zl", "core")
COL = ("zh", "zl", "core")
Z = ("zh", "zl")
ALL = ("zh", "x", "y", "zl", "core")
SIZES = (2, 4, 4, 4, 2)

epsilon = 1e-06
bf16 = jnp.bfloat16
f32 = jnp.float32


def rms_scale(values, gain):
    return (
        values
        * lax.rsqrt(jnp.mean(values * values, axis=-1, keepdims=True) + epsilon)
        * gain.astype(f32)
    )


def rope_tables(length, new):
    half_len = HD // 2
    freqs = 10000.0 ** (-2.0 * jnp.arange(half_len, dtype=f32) / HD)
    positions = (length + jnp.arange(new, dtype=jnp.int32)).astype(f32)
    angles = positions[:, None] * freqs[None, :]
    return jnp.cos(angles), jnp.sin(angles)


def norm_rows(full_ref, gain_ref):
    return rms_scale(full_ref[...].astype(f32), gain_ref[...]).astype(bf16)


def rotate(values, cos_ref, sin_ref):
    cosine = jnp.concatenate([cos_ref[...], cos_ref[...]], axis=1)
    sine = jnp.concatenate([-sin_ref[...], sin_ref[...]], axis=1)
    heads = []
    for head in range(values.shape[1] // HD):
        piece = values[:, head * HD : (head + 1) * HD]
        heads.append(piece * cosine + pltpu.roll(piece, HD // 2, 1) * sine)
    return jnp.concatenate(heads, axis=1).astype(bf16)


def new_kv_body(full_ref, gain_ref, w_ref, cos_ref, sin_ref, o_ref):
    normed = norm_rows(full_ref, gain_ref)
    keys = jnp.dot(normed, w_ref[1], preferred_element_type=f32)
    o_ref[0] = rotate(keys, cos_ref, sin_ref)
    o_ref[1] = jnp.dot(normed, w_ref[2], preferred_element_type=f32).astype(bf16)


def new_kv(full, gain, w_qkv, tables):
    vm = pl.BlockSpec(memory_space=pltpu.VMEM)
    return pl.pallas_call(
        new_kv_body,
        out_shape=jax.ShapeDtypeStruct((2, full.shape[0], w_qkv.shape[2]), bf16),
        in_specs=[vm] * 5,
        out_specs=vm,
        name="new_kv",
    )(full, gain, w_qkv, *tables)


def attend_body(
    len_ref, place_ref, full_ref, gain_ref, qkv_ref, cos_ref, sin_ref, kv_ref, w_ref, om_ref, ot_ref
):
    length = len_ref[0]
    first = place_ref[0] == 0
    ctx = kv_ref.shape[2]
    new = full_ref.shape[0]
    normed = norm_rows(full_ref, gain_ref)
    q_all = rotate(jnp.dot(normed, qkv_ref[0], preferred_element_type=f32), cos_ref, sin_ref)
    k_all = rotate(jnp.dot(normed, qkv_ref[1], preferred_element_type=f32), cos_ref, sin_ref)
    v_all = jnp.dot(normed, qkv_ref[2], preferred_element_type=f32).astype(bf16)
    heads = []
    for head in range(q_all.shape[1] // HD):
        lanes = slice(head * HD, (head + 1) * HD)
        q = q_all[:, lanes]
        s_old = dot_nt(q, kv_ref[0, 0, :, lanes]) * HD ** (-0.5)
        s_new = dot_nt(q, k_all[:, lanes]) * HD ** (-0.5)
        seen_old = lax.broadcasted_iota(jnp.int32, (new, ctx), 1) < length
        seen_new = lax.broadcasted_iota(jnp.int32, (new, new), 1) <= lax.broadcasted_iota(
            jnp.int32, (new, new), 0
        )
        s_old = jnp.where(seen_old, s_old, -1e30)
        s_new = jnp.where(seen_new, s_new, -1e30)
        peak = jnp.maximum(
            jnp.max(s_old, axis=-1, keepdims=True), jnp.max(s_new, axis=-1, keepdims=True)
        )
        e_old = jnp.where(seen_old, jnp.exp(s_old - peak), 0.0)
        e_new = jnp.where(seen_new, jnp.exp(s_new - peak), 0.0)
        total = jnp.sum(e_old, axis=-1, keepdims=True) + jnp.sum(e_new, axis=-1, keepdims=True)
        w_old = (e_old / total).astype(bf16)
        w_new = (e_new / total).astype(bf16)
        out = jnp.dot(w_old, kv_ref[1, 0, :, lanes], preferred_element_type=f32) + jnp.dot(
            w_new, v_all[:, lanes], preferred_element_type=f32
        )
        heads.append(out.astype(bf16))
    attn = jnp.concatenate(heads, axis=1)
    wide = om_ref.shape[2]

    def store(even_ref, odd_ref):
        for part in range(2 * om_ref.shape[0]):
            ref = odd_ref if part % 2 else even_ref
            ref[part // 2] = jnp.dot(
                attn, w_ref[:, part * wide : (part + 1) * wide], preferred_element_type=f32
            ).astype(bf16)

    @pl.when(first)
    def _():
        store(om_ref, ot_ref)

    @pl.when(jnp.logical_not(first))
    def _():
        store(ot_ref, om_ref)


def attend(length, place, full, gain, w_qkv, tables, kv_cache, w_out):
    vm = pl.BlockSpec(memory_space=pltpu.VMEM)
    new = full.shape[0]
    feat = w_out.shape[0]
    shape = jax.ShapeDtypeStruct((w_out.shape[1] // feat // 2, new, feat), bf16)
    return pl.pallas_call(
        attend_body,
        out_shape=(shape, shape),
        in_specs=[pl.BlockSpec(memory_space=pltpu.SMEM)] * 2 + [vm] * 7,
        out_specs=(vm, vm),
        name="attend",
    )(length, place, full, gain, w_qkv, *tables, kv_cache, w_out)


def spread(value, axes, count):
    wide = jnp.broadcast_to(value[None], (count,) + value.shape)
    return lax.all_to_all(wide, axes, 0, 0, tiled=True)


def swap_core(value):
    return lax.ppermute(value, "core", [(0, 1), (1, 0)])


def column_swap(value):
    return lax.ppermute(value, "zh", [(0, 1), (1, 0)])


def dot_nt(a, b):
    return lax.dot_general(a, b, (((1,), (1,)), ((), ())), preferred_element_type=f32)


def expert_rows(rows, gate_w, up_w, down_w):
    gate = dot_nt(rows, gate_w)
    up = dot_nt(rows, up_w)
    inner = (gate / (1.0 + jnp.exp(-gate)) * up).astype(bf16)
    return jnp.dot(inner, down_w, preferred_element_type=f32)


def drain(first, out, mine_ref, theirs_ref):
    feat = out.shape[1] // 8

    def store(even_ref, odd_ref):
        for part in range(4):
            piece = slice(part * feat, (part + 1) * feat)
            even_ref[:, piece] = out[:, 2 * part * feat : (2 * part + 1) * feat]
            odd_ref[:, piece] = out[:, (2 * part + 1) * feat : (2 * part + 2) * feat]

    @pl.when(first)
    def _():
        store(mine_ref, theirs_ref)

    @pl.when(jnp.logical_not(first))
    def _():
        store(theirs_ref, mine_ref)


def experts_body(
    place_ref, a_ref, b_ref, gain_ref, router_ref, in_ref, down_ref, pg_ref, pu_ref, pd_ref,
    si_ref, sd_ref, om_ref, ot_ref, xr_ref, xs_ref, ys_ref,
):
    first = place_ref[0] == 0
    feat = xr_ref.shape[1] // 8
    chunks, span = a_ref.shape[:2]
    routed = xr_ref.shape[0] // chunks
    shared = span - routed

    def fill(even_ref, odd_ref):
        for chunk in range(chunks):
            for part in range(4):
                piece = slice(part * feat, (part + 1) * feat)
                for odd, ref in enumerate((even_ref, odd_ref)):
                    lanes = slice((2 * part + odd) * feat, (2 * part + odd + 1) * feat)
                    rows = ref[chunk, :, piece].astype(f32)
                    xr_ref[chunk * routed : (chunk + 1) * routed, lanes] = rows[:routed]
                    xs_ref[chunk * shared : (chunk + 1) * shared, lanes] = rows[routed:]

    @pl.when(first)
    def _():
        fill(a_ref, b_ref)

    @pl.when(jnp.logical_not(first))
    def _():
        fill(b_ref, a_ref)

    common = norm_rows(xs_ref, gain_ref)
    common = expert_rows(common, si_ref[0], si_ref[1], sd_ref[...])
    common = common + xs_ref[...] * 0.125
    half = shared // 2
    for piece in range(2 * chunks):
        ys_ref[piece, :half, :] = common[piece * half : (piece + 1) * half]

    rows = norm_rows(xr_ref, gain_ref)
    out = expert_rows(rows, in_ref[0], in_ref[1], down_ref[...])
    out = out + expert_rows(rows, pg_ref[...], pu_ref[...], pd_ref[...])
    logits = dot_nt(rows, router_ref[...])
    raised = jnp.exp(logits - jnp.max(logits, axis=-1, keepdims=True))
    own = lax.broadcasted_iota(jnp.int32, logits.shape, 1) == place_ref[1]
    picked = jnp.sum(jnp.where(own, raised, 0.0), axis=-1, keepdims=True)
    xr_ref[...] = out * (picked / jnp.sum(raised, axis=-1, keepdims=True))

    def store(even_ref, odd_ref):
        for chunk in range(chunks):
            origin = [place_ref[2 + 2 * chunk + zo] for zo in range(2)]
            size = routed // 2
            top = [xr_ref[pl.ds(pl.multiple_of(at * size, size), size), :] for at in origin]
            low = [ys_ref[at, :half, :] for at in origin]
            both = jnp.concatenate(top + low, axis=0).astype(bf16)
            for part in range(4):
                piece = slice(part * feat, (part + 1) * feat)
                even_ref[chunk, :, piece] = both[:, 2 * part * feat : (2 * part + 1) * feat]
                odd_ref[chunk, :, piece] = both[:, (2 * part + 1) * feat : (2 * part + 2) * feat]

    @pl.when(first)
    def _():
        store(om_ref, ot_ref)

    @pl.when(jnp.logical_not(first))
    def _():
        store(ot_ref, om_ref)


def experts(place, rows_mine, rows_theirs, *weights):
    vm = pl.BlockSpec(memory_space=pltpu.VMEM)
    count, span, half = rows_mine.shape
    width = 2 * half
    shape = jax.ShapeDtypeStruct(rows_mine.shape, bf16)
    shared = span - 2 * SHARE
    return pl.pallas_call(
        experts_body,
        out_shape=(shape, shape),
        in_specs=[pl.BlockSpec(memory_space=pltpu.SMEM)] + [vm] * (2 + len(weights)),
        out_specs=(vm, vm),
        scratch_shapes=[
            pltpu.VMEM((count * 2 * SHARE, width), f32),
            pltpu.VMEM((count * shared, width), f32),
            pltpu.VMEM((2 * count, 8, width), f32),
        ],
        cost_estimate=pl.CostEstimate(
            flops=6 * count * span * width * 352,
            transcendentals=count * span * 352,
            bytes_accessed=8 * count * span * half + 18 * width * 176,
        ),
        name="experts",
    )(place, rows_mine, rows_theirs, *weights)


def dispatch_body(chosen_ref, parts_ref, out_ref):
    feat = parts_ref.shape[2]
    for part in range(4):
        both = jnp.concatenate([parts_ref[part], parts_ref[4 + part]], axis=0)
        out_ref[:, part * feat : (part + 1) * feat] = jnp.dot(
            chosen_ref[...], both, preferred_element_type=f32
        ).astype(bf16)


def dispatch(chosen_t, parts):
    vm = pl.BlockSpec(memory_space=pltpu.VMEM)
    return pl.pallas_call(
        dispatch_body,
        out_shape=jax.ShapeDtypeStruct((chosen_t.shape[0], 4 * parts.shape[2]), bf16),
        in_specs=[vm, vm],
        out_specs=vm,
        name="dispatch",
    )(chosen_t, parts)


def combine_body(chosen_ref, back_ref, out_ref):
    feat = out_ref.shape[2]
    new = chosen_ref.shape[0] // 2
    last = []
    for zo in range(2):
        total = jnp.dot(
            chosen_ref[zo * new : (zo + 1) * new, :], back_ref[...], preferred_element_type=f32
        )
        for part in range(4):
            piece = total[:, part * feat : (part + 1) * feat]
            out_ref[zo * 4 + part, :new, :] = piece.astype(bf16)
            last.append(piece[new - 1 :, :])
    last = jnp.concatenate(last, axis=0).astype(bf16)
    for dest in range(8):
        out_ref[dest, new:, :] = last


def combine(chosen, back):
    vm = pl.BlockSpec(memory_space=pltpu.VMEM)
    return pl.pallas_call(
        combine_body,
        out_shape=jax.ShapeDtypeStruct((8, chosen.shape[0] // 2 + 8, back.shape[1] // 4), bf16),
        in_specs=[vm, vm],
        out_specs=vm,
        name="combine",
    )(chosen, back)


def finish_body(parts_ref, out_ref, last_ref):
    new, feat = out_ref.shape
    total = parts_ref[0].astype(f32)
    for part in range(1, 8):
        total = total + parts_ref[part].astype(f32)
    out_ref[...] = total[:new].astype(bf16)
    last = total[new:].astype(bf16).astype(f32)
    last = jnp.concatenate([last[:, : feat // 2], last[:, feat // 2 :]], axis=0).astype(bf16)
    last_ref[...] = jnp.broadcast_to(last[None], last_ref.shape)


def finish(parts, copies):
    vm = pl.BlockSpec(memory_space=pltpu.VMEM)
    return pl.pallas_call(
        finish_body,
        out_shape=(
            jax.ShapeDtypeStruct((parts.shape[1] - 8, parts.shape[2]), bf16),
            jax.ShapeDtypeStruct((copies, 16, 128), bf16),
        ),
        in_specs=[vm],
        out_specs=(vm, vm),
        name="finish",
    )(parts)


def head_body(last_ref, gain_ref, w_ref, top_ref, rms_ref):
    plane = last_ref.shape[0] // 2
    rows = jnp.swapaxes(last_ref[...].astype(f32), 0, 1)
    halves = []
    for zo in range(2):
        pieces = []
        for part in range(4):
            for core in range(2):
                for sub in range(2):
                    pieces.append(
                        rows[sub * 8 + zo * 4 + part, core * plane : (core + 1) * plane]
                    )
        halves.append(jnp.concatenate(pieces, axis=1))
    tok = jnp.concatenate(halves, axis=0)
    rms = jnp.sqrt(jnp.mean(tok * tok, axis=-1, keepdims=True) + epsilon)
    head_in = (tok / rms * gain_ref[...].astype(f32)).astype(bf16)
    logits = lax.dot_general(
        w_ref[...], head_in, (((1,), (1,)), ((), ())), preferred_element_type=f32
    )
    top_ref[...] = jnp.broadcast_to(jnp.max(logits, axis=0, keepdims=True), top_ref.shape)
    rms_ref[...] = rms


def head(last, gain, w_head):
    vm = pl.BlockSpec(memory_space=pltpu.VMEM)
    rows = last.shape[0]
    return pl.pallas_call(
        head_body,
        out_shape=(
            jax.ShapeDtypeStruct((256, rows), f32),
            jax.ShapeDtypeStruct((rows, 1), f32),
        ),
        in_specs=[vm, vm, vm],
        out_specs=(vm, vm),
        name="head",
    )(last, gain, w_head)


def local(
    hidden,
    attn_gain,
    w_qkv,
    w_out,
    kv_cache,
    holder_slot,
    lengths,
    ffn_gain,
    w_router,
    expert_ids,
    w_exp_in,
    w_exp_down,
    w_sh_in,
    w_sh_down,
    final_gain,
    w_head,
):
    zh = lax.axis_index("zh")
    zl = lax.axis_index("zl")
    core = lax.axis_index("core")
    expert = lax.axis_index(REQ)
    new, feat = hidden.shape
    width = attn_gain.shape[0]
    half = width // 2
    experts_all = w_router.shape[1]
    plane = experts_all // 2
    reqs = holder_slot.shape[0]
    span = new // reqs
    rows = 2 * (SHARE + span)
    slots = plane * rows
    slot_at = holder_slot.reshape(2, plane).T.reshape(reqs)
    order = (slot_at % plane) * 2 + slot_at // plane
    place = jnp.concatenate([jnp.stack([core, expert]).astype(jnp.int32), order])
    barrier = lax.optimization_barrier

    ids_t = expert_ids.T
    sizes = jnp.concatenate(
        [jnp.broadcast_to(lengths // 32, (feat // 2,)), jnp.broadcast_to(lengths % 32, (feat // 2,))]
    )
    meta = jnp.concatenate([ids_t.reshape(TOPK * new // feat, feat), sizes[None]]).astype(bf16)
    meta = jnp.broadcast_to(meta[None], (reqs,) + meta.shape)
    chunks = jnp.concatenate([hidden.reshape(reqs, span, feat), meta], axis=1)
    w_in = w_exp_in[0].swapaxes(1, 2)
    w_down = w_exp_down[0]
    neighbours = [(0, 1), (1, 0), (2, 3), (3, 2)]
    chunks, ids_out, gate_w = barrier((chunks, ids_t, w_in[0]))
    pair_gate = lax.ppermute(gate_w, "zl", neighbours)
    leg = lax.all_to_all(chunks, REQ, 0, 0, tiled=True)
    ids_there, up_w = barrier((column_swap(ids_out), w_in[1]))

    pair_up = lax.ppermute(up_w, "zl", neighbours)

    req_iota = jnp.arange(reqs, dtype=jnp.int32)
    owner_of = jnp.sum(
        jnp.where(holder_slot[None, :] == req_iota[:, None], req_iota[None, :], 0), axis=1
    )
    leg = leg.at[owner_of].get(mode="promise_in_bounds")
    leg = lax.all_to_all(leg, REQ, 0, 0, tiled=True)
    leg, pair_gate, gain, gain_ffn, gain_final, place = barrier(
        (leg, pair_gate, attn_gain[None], ffn_gain[None], final_gain[None], place)
    )
    held = leg[:, :span].reshape(new, feat)
    held_ids = leg[0, span:-1].reshape(TOPK, new).astype(jnp.int32)
    held_len = leg[0, -1, :1].astype(jnp.int32) * 32 + leg[0, -1, feat // 2 :][:1].astype(jnp.int32)

    full = lax.all_gather(held, TP, axis=1, tiled=True)
    parts_mine, parts_theirs = attend(
        held_len,
        place,
        full,
        gain,
        w_qkv,
        rope_tables(held_len, new),
        kv_cache,
        w_out,
    )
    parts_theirs, pair_up = barrier((parts_theirs, pair_up))
    parts = (parts_mine.astype(f32) + swap_core(parts_theirs).astype(f32)).astype(bf16)
    parts, held_ids = barrier((parts, held_ids))
    parts = lax.all_to_all(parts, "zl", 0, 0, tiled=True)
    held_share = (held.astype(f32) + jnp.sum(parts.astype(f32), axis=0)).astype(bf16)

    slot_iota = jnp.arange(slots, dtype=jnp.int32)

    def chosen_of(ids, other):
        both = jnp.where(zh == 0, jnp.stack([ids, other]), jnp.stack([other, ids]))
        picks = both.reshape(2, TOPK * new)
        onehot = (picks[:, :, None] == jnp.arange(experts_all, dtype=jnp.int32)).astype(bf16)
        order = jnp.arange(TOPK * new, dtype=jnp.int32)
        before = (order[:, None] > order[None, :]).astype(bf16)
        earlier = jnp.einsum("pq,rqe->rpe", before, onehot, preferred_element_type=f32)
        rank = jnp.sum(earlier * onehot.astype(f32), axis=2).astype(jnp.int32)
        rank = rank - (zl % 2) * SHARE
        there = picks - zh * plane
        which = jnp.arange(2, dtype=jnp.int32)[:, None]
        slot = there * rows + which * SHARE + rank
        here = (there >= 0) & (there < plane) & (rank >= 0) & (rank < SHARE)
        slot = jnp.where(here, slot, -1).reshape(2, TOPK, new)
        token = jnp.arange(new, dtype=jnp.int32)[None, :]
        chunk = token // span - zh * plane
        common = chunk * rows + 2 * SHARE + which * span + token % span
        common = jnp.where((chunk >= 0) & (chunk < plane), common, -1)
        chosen = (common.reshape(1, 2 * new) == slot_iota[:, None]).astype(bf16)
        for pick in range(TOPK):
            at = slot[:, pick].reshape(1, 2 * new)
            chosen = chosen + (at == slot_iota[:, None]).astype(bf16)
        return chosen

    chosen_held = chosen_of(held_ids, column_swap(held_ids))
    chosen_own = chosen_of(ids_t, ids_there).T

    outgoing = dispatch(chosen_held, spread(held_share, Z, 8))
    down_w, outgoing = barrier((w_down, outgoing))
    rows_mine = lax.all_to_all(
        outgoing.reshape(plane, rows, half), ("x", "y"), 0, 0, tiled=True
    )
    pair_down = lax.ppermute(down_w, "zl", neighbours)

    rows_mine, pair_down = barrier((rows_mine, pair_down))
    rows_theirs = swap_core(rows_mine)
    served_mine, served_theirs = experts(
        place,
        rows_mine,
        rows_theirs,
        gain_ffn,
        w_router.T,
        w_in,
        w_down,
        pair_gate,
        pair_up,
        pair_down,
        w_sh_in.swapaxes(1, 2),
        w_sh_down,
    )
    served = (served_mine.astype(f32) + swap_core(served_theirs).astype(f32)).astype(bf16)
    served, hidden_late = barrier((served, hidden))
    returned = lax.all_to_all(served, ("x", "y"), 0, 0, tiled=True).reshape(slots, half)

    own_full = lax.all_gather(hidden_late, TP, axis=1, tiled=True)
    returned, own_full = barrier((returned, own_full))
    new_cache = new_kv(own_full, gain, w_qkv, rope_tables(lengths[0], new))[:, None]

    packed = combine(chosen_own, returned)
    summed = lax.all_to_all(packed, Z, 0, 0, tiled=True)
    out_hidden, last = finish(summed, reqs)

    last_all = lax.all_to_all(last, ("core", "x", "y"), 0, 0, tiled=True)
    tops, rms = head(last_all, gain_final, w_head)
    last_rms = rms.reshape(reqs)
    top_logit = jnp.max(lax.all_to_all(tops, ALL, 0, 0, tiled=True), axis=0)
    return (out_hidden, new_cache, last_rms, top_logit)


def solution(mesh):
    fine = Mesh(mesh.devices.reshape(SIZES), ALL)
    return jax.shard_map(
        local,
        mesh=fine,
        in_specs=(
            P(REQ, TP),
            P(),
            P(None, None, TP),
            P(TP, None),
            P(None, REQ, None, TP),
            P(),
            P(REQ),
            P(),
            P(),
            P(REQ, None),
            P(REQ, None, None, TP),
            P(REQ, TP, None),
            P(None, None, TP),
            P(TP, None),
            P(),
            P(REQ + TP, None),
        ),
        out_specs=(P(REQ, TP), P(None, REQ, None, TP), P(), P()),
        check_vma=False,
    )
```

```python
import jax
import jax.numpy as jnp
from jax import lax
from jax.sharding import Mesh, PartitionSpec as P
from jax.experimental import pallas as pl
from jax.experimental.pallas import tpu as pltpu

HD = 128
TOPK = 6
CAP = 32
SHARE = CAP // 2

REQ = ("zh", "x", "y")
TP = ("zl", "core")
COL = ("zh", "zl", "core")
Z = ("zh", "zl")
ALL = ("zh", "x", "y", "zl", "core")
SIZES = (2, 4, 4, 4, 2)

epsilon = 1e-06
bf16 = jnp.bfloat16
f32 = jnp.float32


def rms_scale(values, gain):
    return (
        values
        * lax.rsqrt(jnp.mean(values * values, axis=-1, keepdims=True) + epsilon)
        * gain.astype(f32)
    )


def rope_tables(length, new):
    half_len = HD // 2
    freqs = 10000.0 ** (-2.0 * jnp.arange(half_len, dtype=f32) / HD)
    offsets = jnp.arange(new, dtype=jnp.int32).astype(f32)[:, None] * freqs[None, :]
    shift = length.astype(f32).reshape(1, 1) * freqs[None, :]
    return jnp.cos(offsets), jnp.sin(offsets), jnp.cos(shift), jnp.sin(shift)


def norm_rows(full_ref, gain_ref):
    return rms_scale(full_ref[...].astype(f32), gain_ref[...]).astype(bf16)


def rotate(values, cos_ref, sin_ref, cos_at_ref, sin_at_ref):
    cosine = cos_ref[...] * cos_at_ref[...] - sin_ref[...] * sin_at_ref[...]
    sine = sin_ref[...] * cos_at_ref[...] + cos_ref[...] * sin_at_ref[...]
    cosine = jnp.concatenate([cosine, cosine], axis=1)
    sine = jnp.concatenate([-sine, sine], axis=1)
    heads = []
    for head in range(values.shape[1] // HD):
        piece = values[:, head * HD : (head + 1) * HD]
        heads.append(piece * cosine + pltpu.roll(piece, HD // 2, 1) * sine)
    return jnp.concatenate(heads, axis=1).astype(bf16)


def new_kv_body(full_ref, gain_ref, w_ref, *refs):
    tables, o_ref = refs[:4], refs[4]
    normed = norm_rows(full_ref, gain_ref)
    keys = jnp.dot(normed, w_ref[1], preferred_element_type=f32)
    o_ref[0] = rotate(keys, *tables)
    o_ref[1] = jnp.dot(normed, w_ref[2], preferred_element_type=f32).astype(bf16)


def new_kv(full, gain, w_qkv, tables):
    vm = pl.BlockSpec(memory_space=pltpu.VMEM)
    return pl.pallas_call(
        new_kv_body,
        out_shape=jax.ShapeDtypeStruct((2, full.shape[0], w_qkv.shape[2]), bf16),
        in_specs=[vm] * 7,
        out_specs=vm,
        name="new_kv",
    )(full, gain, w_qkv, *tables)


def attend_body(
    len_ref, place_ref, full_ref, gain_ref, qkv_ref, cos_ref, sin_ref, cos_at_ref, sin_at_ref,
    kv_ref, w_ref, om_ref, ot_ref,
):
    tables = (cos_ref, sin_ref, cos_at_ref, sin_at_ref)
    length = len_ref[0]
    first = place_ref[0] == 0
    ctx = kv_ref.shape[2]
    new = full_ref.shape[0]
    normed = norm_rows(full_ref, gain_ref)
    q_all = rotate(jnp.dot(normed, qkv_ref[0], preferred_element_type=f32), *tables)
    k_all = rotate(jnp.dot(normed, qkv_ref[1], preferred_element_type=f32), *tables)
    v_all = jnp.dot(normed, qkv_ref[2], preferred_element_type=f32).astype(bf16)
    heads = []
    for head in range(q_all.shape[1] // HD):
        lanes = slice(head * HD, (head + 1) * HD)
        q = q_all[:, lanes]
        s_old = dot_nt(q, kv_ref[0, 0, :, lanes]) * HD ** (-0.5)
        s_new = dot_nt(q, k_all[:, lanes]) * HD ** (-0.5)
        seen_old = lax.broadcasted_iota(jnp.int32, (new, ctx), 1) < length
        seen_new = lax.broadcasted_iota(jnp.int32, (new, new), 1) <= lax.broadcasted_iota(
            jnp.int32, (new, new), 0
        )
        s_old = jnp.where(seen_old, s_old, -1e30)
        s_new = jnp.where(seen_new, s_new, -1e30)
        peak = jnp.maximum(
            jnp.max(s_old, axis=-1, keepdims=True), jnp.max(s_new, axis=-1, keepdims=True)
        )
        e_old = jnp.where(seen_old, jnp.exp(s_old - peak), 0.0)
        e_new = jnp.where(seen_new, jnp.exp(s_new - peak), 0.0)
        total = jnp.sum(e_old, axis=-1, keepdims=True) + jnp.sum(e_new, axis=-1, keepdims=True)
        w_old = (e_old / total).astype(bf16)
        w_new = (e_new / total).astype(bf16)
        out = jnp.dot(w_old, kv_ref[1, 0, :, lanes], preferred_element_type=f32) + jnp.dot(
            w_new, v_all[:, lanes], preferred_element_type=f32
        )
        heads.append(out.astype(bf16))
    attn = jnp.concatenate(heads, axis=1)
    wide = om_ref.shape[2]

    def store(even_ref, odd_ref):
        for part in range(2 * om_ref.shape[0]):
            ref = odd_ref if part % 2 else even_ref
            ref[part // 2] = jnp.dot(
                attn, w_ref[:, part * wide : (part + 1) * wide], preferred_element_type=f32
            ).astype(bf16)

    @pl.when(first)
    def _():
        store(om_ref, ot_ref)

    @pl.when(jnp.logical_not(first))
    def _():
        store(ot_ref, om_ref)


def attend(length, place, full, gain, w_qkv, tables, kv_cache, w_out):
    vm = pl.BlockSpec(memory_space=pltpu.VMEM)
    new = full.shape[0]
    feat = w_out.shape[0]
    shape = jax.ShapeDtypeStruct((w_out.shape[1] // feat // 2, new, feat), bf16)
    return pl.pallas_call(
        attend_body,
        out_shape=(shape, shape),
        in_specs=[pl.BlockSpec(memory_space=pltpu.SMEM)] * 2 + [vm] * 9,
        out_specs=(vm, vm),
        name="attend",
    )(length, place, full, gain, w_qkv, *tables, kv_cache, w_out)


def spread(value, axes, count):
    wide = jnp.broadcast_to(value[None], (count,) + value.shape)
    return lax.all_to_all(wide, axes, 0, 0, tiled=True)


def swap_core(value):
    return lax.ppermute(value, "core", [(0, 1), (1, 0)])


def column_swap(value):
    return lax.ppermute(value, "zh", [(0, 1), (1, 0)])


def dot_nt(a, b):
    return lax.dot_general(a, b, (((1,), (1,)), ((), ())), preferred_element_type=f32)


def expert_rows(rows, gate_w, up_w, down_w):
    gate = dot_nt(rows, gate_w)
    up = dot_nt(rows, up_w)
    inner = (gate / (1.0 + jnp.exp(-gate)) * up).astype(bf16)
    return jnp.dot(inner, down_w, preferred_element_type=f32)


def drain(first, out, mine_ref, theirs_ref):
    feat = out.shape[1] // 8

    def store(even_ref, odd_ref):
        for part in range(4):
            piece = slice(part * feat, (part + 1) * feat)
            even_ref[:, piece] = out[:, 2 * part * feat : (2 * part + 1) * feat]
            odd_ref[:, piece] = out[:, (2 * part + 1) * feat : (2 * part + 2) * feat]

    @pl.when(first)
    def _():
        store(mine_ref, theirs_ref)

    @pl.when(jnp.logical_not(first))
    def _():
        store(theirs_ref, mine_ref)


def experts_body(
    place_ref, a_ref, b_ref, gain_ref, router_ref, in_ref, down_ref, pg_ref, pu_ref, pd_ref,
    si_ref, sd_ref, om_ref, ot_ref, xr_ref, xs_ref, ys_ref,
):
    first = place_ref[0] == 0
    feat = xr_ref.shape[1] // 8
    chunks, span = a_ref.shape[:2]
    routed = xr_ref.shape[0] // chunks
    shared = span - routed

    def fill(even_ref, odd_ref):
        for chunk in range(chunks):
            for part in range(4):
                piece = slice(part * feat, (part + 1) * feat)
                for odd, ref in enumerate((even_ref, odd_ref)):
                    lanes = slice((2 * part + odd) * feat, (2 * part + odd + 1) * feat)
                    rows = ref[chunk, :, piece].astype(f32)
                    xr_ref[chunk * routed : (chunk + 1) * routed, lanes] = rows[:routed]
                    xs_ref[chunk * shared : (chunk + 1) * shared, lanes] = rows[routed:]

    @pl.when(first)
    def _():
        fill(a_ref, b_ref)

    @pl.when(jnp.logical_not(first))
    def _():
        fill(b_ref, a_ref)

    common = norm_rows(xs_ref, gain_ref)
    common = expert_rows(common, si_ref[0], si_ref[1], sd_ref[...])
    common = common + xs_ref[...] * 0.125
    half = shared // 2
    for piece in range(2 * chunks):
        ys_ref[piece, :half, :] = common[piece * half : (piece + 1) * half]

    rows = norm_rows(xr_ref, gain_ref)
    out = expert_rows(rows, in_ref[0], in_ref[1], down_ref[...])
    out = out + expert_rows(rows, pg_ref[...], pu_ref[...], pd_ref[...])
    logits = dot_nt(rows, router_ref[...])
    raised = jnp.exp(logits - jnp.max(logits, axis=-1, keepdims=True))
    own = lax.broadcasted_iota(jnp.int32, logits.shape, 1) == place_ref[1]
    picked = jnp.sum(jnp.where(own, raised, 0.0), axis=-1, keepdims=True)
    xr_ref[...] = out * (picked / jnp.sum(raised, axis=-1, keepdims=True))

    def store(even_ref, odd_ref):
        for chunk in range(chunks):
            origin = [place_ref[2 + 2 * chunk + zo] for zo in range(2)]
            size = routed // 2
            top = [xr_ref[pl.ds(pl.multiple_of(at * size, size), size), :] for at in origin]
            low = [ys_ref[at, :half, :] for at in origin]
            both = jnp.concatenate(top + low, axis=0).astype(bf16)
            for part in range(4):
                piece = slice(part * feat, (part + 1) * feat)
                even_ref[chunk, :, piece] = both[:, 2 * part * feat : (2 * part + 1) * feat]
                odd_ref[chunk, :, piece] = both[:, (2 * part + 1) * feat : (2 * part + 2) * feat]

    @pl.when(first)
    def _():
        store(om_ref, ot_ref)

    @pl.when(jnp.logical_not(first))
    def _():
        store(ot_ref, om_ref)


def experts(place, rows_mine, rows_theirs, *weights):
    vm = pl.BlockSpec(memory_space=pltpu.VMEM)
    count, span, half = rows_mine.shape
    width = 2 * half
    shape = jax.ShapeDtypeStruct(rows_mine.shape, bf16)
    shared = span - 2 * SHARE
    return pl.pallas_call(
        experts_body,
        out_shape=(shape, shape),
        in_specs=[pl.BlockSpec(memory_space=pltpu.SMEM)] + [vm] * (2 + len(weights)),
        out_specs=(vm, vm),
        scratch_shapes=[
            pltpu.VMEM((count * 2 * SHARE, width), f32),
            pltpu.VMEM((count * shared, width), f32),
            pltpu.VMEM((2 * count, 8, width), f32),
        ],
        cost_estimate=pl.CostEstimate(
            flops=6 * count * span * width * 352,
            transcendentals=count * span * 352,
            bytes_accessed=8 * count * span * half + 18 * width * 176,
        ),
        name="experts",
    )(place, rows_mine, rows_theirs, *weights)


def dispatch_body(chosen_ref, parts_ref, out_ref):
    both = jnp.concatenate([parts_ref[0, 0], parts_ref[1, 0]], axis=0)
    out_ref[...] = jnp.dot(chosen_ref[...], both, preferred_element_type=f32).astype(bf16)


def dispatch(chosen_t, parts):
    new, feat = parts.shape[1:]
    slots, tokens = chosen_t.shape
    return pl.pallas_call(
        dispatch_body,
        grid=(4,),
        out_shape=jax.ShapeDtypeStruct((slots, 4 * feat), bf16),
        in_specs=[
            pl.BlockSpec((slots, tokens), lambda i: (0, 0)),
            pl.BlockSpec((2, 1, new, feat), lambda i: (0, i, 0, 0)),
        ],
        out_specs=pl.BlockSpec((slots, feat), lambda i: (0, i)),
        name="dispatch",
    )(chosen_t, parts.reshape(2, 4, new, feat))


def combine_body(chosen_ref, back_ref, out_ref):
    feat = out_ref.shape[2]
    new = chosen_ref.shape[0] // 2
    last = []
    for zo in range(2):
        total = jnp.dot(
            chosen_ref[zo * new : (zo + 1) * new, :], back_ref[...], preferred_element_type=f32
        )
        for part in range(4):
            piece = total[:, part * feat : (part + 1) * feat]
            out_ref[zo * 4 + part, :new, :] = piece.astype(bf16)
            last.append(piece[new - 1 :, :])
    last = jnp.concatenate(last, axis=0).astype(bf16)
    for dest in range(8):
        out_ref[dest, new:, :] = last


def combine(chosen, back):
    vm = pl.BlockSpec(memory_space=pltpu.VMEM)
    return pl.pallas_call(
        combine_body,
        out_shape=jax.ShapeDtypeStruct((8, chosen.shape[0] // 2 + 8, back.shape[1] // 4), bf16),
        in_specs=[vm, vm],
        out_specs=vm,
        name="combine",
    )(chosen, back)


def finish_body(parts_ref, out_ref, last_ref):
    new, feat = out_ref.shape
    total = parts_ref[0].astype(f32)
    for part in range(1, 8):
        total = total + parts_ref[part].astype(f32)
    out_ref[...] = total[:new].astype(bf16)
    last = total[new:].astype(bf16).astype(f32)
    last = jnp.concatenate([last[:, : feat // 2], last[:, feat // 2 :]], axis=0).astype(bf16)
    last_ref[...] = jnp.broadcast_to(last[None], last_ref.shape)


def finish(parts, copies):
    vm = pl.BlockSpec(memory_space=pltpu.VMEM)
    return pl.pallas_call(
        finish_body,
        out_shape=(
            jax.ShapeDtypeStruct((parts.shape[1] - 8, parts.shape[2]), bf16),
            jax.ShapeDtypeStruct((copies, 16, 128), bf16),
        ),
        in_specs=[vm],
        out_specs=(vm, vm),
        name="finish",
    )(parts)


def head_body(last_ref, gain_ref, w_ref, top_ref, rms_ref):
    plane = last_ref.shape[0] // 2
    rows = jnp.swapaxes(last_ref[...].astype(f32), 0, 1)
    halves = []
    for zo in range(2):
        pieces = []
        for part in range(4):
            for core in range(2):
                for sub in range(2):
                    pieces.append(
                        rows[sub * 8 + zo * 4 + part, core * plane : (core + 1) * plane]
                    )
        halves.append(jnp.concatenate(pieces, axis=1))
    tok = jnp.concatenate(halves, axis=0)
    rms = jnp.sqrt(jnp.mean(tok * tok, axis=-1, keepdims=True) + epsilon)
    head_in = (tok / rms * gain_ref[...].astype(f32)).astype(bf16)
    logits = lax.dot_general(
        w_ref[...], head_in, (((1,), (1,)), ((), ())), preferred_element_type=f32
    )
    top_ref[...] = jnp.broadcast_to(jnp.max(logits, axis=0, keepdims=True), top_ref.shape)
    rms_ref[...] = rms


def head(last, gain, w_head):
    vm = pl.BlockSpec(memory_space=pltpu.VMEM)
    rows = last.shape[0]
    return pl.pallas_call(
        head_body,
        out_shape=(
            jax.ShapeDtypeStruct((256, rows), f32),
            jax.ShapeDtypeStruct((rows, 1), f32),
        ),
        in_specs=[vm, vm, vm],
        out_specs=(vm, vm),
        name="head",
    )(last, gain, w_head)


def local(
    hidden,
    attn_gain,
    w_qkv,
    w_out,
    kv_cache,
    holder_slot,
    lengths,
    ffn_gain,
    w_router,
    expert_ids,
    w_exp_in,
    w_exp_down,
    w_sh_in,
    w_sh_down,
    final_gain,
    w_head,
):
    zh = lax.axis_index("zh")
    zl = lax.axis_index("zl")
    core = lax.axis_index("core")
    expert = lax.axis_index(REQ)
    new, feat = hidden.shape
    width = attn_gain.shape[0]
    half = width // 2
    experts_all = w_router.shape[1]
    plane = experts_all // 2
    reqs = holder_slot.shape[0]
    span = new // reqs
    rows = 2 * (SHARE + span)
    slots = plane * rows
    slot_at = holder_slot.reshape(2, plane).T.reshape(reqs)
    order = (slot_at % plane) * 2 + slot_at // plane
    place = jnp.concatenate([jnp.stack([core, expert]).astype(jnp.int32), order])
    barrier = lax.optimization_barrier

    ids_t = expert_ids.T
    sizes = jnp.concatenate(
        [jnp.broadcast_to(lengths // 32, (feat // 2,)), jnp.broadcast_to(lengths % 32, (feat // 2,))]
    )
    meta = jnp.concatenate([ids_t.reshape(TOPK * new // feat, feat), sizes[None]]).astype(bf16)
    meta = jnp.broadcast_to(meta[None], (reqs,) + meta.shape)
    chunks = jnp.concatenate([hidden.reshape(reqs, span, feat), meta], axis=1)
    w_in = w_exp_in[0].swapaxes(1, 2)
    w_down = w_exp_down[0]
    neighbours = [(0, 1), (1, 0), (2, 3), (3, 2)]
    pair_gate = lax.ppermute(w_in[0], "zl", neighbours)
    leg = lax.all_to_all(chunks, REQ, 0, 0, tiled=True)
    ids_there = column_swap(ids_t)


    req_iota = jnp.arange(reqs, dtype=jnp.int32)
    owner_of = jnp.sum(
        jnp.where(holder_slot[None, :] == req_iota[:, None], req_iota[None, :], 0), axis=1
    )
    leg = leg.at[owner_of].get(mode="promise_in_bounds")
    leg, up_w = barrier((leg, w_in[1]))
    pair_up = lax.ppermute(up_w, "zl", neighbours)
    leg = lax.all_to_all(leg, REQ, 0, 0, tiled=True)
    leg, pair_gate, gain, gain_ffn, gain_final, place = barrier(
        (leg, pair_gate, attn_gain[None], ffn_gain[None], final_gain[None], place)
    )
    held = leg[:, :span].reshape(new, feat)
    held_ids = leg[0, span:-1].reshape(TOPK, new).astype(jnp.int32)
    held_len = leg[0, -1, :1].astype(jnp.int32) * 32 + leg[0, -1, feat // 2 :][:1].astype(jnp.int32)

    full = lax.all_gather(held, TP, axis=1, tiled=True)
    parts_mine, parts_theirs = attend(
        held_len,
        place,
        full,
        gain,
        w_qkv,
        rope_tables(held_len, new),
        kv_cache,
        w_out,
    )
    parts_theirs, pair_up = barrier((parts_theirs, pair_up))
    parts = (parts_mine.astype(f32) + swap_core(parts_theirs).astype(f32)).astype(bf16)
    parts, held_ids = barrier((parts, held_ids))
    parts = lax.all_to_all(parts, "zl", 0, 0, tiled=True)
    held_share = (held.astype(f32) + jnp.sum(parts.astype(f32), axis=0)).astype(bf16)

    slot_iota = jnp.arange(slots, dtype=jnp.int32)

    def chosen_of(ids, other):
        both = jnp.where(zh == 0, jnp.stack([ids, other]), jnp.stack([other, ids]))
        picks = both.reshape(2, TOPK * new)
        onehot = (picks[:, :, None] == jnp.arange(experts_all, dtype=jnp.int32)).astype(bf16)
        order = jnp.arange(TOPK * new, dtype=jnp.int32)
        before = (order[:, None] > order[None, :]).astype(bf16)
        earlier = jnp.einsum("pq,rqe->rpe", before, onehot, preferred_element_type=f32)
        rank = jnp.sum(earlier * onehot.astype(f32), axis=2).astype(jnp.int32)
        rank = rank - (zl % 2) * SHARE
        there = picks - zh * plane
        which = jnp.arange(2, dtype=jnp.int32)[:, None]
        slot = there * rows + which * SHARE + rank
        here = (there >= 0) & (there < plane) & (rank >= 0) & (rank < SHARE)
        slot = jnp.where(here, slot, -1).reshape(2, TOPK, new)
        token = jnp.arange(new, dtype=jnp.int32)[None, :]
        chunk = token // span - zh * plane
        common = chunk * rows + 2 * SHARE + which * span + token % span
        common = jnp.where((chunk >= 0) & (chunk < plane), common, -1)
        chosen = (common.reshape(1, 2 * new) == slot_iota[:, None]).astype(bf16)
        for pick in range(TOPK):
            at = slot[:, pick].reshape(1, 2 * new)
            chosen = chosen + (at == slot_iota[:, None]).astype(bf16)
        return chosen

    chosen_held = chosen_of(held_ids, column_swap(held_ids))
    chosen_own = chosen_of(ids_t, ids_there).T

    outgoing = dispatch(chosen_held, spread(held_share, Z, 8))
    down_w, outgoing = barrier((w_down, outgoing))
    rows_mine = lax.all_to_all(
        outgoing.reshape(plane, rows, half), ("x", "y"), 0, 0, tiled=True
    )
    pair_down = lax.ppermute(down_w, "zl", neighbours)

    rows_mine, pair_down = barrier((rows_mine, pair_down))
    rows_theirs = swap_core(rows_mine)
    served_mine, served_theirs = experts(
        place,
        rows_mine,
        rows_theirs,
        gain_ffn,
        w_router.T,
        w_in,
        w_down,
        pair_gate,
        pair_up,
        pair_down,
        w_sh_in.swapaxes(1, 2),
        w_sh_down,
    )
    served = (served_mine.astype(f32) + swap_core(served_theirs).astype(f32)).astype(bf16)
    served, hidden_late = barrier((served, hidden))
    returned = lax.all_to_all(served, ("x", "y"), 0, 0, tiled=True).reshape(slots, half)

    own_full = lax.all_gather(hidden_late, TP, axis=1, tiled=True)
    returned, own_full = barrier((returned, own_full))
    new_cache = new_kv(own_full, gain, w_qkv, rope_tables(lengths[0], new))[:, None]

    packed = combine(chosen_own, returned)
    summed = lax.all_to_all(packed, Z, 0, 0, tiled=True)
    out_hidden, last = finish(summed, reqs)

    last_all = lax.all_to_all(last, ("core", "x", "y"), 0, 0, tiled=True)
    tops, rms = head(last_all, gain_final, w_head)
    last_rms = rms.reshape(reqs)
    top_logit = jnp.max(lax.all_to_all(tops, ALL, 0, 0, tiled=True), axis=0)
    return (out_hidden, new_cache, last_rms, top_logit)


def solution(mesh):
    fine = Mesh(mesh.devices.reshape(SIZES), ALL)
    return jax.shard_map(
        local,
        mesh=fine,
        in_specs=(
            P(REQ, TP),
            P(),
            P(None, None, TP),
            P(TP, None),
            P(None, REQ, None, TP),
            P(),
            P(REQ),
            P(),
            P(),
            P(REQ, None),
            P(REQ, None, None, TP),
            P(REQ, TP, None),
            P(None, None, TP),
            P(TP, None),
            P(),
            P(REQ + TP, None),
        ),
        out_specs=(P(REQ, TP), P(None, REQ, None, TP), P(), P()),
        check_vma=False,
    )
```

```python
import jax
import jax.numpy as jnp
from jax import lax
from jax.sharding import Mesh, PartitionSpec as P
from jax.experimental import pallas as pl
from jax.experimental.pallas import tpu as pltpu

HD = 128
TOPK = 6
CAP = 32
SHARE = CAP // 2

REQ = ("zh", "x", "y")
TP = ("zl", "core")
COL = ("zh", "zl", "core")
Z = ("zh", "zl")
ALL = ("zh", "x", "y", "zl", "core")
SIZES = (2, 4, 4, 4, 2)

epsilon = 1e-06
bf16 = jnp.bfloat16
f32 = jnp.float32


def rms_scale(values, gain):
    return (
        values
        * lax.rsqrt(jnp.mean(values * values, axis=-1, keepdims=True) + epsilon)
        * gain.astype(f32)
    )


def rope_tables(length, new):
    half_len = HD // 2
    freqs = 10000.0 ** (-2.0 * jnp.arange(half_len, dtype=f32) / HD)
    offsets = jnp.arange(new, dtype=jnp.int32).astype(f32)[:, None] * freqs[None, :]
    shift = length.astype(f32).reshape(1, 1) * freqs[None, :]
    return jnp.cos(offsets), jnp.sin(offsets), jnp.cos(shift), jnp.sin(shift)


def norm_rows(full_ref, gain_ref):
    return rms_scale(full_ref[...].astype(f32), gain_ref[...]).astype(bf16)


def rotate(values, cos_ref, sin_ref, cos_at_ref, sin_at_ref):
    cosine = cos_ref[...] * cos_at_ref[...] - sin_ref[...] * sin_at_ref[...]
    sine = sin_ref[...] * cos_at_ref[...] + cos_ref[...] * sin_at_ref[...]
    cosine = jnp.concatenate([cosine, cosine], axis=1)
    sine = jnp.concatenate([-sine, sine], axis=1)
    heads = []
    for head in range(values.shape[1] // HD):
        piece = values[:, head * HD : (head + 1) * HD]
        heads.append(piece * cosine + pltpu.roll(piece, HD // 2, 1) * sine)
    return jnp.concatenate(heads, axis=1).astype(bf16)


def new_kv_body(full_ref, gain_ref, w_ref, *refs):
    tables, o_ref = refs[:4], refs[4]
    normed = norm_rows(full_ref, gain_ref)
    keys = jnp.dot(normed, w_ref[1], preferred_element_type=f32)
    o_ref[0] = rotate(keys, *tables)
    o_ref[1] = jnp.dot(normed, w_ref[2], preferred_element_type=f32).astype(bf16)


def new_kv(full, gain, w_qkv, tables):
    vm = pl.BlockSpec(memory_space=pltpu.VMEM)
    return pl.pallas_call(
        new_kv_body,
        out_shape=jax.ShapeDtypeStruct((2, full.shape[0], w_qkv.shape[2]), bf16),
        in_specs=[vm] * 7,
        out_specs=vm,
        name="new_kv",
    )(full, gain, w_qkv, *tables)


def attend_body(
    len_ref, place_ref, full_ref, gain_ref, qkv_ref, cos_ref, sin_ref, cos_at_ref, sin_at_ref,
    kv_ref, w_ref, om_ref, ot_ref,
):
    tables = (cos_ref, sin_ref, cos_at_ref, sin_at_ref)
    length = len_ref[0]
    first = place_ref[0] == 0
    ctx = kv_ref.shape[2]
    new = full_ref.shape[0]
    normed = norm_rows(full_ref, gain_ref)
    q_all = rotate(jnp.dot(normed, qkv_ref[0], preferred_element_type=f32), *tables)
    k_all = rotate(jnp.dot(normed, qkv_ref[1], preferred_element_type=f32), *tables)
    v_all = jnp.dot(normed, qkv_ref[2], preferred_element_type=f32).astype(bf16)
    heads = []
    for head in range(q_all.shape[1] // HD):
        lanes = slice(head * HD, (head + 1) * HD)
        q = q_all[:, lanes]
        s_old = dot_nt(q, kv_ref[0, 0, :, lanes]) * HD ** (-0.5)
        s_new = dot_nt(q, k_all[:, lanes]) * HD ** (-0.5)
        seen_old = lax.broadcasted_iota(jnp.int32, (new, ctx), 1) < length
        seen_new = lax.broadcasted_iota(jnp.int32, (new, new), 1) <= lax.broadcasted_iota(
            jnp.int32, (new, new), 0
        )
        s_old = jnp.where(seen_old, s_old, -1e30)
        s_new = jnp.where(seen_new, s_new, -1e30)
        peak = jnp.maximum(
            jnp.max(s_old, axis=-1, keepdims=True), jnp.max(s_new, axis=-1, keepdims=True)
        )
        e_old = jnp.where(seen_old, jnp.exp(s_old - peak), 0.0)
        e_new = jnp.where(seen_new, jnp.exp(s_new - peak), 0.0)
        total = jnp.sum(e_old, axis=-1, keepdims=True) + jnp.sum(e_new, axis=-1, keepdims=True)
        w_old = (e_old / total).astype(bf16)
        w_new = (e_new / total).astype(bf16)
        out = jnp.dot(w_old, kv_ref[1, 0, :, lanes], preferred_element_type=f32) + jnp.dot(
            w_new, v_all[:, lanes], preferred_element_type=f32
        )
        heads.append(out.astype(bf16))
    attn = jnp.concatenate(heads, axis=1)
    wide = om_ref.shape[2]

    def store(even_ref, odd_ref):
        for part in range(2 * om_ref.shape[0]):
            ref = odd_ref if part % 2 else even_ref
            ref[part // 2] = jnp.dot(
                attn, w_ref[:, part * wide : (part + 1) * wide], preferred_element_type=f32
            ).astype(bf16)

    @pl.when(first)
    def _():
        store(om_ref, ot_ref)

    @pl.when(jnp.logical_not(first))
    def _():
        store(ot_ref, om_ref)


def attend(length, place, full, gain, w_qkv, tables, kv_cache, w_out):
    vm = pl.BlockSpec(memory_space=pltpu.VMEM)
    new = full.shape[0]
    feat = w_out.shape[0]
    shape = jax.ShapeDtypeStruct((w_out.shape[1] // feat // 2, new, feat), bf16)
    return pl.pallas_call(
        attend_body,
        out_shape=(shape, shape),
        in_specs=[pl.BlockSpec(memory_space=pltpu.SMEM)] * 2 + [vm] * 9,
        out_specs=(vm, vm),
        name="attend",
    )(length, place, full, gain, w_qkv, *tables, kv_cache, w_out)


def spread(value, axes, count):
    wide = jnp.broadcast_to(value[None], (count,) + value.shape)
    return lax.all_to_all(wide, axes, 0, 0, tiled=True)


def swap_core(value):
    return lax.ppermute(value, "core", [(0, 1), (1, 0)])


def column_swap(value):
    return lax.ppermute(value, "zh", [(0, 1), (1, 0)])


def dot_nt(a, b):
    return lax.dot_general(a, b, (((1,), (1,)), ((), ())), preferred_element_type=f32)


def expert_rows(rows, gate_w, up_w, down_w):
    gate = dot_nt(rows, gate_w)
    up = dot_nt(rows, up_w)
    inner = (gate / (1.0 + jnp.exp(-gate)) * up).astype(bf16)
    return jnp.dot(inner, down_w, preferred_element_type=f32)


def drain(first, out, mine_ref, theirs_ref):
    feat = out.shape[1] // 8

    def store(even_ref, odd_ref):
        for part in range(4):
            piece = slice(part * feat, (part + 1) * feat)
            even_ref[:, piece] = out[:, 2 * part * feat : (2 * part + 1) * feat]
            odd_ref[:, piece] = out[:, (2 * part + 1) * feat : (2 * part + 2) * feat]

    @pl.when(first)
    def _():
        store(mine_ref, theirs_ref)

    @pl.when(jnp.logical_not(first))
    def _():
        store(theirs_ref, mine_ref)


def experts_body(
    place_ref, a_ref, b_ref, gain_ref, router_ref, in_ref, down_ref, pg_ref, pu_ref, pd_ref,
    si_ref, sd_ref, om_ref, ot_ref, xr_ref, xs_ref, ys_ref,
):
    first = place_ref[0] == 0
    feat = xr_ref.shape[1] // 8
    chunks, span = a_ref.shape[:2]
    routed = xr_ref.shape[0] // chunks
    shared = span - routed

    def fill(even_ref, odd_ref):
        for chunk in range(chunks):
            for part in range(4):
                piece = slice(part * feat, (part + 1) * feat)
                for odd, ref in enumerate((even_ref, odd_ref)):
                    lanes = slice((2 * part + odd) * feat, (2 * part + odd + 1) * feat)
                    rows = ref[chunk, :, piece].astype(f32)
                    xr_ref[chunk * routed : (chunk + 1) * routed, lanes] = rows[:routed]
                    xs_ref[chunk * shared : (chunk + 1) * shared, lanes] = rows[routed:]

    @pl.when(first)
    def _():
        fill(a_ref, b_ref)

    @pl.when(jnp.logical_not(first))
    def _():
        fill(b_ref, a_ref)

    common = norm_rows(xs_ref, gain_ref)
    common = expert_rows(common, si_ref[0], si_ref[1], sd_ref[...])
    common = common + xs_ref[...] * 0.125
    half = shared // 2
    for piece in range(2 * chunks):
        ys_ref[piece, :half, :] = common[piece * half : (piece + 1) * half]

    rows = norm_rows(xr_ref, gain_ref)
    out = expert_rows(rows, in_ref[0], in_ref[1], down_ref[...])
    out = out + expert_rows(rows, pg_ref[...], pu_ref[...], pd_ref[...])
    logits = dot_nt(rows, router_ref[...])
    raised = jnp.exp(logits - jnp.max(logits, axis=-1, keepdims=True))
    own = lax.broadcasted_iota(jnp.int32, logits.shape, 1) == place_ref[1]
    picked = jnp.sum(jnp.where(own, raised, 0.0), axis=-1, keepdims=True)
    xr_ref[...] = out * (picked / jnp.sum(raised, axis=-1, keepdims=True))

    def store(even_ref, odd_ref):
        for chunk in range(chunks):
            origin = [place_ref[2 + 2 * chunk + zo] for zo in range(2)]
            size = routed // 2
            top = [xr_ref[pl.ds(pl.multiple_of(at * size, size), size), :] for at in origin]
            low = [ys_ref[at, :half, :] for at in origin]
            both = jnp.concatenate(top + low, axis=0).astype(bf16)
            for part in range(4):
                piece = slice(part * feat, (part + 1) * feat)
                even_ref[chunk, :, piece] = both[:, 2 * part * feat : (2 * part + 1) * feat]
                odd_ref[chunk, :, piece] = both[:, (2 * part + 1) * feat : (2 * part + 2) * feat]

    @pl.when(first)
    def _():
        store(om_ref, ot_ref)

    @pl.when(jnp.logical_not(first))
    def _():
        store(ot_ref, om_ref)


def experts(place, rows_mine, rows_theirs, *weights):
    vm = pl.BlockSpec(memory_space=pltpu.VMEM)
    count, span, half = rows_mine.shape
    width = 2 * half
    shape = jax.ShapeDtypeStruct(rows_mine.shape, bf16)
    shared = span - 2 * SHARE
    return pl.pallas_call(
        experts_body,
        out_shape=(shape, shape),
        in_specs=[pl.BlockSpec(memory_space=pltpu.SMEM)] + [vm] * (2 + len(weights)),
        out_specs=(vm, vm),
        scratch_shapes=[
            pltpu.VMEM((count * 2 * SHARE, width), f32),
            pltpu.VMEM((count * shared, width), f32),
            pltpu.VMEM((2 * count, 8, width), f32),
        ],
        cost_estimate=pl.CostEstimate(
            flops=6 * count * span * width * 352,
            transcendentals=count * span * 352,
            bytes_accessed=8 * count * span * half + 18 * width * 176,
        ),
        name="experts",
    )(place, rows_mine, rows_theirs, *weights)


def dispatch_body(chosen_ref, parts_ref, out_ref):
    feat = parts_ref.shape[2]
    for part in range(4):
        both = jnp.concatenate([parts_ref[part], parts_ref[4 + part]], axis=0)
        out_ref[:, part * feat : (part + 1) * feat] = jnp.dot(
            chosen_ref[...], both, preferred_element_type=f32
        ).astype(bf16)


def dispatch(chosen_t, parts):
    vm = pl.BlockSpec(memory_space=pltpu.VMEM)
    return pl.pallas_call(
        dispatch_body,
        out_shape=jax.ShapeDtypeStruct((chosen_t.shape[0], 4 * parts.shape[2]), bf16),
        in_specs=[vm, vm],
        out_specs=vm,
        name="dispatch",
    )(chosen_t, parts)


def combine_body(chosen_ref, back_ref, out_ref, last_ref):
    feat = out_ref.shape[2]
    new = chosen_ref.shape[0] // 2
    last = []
    for zo in range(2):
        total = jnp.dot(
            chosen_ref[zo * new : (zo + 1) * new, :], back_ref[...], preferred_element_type=f32
        )
        for part in range(4):
            piece = total[:, part * feat : (part + 1) * feat]
            out_ref[zo * 4 + part] = piece.astype(bf16)
            last.append(piece[new - 1 :, :])
    last = jnp.concatenate(last, axis=0).astype(bf16)
    for dest in range(8):
        last_ref[dest] = last


def combine(chosen, back):
    vm = pl.BlockSpec(memory_space=pltpu.VMEM)
    feat = back.shape[1] // 4
    return pl.pallas_call(
        combine_body,
        out_shape=(
            jax.ShapeDtypeStruct((8, chosen.shape[0] // 2, feat), bf16),
            jax.ShapeDtypeStruct((8, 8, feat), bf16),
        ),
        in_specs=[vm, vm],
        out_specs=(vm, vm),
        name="combine",
    )(chosen, back)


def finish_body(parts_ref, last_ref):
    feat = parts_ref.shape[2]
    total = jnp.sum(parts_ref[...].astype(f32), axis=0)
    last = total.astype(bf16).astype(f32)
    last = jnp.concatenate([last[:, : feat // 2], last[:, feat // 2 :]], axis=0).astype(bf16)
    last_ref[...] = jnp.broadcast_to(last[None], last_ref.shape)


def finish(parts, copies):
    vm = pl.BlockSpec(memory_space=pltpu.VMEM)
    return pl.pallas_call(
        finish_body,
        out_shape=jax.ShapeDtypeStruct((copies, 16, 128), bf16),
        in_specs=[vm],
        out_specs=vm,
        name="finish",
    )(parts)


def head_body(last_ref, gain_ref, w_ref, top_ref, rms_ref):
    plane = last_ref.shape[0] // 2
    rows = jnp.swapaxes(last_ref[...].astype(f32), 0, 1)
    halves = []
    for zo in range(2):
        pieces = []
        for part in range(4):
            for core in range(2):
                for sub in range(2):
                    pieces.append(
                        rows[sub * 8 + zo * 4 + part, core * plane : (core + 1) * plane]
                    )
        halves.append(jnp.concatenate(pieces, axis=1))
    tok = jnp.concatenate(halves, axis=0)
    rms = jnp.sqrt(jnp.mean(tok * tok, axis=-1, keepdims=True) + epsilon)
    head_in = (tok / rms * gain_ref[...].astype(f32)).astype(bf16)
    logits = lax.dot_general(
        w_ref[...], head_in, (((1,), (1,)), ((), ())), preferred_element_type=f32
    )
    top_ref[...] = jnp.broadcast_to(jnp.max(logits, axis=0, keepdims=True), top_ref.shape)
    rms_ref[...] = rms


def head(last, gain, w_head):
    vm = pl.BlockSpec(memory_space=pltpu.VMEM)
    rows = last.shape[0]
    return pl.pallas_call(
        head_body,
        out_shape=(
            jax.ShapeDtypeStruct((256, rows), f32),
            jax.ShapeDtypeStruct((rows, 1), f32),
        ),
        in_specs=[vm, vm, vm],
        out_specs=(vm, vm),
        name="head",
    )(last, gain, w_head)


def local(
    hidden,
    attn_gain,
    w_qkv,
    w_out,
    kv_cache,
    holder_slot,
    lengths,
    ffn_gain,
    w_router,
    expert_ids,
    w_exp_in,
    w_exp_down,
    w_sh_in,
    w_sh_down,
    final_gain,
    w_head,
):
    zh = lax.axis_index("zh")
    zl = lax.axis_index("zl")
    core = lax.axis_index("core")
    expert = lax.axis_index(REQ)
    new, feat = hidden.shape
    width = attn_gain.shape[0]
    half = width // 2
    experts_all = w_router.shape[1]
    plane = experts_all // 2
    reqs = holder_slot.shape[0]
    span = new // reqs
    rows = 2 * (SHARE + span)
    slots = plane * rows
    slot_at = holder_slot.reshape(2, plane).T.reshape(reqs)
    order = (slot_at % plane) * 2 + slot_at // plane
    place = jnp.concatenate([jnp.stack([core, expert]).astype(jnp.int32), order])
    barrier = lax.optimization_barrier

    ids_t = expert_ids.T
    sizes = jnp.concatenate(
        [jnp.broadcast_to(lengths // 32, (feat // 2,)), jnp.broadcast_to(lengths % 32, (feat // 2,))]
    )
    meta = jnp.concatenate([ids_t.reshape(TOPK * new // feat, feat), sizes[None]]).astype(bf16)
    meta = jnp.broadcast_to(meta[None], (reqs,) + meta.shape)
    chunks = jnp.concatenate([hidden.reshape(reqs, span, feat), meta], axis=1)
    w_in = w_exp_in[0].swapaxes(1, 2)
    w_down = w_exp_down[0]
    neighbours = [(0, 1), (1, 0), (2, 3), (3, 2)]
    pair_gate = lax.ppermute(w_in[0], "zl", neighbours)
    leg = lax.all_to_all(chunks, REQ, 0, 0, tiled=True)
    ids_there = column_swap(ids_t)


    req_iota = jnp.arange(reqs, dtype=jnp.int32)
    owner_of = jnp.sum(
        jnp.where(holder_slot[None, :] == req_iota[:, None], req_iota[None, :], 0), axis=1
    )
    leg = leg.at[owner_of].get(mode="promise_in_bounds")
    leg, up_w = barrier((leg, w_in[1]))
    pair_up = lax.ppermute(up_w, "zl", neighbours)
    leg = lax.all_to_all(leg, REQ, 0, 0, tiled=True)
    leg, pair_gate, gain, gain_ffn, gain_final, place = barrier(
        (leg, pair_gate, attn_gain[None], ffn_gain[None], final_gain[None], place)
    )
    held = leg[:, :span].reshape(new, feat)
    held_ids = leg[0, span:-1].reshape(TOPK, new).astype(jnp.int32)
    held_len = leg[0, -1, :1].astype(jnp.int32) * 32 + leg[0, -1, feat // 2 :][:1].astype(jnp.int32)

    full = lax.all_gather(held, TP, axis=1, tiled=True)
    parts_mine, parts_theirs = attend(
        held_len,
        place,
        full,
        gain,
        w_qkv,
        rope_tables(held_len, new),
        kv_cache,
        w_out,
    )
    parts_theirs, pair_up = barrier((parts_theirs, pair_up))
    parts = (parts_mine.astype(f32) + swap_core(parts_theirs).astype(f32)).astype(bf16)
    parts, held_ids = barrier((parts, held_ids))
    parts = lax.all_to_all(parts, "zl", 0, 0, tiled=True)
    held_share = (held.astype(f32) + jnp.sum(parts.astype(f32), axis=0)).astype(bf16)

    slot_iota = jnp.arange(slots, dtype=jnp.int32)

    def chosen_of(ids, other):
        both = jnp.where(zh == 0, jnp.stack([ids, other]), jnp.stack([other, ids]))
        picks = both.reshape(2, TOPK * new)
        onehot = (picks[:, :, None] == jnp.arange(experts_all, dtype=jnp.int32)).astype(bf16)
        order = jnp.arange(TOPK * new, dtype=jnp.int32)
        before = (order[:, None] > order[None, :]).astype(bf16)
        earlier = jnp.einsum("pq,rqe->rpe", before, onehot, preferred_element_type=f32)
        rank = jnp.sum(earlier * onehot.astype(f32), axis=2).astype(jnp.int32)
        rank = rank - (zl % 2) * SHARE
        there = picks - zh * plane
        which = jnp.arange(2, dtype=jnp.int32)[:, None]
        slot = there * rows + which * SHARE + rank
        here = (there >= 0) & (there < plane) & (rank >= 0) & (rank < SHARE)
        slot = jnp.where(here, slot, -1).reshape(2, TOPK, new)
        token = jnp.arange(new, dtype=jnp.int32)[None, :]
        chunk = token // span - zh * plane
        common = chunk * rows + 2 * SHARE + which * span + token % span
        common = jnp.where((chunk >= 0) & (chunk < plane), common, -1)
        chosen = (common.reshape(1, 2 * new) == slot_iota[:, None]).astype(bf16)
        for pick in range(TOPK):
            at = slot[:, pick].reshape(1, 2 * new)
            chosen = chosen + (at == slot_iota[:, None]).astype(bf16)
        return chosen

    chosen_held = chosen_of(held_ids, column_swap(held_ids))
    chosen_own = chosen_of(ids_t, ids_there).T

    outgoing = dispatch(chosen_held, spread(held_share, Z, 8))
    down_w, outgoing = barrier((w_down, outgoing))
    rows_mine = lax.all_to_all(
        outgoing.reshape(plane, rows, half), ("x", "y"), 0, 0, tiled=True
    )
    pair_down = lax.ppermute(down_w, "zl", neighbours)

    rows_mine, pair_down = barrier((rows_mine, pair_down))
    rows_theirs = swap_core(rows_mine)
    served_mine, served_theirs = experts(
        place,
        rows_mine,
        rows_theirs,
        gain_ffn,
        w_router.T,
        w_in,
        w_down,
        pair_gate,
        pair_up,
        pair_down,
        w_sh_in.swapaxes(1, 2),
        w_sh_down,
    )
    served = (served_mine.astype(f32) + swap_core(served_theirs).astype(f32)).astype(bf16)
    served, hidden_late = barrier((served, hidden))
    returned = lax.all_to_all(served, ("x", "y"), 0, 0, tiled=True).reshape(slots, half)

    own_full = lax.all_gather(hidden_late, TP, axis=1, tiled=True)
    returned, own_full = barrier((returned, own_full))
    new_cache = new_kv(own_full, gain, w_qkv, rope_tables(lengths[0], new))[:, None]

    shares, last = combine(chosen_own, returned)
    out_hidden = lax.psum_scatter(shares, Z, scatter_dimension=0)
    last = finish(lax.all_to_all(last, Z, 0, 0, tiled=True), reqs)

    last_all = lax.all_to_all(last, ("core", "x", "y"), 0, 0, tiled=True)
    tops, rms = head(last_all, gain_final, w_head)
    last_rms = rms.reshape(reqs)
    top_logit = jnp.max(lax.all_to_all(tops, ALL, 0, 0, tiled=True), axis=0)
    return (out_hidden, new_cache, last_rms, top_logit)


def solution(mesh):
    fine = Mesh(mesh.devices.reshape(SIZES), ALL)
    return jax.shard_map(
        local,
        mesh=fine,
        in_specs=(
            P(REQ, TP),
            P(),
            P(None, None, TP),
            P(TP, None),
            P(None, REQ, None, TP),
            P(),
            P(REQ),
            P(),
            P(),
            P(REQ, None),
            P(REQ, None, None, TP),
            P(REQ, TP, None),
            P(None, None, TP),
            P(TP, None),
            P(),
            P(REQ + TP, None),
        ),
        out_specs=(P(REQ, TP), P(None, REQ, None, TP), P(), P()),
        check_vma=False,
    )
```

```python
import jax
import jax.numpy as jnp
from jax import lax
from jax.sharding import Mesh, PartitionSpec as P
from jax.experimental import pallas as pl
from jax.experimental.pallas import tpu as pltpu

HD = 128
TOPK = 6
CAP = 32
SHARE = CAP // 2

REQ = ("zh", "x", "y")
TP = ("zl", "core")
COL = ("zh", "zl", "core")
Z = ("zh", "zl")
ALL = ("zh", "x", "y", "zl", "core")
SIZES = (2, 4, 4, 4, 2)

epsilon = 1e-06
bf16 = jnp.bfloat16
f32 = jnp.float32


def rms_scale(values, gain):
    return (
        values
        * lax.rsqrt(jnp.mean(values * values, axis=-1, keepdims=True) + epsilon)
        * gain.astype(f32)
    )


def rope_tables(length, new):
    half_len = HD // 2
    freqs = 10000.0 ** (-2.0 * jnp.arange(half_len, dtype=f32) / HD)
    offsets = jnp.arange(new, dtype=jnp.int32).astype(f32)[:, None] * freqs[None, :]
    shift = length.astype(f32).reshape(1, 1) * freqs[None, :]
    return jnp.cos(offsets), jnp.sin(offsets), jnp.cos(shift), jnp.sin(shift)


def norm_rows(full_ref, gain_ref):
    return rms_scale(full_ref[...].astype(f32), gain_ref[...]).astype(bf16)


def rotate(values, cos_ref, sin_ref, cos_at_ref, sin_at_ref):
    cosine = cos_ref[...] * cos_at_ref[...] - sin_ref[...] * sin_at_ref[...]
    sine = sin_ref[...] * cos_at_ref[...] + cos_ref[...] * sin_at_ref[...]
    cosine = jnp.concatenate([cosine, cosine], axis=1)
    sine = jnp.concatenate([-sine, sine], axis=1)
    heads = []
    for head in range(values.shape[1] // HD):
        piece = values[:, head * HD : (head + 1) * HD]
        heads.append(piece * cosine + pltpu.roll(piece, HD // 2, 1) * sine)
    return jnp.concatenate(heads, axis=1).astype(bf16)


def new_kv_body(full_ref, gain_ref, w_ref, *refs):
    tables, o_ref = refs[:4], refs[4]
    normed = norm_rows(full_ref, gain_ref)
    keys = jnp.dot(normed, w_ref[1], preferred_element_type=f32)
    o_ref[0] = rotate(keys, *tables)
    o_ref[1] = jnp.dot(normed, w_ref[2], preferred_element_type=f32).astype(bf16)


def new_kv(full, gain, w_qkv, tables):
    vm = pl.BlockSpec(memory_space=pltpu.VMEM)
    return pl.pallas_call(
        new_kv_body,
        out_shape=jax.ShapeDtypeStruct((2, full.shape[0], w_qkv.shape[2]), bf16),
        in_specs=[vm] * 7,
        out_specs=vm,
        name="new_kv",
    )(full, gain, w_qkv, *tables)


def attend_body(
    len_ref, place_ref, full_ref, gain_ref, qkv_ref, cos_ref, sin_ref, cos_at_ref, sin_at_ref,
    kv_ref, w_ref, om_ref, ot_ref,
):
    tables = (cos_ref, sin_ref, cos_at_ref, sin_at_ref)
    length = len_ref[0]
    first = place_ref[0] == 0
    ctx = kv_ref.shape[2]
    new = full_ref.shape[0]
    normed = norm_rows(full_ref, gain_ref)
    q_all = rotate(jnp.dot(normed, qkv_ref[0], preferred_element_type=f32), *tables)
    k_all = rotate(jnp.dot(normed, qkv_ref[1], preferred_element_type=f32), *tables)
    v_all = jnp.dot(normed, qkv_ref[2], preferred_element_type=f32).astype(bf16)
    heads = []
    for head in range(q_all.shape[1] // HD):
        lanes = slice(head * HD, (head + 1) * HD)
        q = q_all[:, lanes]
        s_old = dot_nt(q, kv_ref[0, 0, :, lanes]) * HD ** (-0.5)
        s_new = dot_nt(q, k_all[:, lanes]) * HD ** (-0.5)
        seen_old = lax.broadcasted_iota(jnp.int32, (new, ctx), 1) < length
        seen_new = lax.broadcasted_iota(jnp.int32, (new, new), 1) <= lax.broadcasted_iota(
            jnp.int32, (new, new), 0
        )
        s_old = jnp.where(seen_old, s_old, -1e30)
        s_new = jnp.where(seen_new, s_new, -1e30)
        peak = jnp.maximum(
            jnp.max(s_old, axis=-1, keepdims=True), jnp.max(s_new, axis=-1, keepdims=True)
        )
        e_old = jnp.where(seen_old, jnp.exp(s_old - peak), 0.0)
        e_new = jnp.where(seen_new, jnp.exp(s_new - peak), 0.0)
        total = jnp.sum(e_old, axis=-1, keepdims=True) + jnp.sum(e_new, axis=-1, keepdims=True)
        w_old = (e_old / total).astype(bf16)
        w_new = (e_new / total).astype(bf16)
        out = jnp.dot(w_old, kv_ref[1, 0, :, lanes], preferred_element_type=f32) + jnp.dot(
            w_new, v_all[:, lanes], preferred_element_type=f32
        )
        heads.append(out.astype(bf16))
    attn = jnp.concatenate(heads, axis=1)
    wide = om_ref.shape[2]

    def store(even_ref, odd_ref):
        for part in range(2 * om_ref.shape[0]):
            ref = odd_ref if part % 2 else even_ref
            ref[part // 2] = jnp.dot(
                attn, w_ref[:, part * wide : (part + 1) * wide], preferred_element_type=f32
            ).astype(bf16)

    @pl.when(first)
    def _():
        store(om_ref, ot_ref)

    @pl.when(jnp.logical_not(first))
    def _():
        store(ot_ref, om_ref)


def attend(length, place, full, gain, w_qkv, tables, kv_cache, w_out):
    vm = pl.BlockSpec(memory_space=pltpu.VMEM)
    new = full.shape[0]
    feat = w_out.shape[0]
    shape = jax.ShapeDtypeStruct((w_out.shape[1] // feat // 2, new, feat), bf16)
    return pl.pallas_call(
        attend_body,
        out_shape=(shape, shape),
        in_specs=[pl.BlockSpec(memory_space=pltpu.SMEM)] * 2 + [vm] * 9,
        out_specs=(vm, vm),
        name="attend",
    )(length, place, full, gain, w_qkv, *tables, kv_cache, w_out)


def spread(value, axes, count):
    wide = jnp.broadcast_to(value[None], (count,) + value.shape)
    return lax.all_to_all(wide, axes, 0, 0, tiled=True)


def swap_core(value):
    return lax.ppermute(value, "core", [(0, 1), (1, 0)])


def column_swap(value):
    return lax.ppermute(value, "zh", [(0, 1), (1, 0)])


def dot_nt(a, b):
    return lax.dot_general(a, b, (((1,), (1,)), ((), ())), preferred_element_type=f32)


def expert_rows(rows, gate_w, up_w, down_w):
    gate = dot_nt(rows, gate_w)
    up = dot_nt(rows, up_w)
    inner = (gate / (1.0 + jnp.exp(-gate)) * up).astype(bf16)
    return jnp.dot(inner, down_w, preferred_element_type=f32)


def drain(first, out, mine_ref, theirs_ref):
    feat = out.shape[1] // 8

    def store(even_ref, odd_ref):
        for part in range(4):
            piece = slice(part * feat, (part + 1) * feat)
            even_ref[:, piece] = out[:, 2 * part * feat : (2 * part + 1) * feat]
            odd_ref[:, piece] = out[:, (2 * part + 1) * feat : (2 * part + 2) * feat]

    @pl.when(first)
    def _():
        store(mine_ref, theirs_ref)

    @pl.when(jnp.logical_not(first))
    def _():
        store(theirs_ref, mine_ref)


def experts_body(
    place_ref, a_ref, b_ref, gain_ref, router_ref, in_ref, down_ref, pg_ref, pu_ref, pd_ref,
    si_ref, sd_ref, om_ref, ot_ref, xr_ref, xs_ref, ys_ref,
):
    first = place_ref[0] == 0
    feat = xr_ref.shape[1] // 8
    chunks, span = a_ref.shape[:2]
    routed = xr_ref.shape[0] // chunks
    shared = span - routed

    def fill(even_ref, odd_ref):
        for chunk in range(chunks):
            for part in range(4):
                piece = slice(part * feat, (part + 1) * feat)
                for odd, ref in enumerate((even_ref, odd_ref)):
                    lanes = slice((2 * part + odd) * feat, (2 * part + odd + 1) * feat)
                    rows = ref[chunk, :, piece].astype(f32)
                    xr_ref[chunk * routed : (chunk + 1) * routed, lanes] = rows[:routed]
                    xs_ref[chunk * shared : (chunk + 1) * shared, lanes] = rows[routed:]

    @pl.when(first)
    def _():
        fill(a_ref, b_ref)

    @pl.when(jnp.logical_not(first))
    def _():
        fill(b_ref, a_ref)

    common = norm_rows(xs_ref, gain_ref)
    common = expert_rows(common, si_ref[0], si_ref[1], sd_ref[...])
    common = common + xs_ref[...] * 0.125
    half = shared // 2
    for piece in range(2 * chunks):
        ys_ref[piece, :half, :] = common[piece * half : (piece + 1) * half]

    rows = norm_rows(xr_ref, gain_ref)
    out = expert_rows(rows, in_ref[0], in_ref[1], down_ref[...])
    out = out + expert_rows(rows, pg_ref[...], pu_ref[...], pd_ref[...])
    logits = dot_nt(rows, router_ref[...])
    raised = jnp.exp(logits - jnp.max(logits, axis=-1, keepdims=True))
    own = lax.broadcasted_iota(jnp.int32, logits.shape, 1) == place_ref[1]
    picked = jnp.sum(jnp.where(own, raised, 0.0), axis=-1, keepdims=True)
    xr_ref[...] = out * (picked / jnp.sum(raised, axis=-1, keepdims=True))

    def store(even_ref, odd_ref):
        for chunk in range(chunks):
            origin = [place_ref[2 + 2 * chunk + zo] for zo in range(2)]
            size = routed // 2
            top = [xr_ref[pl.ds(pl.multiple_of(at * size, size), size), :] for at in origin]
            low = [ys_ref[at, :half, :] for at in origin]
            both = jnp.concatenate(top + low, axis=0).astype(bf16)
            for part in range(4):
                piece = slice(part * feat, (part + 1) * feat)
                even_ref[chunk, :, piece] = both[:, 2 * part * feat : (2 * part + 1) * feat]
                odd_ref[chunk, :, piece] = both[:, (2 * part + 1) * feat : (2 * part + 2) * feat]

    @pl.when(first)
    def _():
        store(om_ref, ot_ref)

    @pl.when(jnp.logical_not(first))
    def _():
        store(ot_ref, om_ref)


def experts(place, rows_mine, rows_theirs, *weights):
    vm = pl.BlockSpec(memory_space=pltpu.VMEM)
    count, span, half = rows_mine.shape
    width = 2 * half
    shape = jax.ShapeDtypeStruct(rows_mine.shape, bf16)
    shared = span - 2 * SHARE
    return pl.pallas_call(
        experts_body,
        out_shape=(shape, shape),
        in_specs=[pl.BlockSpec(memory_space=pltpu.SMEM)] + [vm] * (2 + len(weights)),
        out_specs=(vm, vm),
        scratch_shapes=[
            pltpu.VMEM((count * 2 * SHARE, width), f32),
            pltpu.VMEM((count * shared, width), f32),
            pltpu.VMEM((2 * count, 8, width), f32),
        ],
        cost_estimate=pl.CostEstimate(
            flops=6 * count * span * width * 352,
            transcendentals=count * span * 352,
            bytes_accessed=8 * count * span * half + 18 * width * 176,
        ),
        name="experts",
    )(place, rows_mine, rows_theirs, *weights)


def dispatch_body(chosen_ref, parts_ref, out_ref):
    feat = parts_ref.shape[2]
    for part in range(4):
        both = jnp.concatenate([parts_ref[part], parts_ref[4 + part]], axis=0)
        out_ref[:, part * feat : (part + 1) * feat] = jnp.dot(
            chosen_ref[...], both, preferred_element_type=f32
        ).astype(bf16)


def dispatch(chosen_t, parts):
    vm = pl.BlockSpec(memory_space=pltpu.VMEM)
    return pl.pallas_call(
        dispatch_body,
        out_shape=jax.ShapeDtypeStruct((chosen_t.shape[0], 4 * parts.shape[2]), bf16),
        in_specs=[vm, vm],
        out_specs=vm,
        name="dispatch",
    )(chosen_t, parts)


def combine_body(place_ref, chosen_ref, back_ref, keep_ref, send_ref, last_ref):
    zh = place_ref[0]
    zl = place_ref[1]
    feat = keep_ref.shape[2]
    new = chosen_ref.shape[0] // 2
    last = []
    for zo in range(2):
        total = jnp.dot(
            chosen_ref[zo * new : (zo + 1) * new, :], back_ref[...], preferred_element_type=f32
        )
        pieces = [total[:, part * feat : (part + 1) * feat] for part in range(4)]
        last += [piece[new - 1 :, :] for piece in pieces]

        def store(ref, pieces=pieces):
            for part in range(4):
                ref[jnp.bitwise_xor(zl, part)] = pieces[part].astype(bf16)

        @pl.when(zh == zo)
        def _(store=store):
            store(keep_ref)

        @pl.when(zh != zo)
        def _(store=store):
            store(send_ref)

    last = jnp.concatenate(last, axis=0).astype(bf16)
    for dest in range(8):
        last_ref[dest] = last


def combine(place, chosen, back):
    vm = pl.BlockSpec(memory_space=pltpu.VMEM)
    feat = back.shape[1] // 4
    shape = jax.ShapeDtypeStruct((4, chosen.shape[0] // 2, feat), bf16)
    return pl.pallas_call(
        combine_body,
        out_shape=(shape, shape, jax.ShapeDtypeStruct((8, 8, feat), bf16)),
        in_specs=[pl.BlockSpec(memory_space=pltpu.SMEM), vm, vm],
        out_specs=(vm, vm, vm),
        name="combine",
    )(place, chosen, back)


def finish_body(parts_ref, last_ref):
    feat = parts_ref.shape[2]
    total = jnp.sum(parts_ref[...].astype(f32), axis=0)
    last = total.astype(bf16).astype(f32)
    last = jnp.concatenate([last[:, : feat // 2], last[:, feat // 2 :]], axis=0).astype(bf16)
    last_ref[...] = jnp.broadcast_to(last[None], last_ref.shape)


def finish(parts, copies):
    vm = pl.BlockSpec(memory_space=pltpu.VMEM)
    return pl.pallas_call(
        finish_body,
        out_shape=jax.ShapeDtypeStruct((copies, 16, 128), bf16),
        in_specs=[vm],
        out_specs=vm,
        name="finish",
    )(parts)


def head_body(last_ref, gain_ref, w_ref, top_ref, rms_ref):
    plane = last_ref.shape[0] // 2
    rows = jnp.swapaxes(last_ref[...].astype(f32), 0, 1)
    halves = []
    for zo in range(2):
        pieces = []
        for part in range(4):
            for core in range(2):
                for sub in range(2):
                    pieces.append(
                        rows[sub * 8 + zo * 4 + part, core * plane : (core + 1) * plane]
                    )
        halves.append(jnp.concatenate(pieces, axis=1))
    tok = jnp.concatenate(halves, axis=0)
    rms = jnp.sqrt(jnp.mean(tok * tok, axis=-1, keepdims=True) + epsilon)
    head_in = (tok / rms * gain_ref[...].astype(f32)).astype(bf16)
    logits = lax.dot_general(
        w_ref[...], head_in, (((1,), (1,)), ((), ())), preferred_element_type=f32
    )
    top_ref[...] = jnp.broadcast_to(jnp.max(logits, axis=0, keepdims=True), top_ref.shape)
    rms_ref[...] = rms


def head(last, gain, w_head):
    vm = pl.BlockSpec(memory_space=pltpu.VMEM)
    rows = last.shape[0]
    return pl.pallas_call(
        head_body,
        out_shape=(
            jax.ShapeDtypeStruct((256, rows), f32),
            jax.ShapeDtypeStruct((rows, 1), f32),
        ),
        in_specs=[vm, vm, vm],
        out_specs=(vm, vm),
        name="head",
    )(last, gain, w_head)


def local(
    hidden,
    attn_gain,
    w_qkv,
    w_out,
    kv_cache,
    holder_slot,
    lengths,
    ffn_gain,
    w_router,
    expert_ids,
    w_exp_in,
    w_exp_down,
    w_sh_in,
    w_sh_down,
    final_gain,
    w_head,
):
    zh = lax.axis_index("zh")
    zl = lax.axis_index("zl")
    core = lax.axis_index("core")
    expert = lax.axis_index(REQ)
    new, feat = hidden.shape
    width = attn_gain.shape[0]
    half = width // 2
    experts_all = w_router.shape[1]
    plane = experts_all // 2
    reqs = holder_slot.shape[0]
    span = new // reqs
    rows = 2 * (SHARE + span)
    slots = plane * rows
    slot_at = holder_slot.reshape(2, plane).T.reshape(reqs)
    order = (slot_at % plane) * 2 + slot_at // plane
    place = jnp.concatenate([jnp.stack([core, expert]).astype(jnp.int32), order])
    barrier = lax.optimization_barrier

    ids_t = expert_ids.T
    sizes = jnp.concatenate(
        [jnp.broadcast_to(lengths // 32, (feat // 2,)), jnp.broadcast_to(lengths % 32, (feat // 2,))]
    )
    meta = jnp.concatenate([ids_t.reshape(TOPK * new // feat, feat), sizes[None]]).astype(bf16)
    meta = jnp.broadcast_to(meta[None], (reqs,) + meta.shape)
    chunks = jnp.concatenate([hidden.reshape(reqs, span, feat), meta], axis=1)
    w_in = w_exp_in[0].swapaxes(1, 2)
    w_down = w_exp_down[0]
    neighbours = [(0, 1), (1, 0), (2, 3), (3, 2)]
    pair_gate = lax.ppermute(w_in[0], "zl", neighbours)
    leg = lax.all_to_all(chunks, REQ, 0, 0, tiled=True)
    ids_there = column_swap(ids_t)


    req_iota = jnp.arange(reqs, dtype=jnp.int32)
    owner_of = jnp.sum(
        jnp.where(holder_slot[None, :] == req_iota[:, None], req_iota[None, :], 0), axis=1
    )
    leg = leg.at[owner_of].get(mode="promise_in_bounds")
    leg, up_w = barrier((leg, w_in[1]))
    pair_up = lax.ppermute(up_w, "zl", neighbours)
    leg = lax.all_to_all(leg, REQ, 0, 0, tiled=True)
    leg, pair_gate, gain, gain_ffn, gain_final, place = barrier(
        (leg, pair_gate, attn_gain[None], ffn_gain[None], final_gain[None], place)
    )
    held = leg[:, :span].reshape(new, feat)
    held_ids = leg[0, span:-1].reshape(TOPK, new).astype(jnp.int32)
    held_len = leg[0, -1, :1].astype(jnp.int32) * 32 + leg[0, -1, feat // 2 :][:1].astype(jnp.int32)

    full = lax.all_gather(held, TP, axis=1, tiled=True)
    parts_mine, parts_theirs = attend(
        held_len,
        place,
        full,
        gain,
        w_qkv,
        rope_tables(held_len, new),
        kv_cache,
        w_out,
    )
    parts_theirs, pair_up = barrier((parts_theirs, pair_up))
    parts = (parts_mine.astype(f32) + swap_core(parts_theirs).astype(f32)).astype(bf16)
    parts, held_ids = barrier((parts, held_ids))
    parts = lax.all_to_all(parts, "zl", 0, 0, tiled=True)
    held_share = (held.astype(f32) + jnp.sum(parts.astype(f32), axis=0)).astype(bf16)

    slot_iota = jnp.arange(slots, dtype=jnp.int32)

    def chosen_of(ids, other):
        both = jnp.where(zh == 0, jnp.stack([ids, other]), jnp.stack([other, ids]))
        picks = both.reshape(2, TOPK * new)
        onehot = (picks[:, :, None] == jnp.arange(experts_all, dtype=jnp.int32)).astype(bf16)
        order = jnp.arange(TOPK * new, dtype=jnp.int32)
        before = (order[:, None] > order[None, :]).astype(bf16)
        earlier = jnp.einsum("pq,rqe->rpe", before, onehot, preferred_element_type=f32)
        rank = jnp.sum(earlier * onehot.astype(f32), axis=2).astype(jnp.int32)
        rank = rank - (zl % 2) * SHARE
        there = picks - zh * plane
        which = jnp.arange(2, dtype=jnp.int32)[:, None]
        slot = there * rows + which * SHARE + rank
        here = (there >= 0) & (there < plane) & (rank >= 0) & (rank < SHARE)
        slot = jnp.where(here, slot, -1).reshape(2, TOPK, new)
        token = jnp.arange(new, dtype=jnp.int32)[None, :]
        chunk = token // span - zh * plane
        common = chunk * rows + 2 * SHARE + which * span + token % span
        common = jnp.where((chunk >= 0) & (chunk < plane), common, -1)
        chosen = (common.reshape(1, 2 * new) == slot_iota[:, None]).astype(bf16)
        for pick in range(TOPK):
            at = slot[:, pick].reshape(1, 2 * new)
            chosen = chosen + (at == slot_iota[:, None]).astype(bf16)
        return chosen

    chosen_held = chosen_of(held_ids, column_swap(held_ids))
    chosen_own = chosen_of(ids_t, ids_there).T

    outgoing = dispatch(chosen_held, spread(held_share, Z, 8))
    down_w, outgoing = barrier((w_down, outgoing))
    rows_mine = lax.all_to_all(
        outgoing.reshape(plane, rows, half), ("x", "y"), 0, 0, tiled=True
    )
    pair_down = lax.ppermute(down_w, "zl", neighbours)

    rows_mine, pair_down = barrier((rows_mine, pair_down))
    rows_theirs = swap_core(rows_mine)
    served_mine, served_theirs = experts(
        place,
        rows_mine,
        rows_theirs,
        gain_ffn,
        w_router.T,
        w_in,
        w_down,
        pair_gate,
        pair_up,
        pair_down,
        w_sh_in.swapaxes(1, 2),
        w_sh_down,
    )
    served = (served_mine.astype(f32) + swap_core(served_theirs).astype(f32)).astype(bf16)
    served, hidden_late = barrier((served, hidden))
    returned = lax.all_to_all(served, ("x", "y"), 0, 0, tiled=True).reshape(slots, half)

    own_full = lax.all_gather(hidden_late, TP, axis=1, tiled=True)
    returned, own_full = barrier((returned, own_full))
    new_cache = new_kv(own_full, gain, w_qkv, rope_tables(lengths[0], new))[:, None]

    keep, send, last = combine(jnp.stack([zh, zl]).astype(jnp.int32), chosen_own, returned)
    last = finish(lax.all_to_all(last, Z, 0, 0, tiled=True), reqs)

    def add(mine, theirs):
        return (mine.astype(f32) + theirs.astype(f32)).astype(bf16)

    keep = add(keep, column_swap(send))
    keep = add(keep[:2], lax.ppermute(keep[2:], "zl", [(0, 2), (1, 3), (2, 0), (3, 1)]))
    out_hidden = add(keep[0], lax.ppermute(keep[1], "zl", neighbours))

    last_all = lax.all_to_all(last, ("core", "x", "y"), 0, 0, tiled=True)
    tops, rms = head(last_all, gain_final, w_head)
    last_rms = rms.reshape(reqs)
    top_logit = jnp.max(lax.all_to_all(tops, ALL, 0, 0, tiled=True), axis=0)
    return (out_hidden, new_cache, last_rms, top_logit)


def solution(mesh):
    fine = Mesh(mesh.devices.reshape(SIZES), ALL)
    return jax.shard_map(
        local,
        mesh=fine,
        in_specs=(
            P(REQ, TP),
            P(),
            P(None, None, TP),
            P(TP, None),
            P(None, REQ, None, TP),
            P(),
            P(REQ),
            P(),
            P(),
            P(REQ, None),
            P(REQ, None, None, TP),
            P(REQ, TP, None),
            P(None, None, TP),
            P(TP, None),
            P(),
            P(REQ + TP, None),
        ),
        out_specs=(P(REQ, TP), P(None, REQ, None, TP), P(), P()),
        check_vma=False,
    )
```

```python
import jax
import jax.numpy as jnp
from jax import lax
from jax.sharding import Mesh, PartitionSpec as P
from jax.experimental import pallas as pl
from jax.experimental.pallas import tpu as pltpu

HD = 128
TOPK = 6
CAP = 32
SHARE = CAP // 2

REQ = ("zh", "x", "y")
TP = ("zl", "core")
COL = ("zh", "zl", "core")
Z = ("zh", "zl")
ALL = ("zh", "x", "y", "zl", "core")
SIZES = (2, 4, 4, 4, 2)

epsilon = 1e-06
bf16 = jnp.bfloat16
f32 = jnp.float32


def rms_scale(values, gain):
    return (
        values
        * lax.rsqrt(jnp.mean(values * values, axis=-1, keepdims=True) + epsilon)
        * gain.astype(f32)
    )


def rope_tables(length, new):
    half_len = HD // 2
    freqs = 10000.0 ** (-2.0 * jnp.arange(half_len, dtype=f32) / HD)
    offsets = jnp.arange(new, dtype=jnp.int32).astype(f32)[:, None] * freqs[None, :]
    shift = length.astype(f32).reshape(1, 1) * freqs[None, :]
    return jnp.cos(offsets), jnp.sin(offsets), jnp.cos(shift), jnp.sin(shift)


def norm_rows(full_ref, gain_ref):
    return rms_scale(full_ref[...].astype(f32), gain_ref[...]).astype(bf16)


def rotate(values, cos_ref, sin_ref, cos_at_ref, sin_at_ref):
    cosine = cos_ref[...] * cos_at_ref[...] - sin_ref[...] * sin_at_ref[...]
    sine = sin_ref[...] * cos_at_ref[...] + cos_ref[...] * sin_at_ref[...]
    cosine = jnp.concatenate([cosine, cosine], axis=1)
    sine = jnp.concatenate([-sine, sine], axis=1)
    heads = []
    for head in range(values.shape[1] // HD):
        piece = values[:, head * HD : (head + 1) * HD]
        heads.append(piece * cosine + pltpu.roll(piece, HD // 2, 1) * sine)
    return jnp.concatenate(heads, axis=1).astype(bf16)


def new_kv_body(full_ref, gain_ref, w_ref, *refs):
    tables, o_ref = refs[:4], refs[4]
    normed = norm_rows(full_ref, gain_ref)
    keys = jnp.dot(normed, w_ref[1], preferred_element_type=f32)
    o_ref[0] = rotate(keys, *tables)
    o_ref[1] = jnp.dot(normed, w_ref[2], preferred_element_type=f32).astype(bf16)


def new_kv(full, gain, w_qkv, tables):
    vm = pl.BlockSpec(memory_space=pltpu.VMEM)
    return pl.pallas_call(
        new_kv_body,
        out_shape=jax.ShapeDtypeStruct((2, full.shape[0], w_qkv.shape[2]), bf16),
        in_specs=[vm] * 7,
        out_specs=vm,
        name="new_kv",
    )(full, gain, w_qkv, *tables)


def attend_body(
    len_ref, place_ref, full_ref, gain_ref, qkv_ref, cos_ref, sin_ref, cos_at_ref, sin_at_ref,
    kv_ref, w_ref, om_ref, ot_ref,
):
    tables = (cos_ref, sin_ref, cos_at_ref, sin_at_ref)
    length = len_ref[0]
    first = place_ref[0] == 0
    ctx = kv_ref.shape[2]
    new = full_ref.shape[0]
    normed = norm_rows(full_ref, gain_ref)
    q_all = rotate(jnp.dot(normed, qkv_ref[0], preferred_element_type=f32), *tables)
    k_all = rotate(jnp.dot(normed, qkv_ref[1], preferred_element_type=f32), *tables)
    v_all = jnp.dot(normed, qkv_ref[2], preferred_element_type=f32).astype(bf16)
    heads = []
    for head in range(q_all.shape[1] // HD):
        lanes = slice(head * HD, (head + 1) * HD)
        q = q_all[:, lanes]
        s_old = dot_nt(q, kv_ref[0, 0, :, lanes]) * HD ** (-0.5)
        s_new = dot_nt(q, k_all[:, lanes]) * HD ** (-0.5)
        seen_old = lax.broadcasted_iota(jnp.int32, (new, ctx), 1) < length
        seen_new = lax.broadcasted_iota(jnp.int32, (new, new), 1) <= lax.broadcasted_iota(
            jnp.int32, (new, new), 0
        )
        s_old = jnp.where(seen_old, s_old, -1e30)
        s_new = jnp.where(seen_new, s_new, -1e30)
        peak = jnp.maximum(
            jnp.max(s_old, axis=-1, keepdims=True), jnp.max(s_new, axis=-1, keepdims=True)
        )
        e_old = jnp.where(seen_old, jnp.exp(s_old - peak), 0.0)
        e_new = jnp.where(seen_new, jnp.exp(s_new - peak), 0.0)
        total = jnp.sum(e_old, axis=-1, keepdims=True) + jnp.sum(e_new, axis=-1, keepdims=True)
        w_old = (e_old / total).astype(bf16)
        w_new = (e_new / total).astype(bf16)
        out = jnp.dot(w_old, kv_ref[1, 0, :, lanes], preferred_element_type=f32) + jnp.dot(
            w_new, v_all[:, lanes], preferred_element_type=f32
        )
        heads.append(out.astype(bf16))
    attn = jnp.concatenate(heads, axis=1)
    wide = om_ref.shape[2]

    def store(even_ref, odd_ref):
        for part in range(2 * om_ref.shape[0]):
            ref = odd_ref if part % 2 else even_ref
            ref[part // 2] = jnp.dot(
                attn, w_ref[:, part * wide : (part + 1) * wide], preferred_element_type=f32
            ).astype(bf16)

    @pl.when(first)
    def _():
        store(om_ref, ot_ref)

    @pl.when(jnp.logical_not(first))
    def _():
        store(ot_ref, om_ref)


def attend(length, place, full, gain, w_qkv, tables, kv_cache, w_out):
    vm = pl.BlockSpec(memory_space=pltpu.VMEM)
    new = full.shape[0]
    feat = w_out.shape[0]
    shape = jax.ShapeDtypeStruct((w_out.shape[1] // feat // 2, new, feat), bf16)
    return pl.pallas_call(
        attend_body,
        out_shape=(shape, shape),
        in_specs=[pl.BlockSpec(memory_space=pltpu.SMEM)] * 2 + [vm] * 9,
        out_specs=(vm, vm),
        name="attend",
    )(length, place, full, gain, w_qkv, *tables, kv_cache, w_out)


def spread(value, axes, count):
    wide = jnp.broadcast_to(value[None], (count,) + value.shape)
    return lax.all_to_all(wide, axes, 0, 0, tiled=True)


def swap_core(value):
    return lax.ppermute(value, "core", [(0, 1), (1, 0)])


def column_swap(value):
    return lax.ppermute(value, "zh", [(0, 1), (1, 0)])


def dot_nt(a, b):
    return lax.dot_general(a, b, (((1,), (1,)), ((), ())), preferred_element_type=f32)


def expert_rows(rows, gate_w, up_w, down_w):
    gate = dot_nt(rows, gate_w)
    up = dot_nt(rows, up_w)
    inner = (gate / (1.0 + jnp.exp(-gate)) * up).astype(bf16)
    return jnp.dot(inner, down_w, preferred_element_type=f32)


def drain(first, out, mine_ref, theirs_ref):
    feat = out.shape[1] // 8

    def store(even_ref, odd_ref):
        for part in range(4):
            piece = slice(part * feat, (part + 1) * feat)
            even_ref[:, piece] = out[:, 2 * part * feat : (2 * part + 1) * feat]
            odd_ref[:, piece] = out[:, (2 * part + 1) * feat : (2 * part + 2) * feat]

    @pl.when(first)
    def _():
        store(mine_ref, theirs_ref)

    @pl.when(jnp.logical_not(first))
    def _():
        store(theirs_ref, mine_ref)


def experts_body(
    place_ref, a_ref, b_ref, gain_ref, router_ref, in_ref, down_ref, pg_ref, pu_ref, pd_ref,
    si_ref, sd_ref, om_ref, ot_ref, xr_ref, xs_ref, ys_ref,
):
    first = place_ref[0] == 0
    feat = xr_ref.shape[1] // 8
    chunks, span = a_ref.shape[:2]
    routed = xr_ref.shape[0] // chunks
    shared = span - routed

    def fill(even_ref, odd_ref):
        for chunk in range(chunks):
            for part in range(4):
                piece = slice(part * feat, (part + 1) * feat)
                for odd, ref in enumerate((even_ref, odd_ref)):
                    lanes = slice((2 * part + odd) * feat, (2 * part + odd + 1) * feat)
                    rows = ref[chunk, :, piece].astype(f32)
                    xr_ref[chunk * routed : (chunk + 1) * routed, lanes] = rows[:routed]
                    xs_ref[chunk * shared : (chunk + 1) * shared, lanes] = rows[routed:]

    @pl.when(first)
    def _():
        fill(a_ref, b_ref)

    @pl.when(jnp.logical_not(first))
    def _():
        fill(b_ref, a_ref)

    common = norm_rows(xs_ref, gain_ref)
    common = expert_rows(common, si_ref[0], si_ref[1], sd_ref[...])
    common = common + xs_ref[...] * 0.125
    half = shared // 2
    for piece in range(2 * chunks):
        ys_ref[piece, :half, :] = common[piece * half : (piece + 1) * half]

    rows = norm_rows(xr_ref, gain_ref)
    out = expert_rows(rows, in_ref[0], in_ref[1], down_ref[...])
    out = out + expert_rows(rows, pg_ref[...], pu_ref[...], pd_ref[...])
    logits = dot_nt(rows, router_ref[...])
    raised = jnp.exp(logits - jnp.max(logits, axis=-1, keepdims=True))
    own = lax.broadcasted_iota(jnp.int32, logits.shape, 1) == place_ref[1]
    picked = jnp.sum(jnp.where(own, raised, 0.0), axis=-1, keepdims=True)
    xr_ref[...] = out * (picked / jnp.sum(raised, axis=-1, keepdims=True))

    def store(even_ref, odd_ref):
        for chunk in range(chunks):
            origin = [place_ref[2 + 2 * chunk + zo] for zo in range(2)]
            size = routed // 2
            top = [xr_ref[pl.ds(pl.multiple_of(at * size, size), size), :] for at in origin]
            low = [ys_ref[at, :half, :] for at in origin]
            both = jnp.concatenate(top + low, axis=0).astype(bf16)
            for part in range(4):
                piece = slice(part * feat, (part + 1) * feat)
                even_ref[chunk, :, piece] = both[:, 2 * part * feat : (2 * part + 1) * feat]
                odd_ref[chunk, :, piece] = both[:, (2 * part + 1) * feat : (2 * part + 2) * feat]

    @pl.when(first)
    def _():
        store(om_ref, ot_ref)

    @pl.when(jnp.logical_not(first))
    def _():
        store(ot_ref, om_ref)


def experts(place, rows_mine, rows_theirs, *weights):
    vm = pl.BlockSpec(memory_space=pltpu.VMEM)
    count, span, half = rows_mine.shape
    width = 2 * half
    shape = jax.ShapeDtypeStruct(rows_mine.shape, bf16)
    shared = span - 2 * SHARE
    return pl.pallas_call(
        experts_body,
        out_shape=(shape, shape),
        in_specs=[pl.BlockSpec(memory_space=pltpu.SMEM)] + [vm] * (2 + len(weights)),
        out_specs=(vm, vm),
        scratch_shapes=[
            pltpu.VMEM((count * 2 * SHARE, width), f32),
            pltpu.VMEM((count * shared, width), f32),
            pltpu.VMEM((2 * count, 8, width), f32),
        ],
        cost_estimate=pl.CostEstimate(
            flops=6 * count * span * width * 352,
            transcendentals=count * span * 352,
            bytes_accessed=8 * count * span * half + 18 * width * 176,
        ),
        name="experts",
    )(place, rows_mine, rows_theirs, *weights)


def dispatch_body(chosen_ref, parts_ref, out_ref):
    feat = parts_ref.shape[2]
    for part in range(4):
        both = jnp.concatenate([parts_ref[part], parts_ref[4 + part]], axis=0)
        out_ref[:, part * feat : (part + 1) * feat] = jnp.dot(
            chosen_ref[...], both, preferred_element_type=f32
        ).astype(bf16)


def dispatch(chosen_t, parts):
    vm = pl.BlockSpec(memory_space=pltpu.VMEM)
    return pl.pallas_call(
        dispatch_body,
        out_shape=jax.ShapeDtypeStruct((chosen_t.shape[0], 4 * parts.shape[2]), bf16),
        in_specs=[vm, vm],
        out_specs=vm,
        name="dispatch",
    )(chosen_t, parts)


def combine_body(place_ref, chosen_ref, back_ref, keep_ref, send_ref, last_ref):
    zh = place_ref[0]
    zl = place_ref[1]
    feat = keep_ref.shape[2]
    new = chosen_ref.shape[0] // 2
    last = []
    for zo in range(2):
        total = jnp.dot(
            chosen_ref[zo * new : (zo + 1) * new, :], back_ref[...], preferred_element_type=f32
        )
        pieces = [total[:, part * feat : (part + 1) * feat] for part in range(4)]
        last += [piece[new - 1 :, :] for piece in pieces]

        def store(ref, pieces=pieces):
            for part in range(4):
                ref[jnp.bitwise_xor(zl, part)] = pieces[part].astype(bf16)

        @pl.when(zh == zo)
        def _(store=store):
            store(keep_ref)

        @pl.when(zh != zo)
        def _(store=store):
            store(send_ref)

    last = jnp.concatenate(last, axis=0).astype(bf16)
    for dest in range(8):
        last_ref[dest] = last


def combine(place, chosen, back):
    vm = pl.BlockSpec(memory_space=pltpu.VMEM)
    feat = back.shape[1] // 4
    shape = jax.ShapeDtypeStruct((4, chosen.shape[0] // 2, feat), bf16)
    return pl.pallas_call(
        combine_body,
        out_shape=(shape, shape, jax.ShapeDtypeStruct((8, 8, feat), bf16)),
        in_specs=[pl.BlockSpec(memory_space=pltpu.SMEM), vm, vm],
        out_specs=(vm, vm, vm),
        name="combine",
    )(place, chosen, back)


def finish_body(parts_ref, last_ref):
    feat = parts_ref.shape[2]
    total = jnp.sum(parts_ref[...].astype(f32), axis=0)
    last = total.astype(bf16).astype(f32)
    last = jnp.concatenate([last[:, : feat // 2], last[:, feat // 2 :]], axis=0).astype(bf16)
    last_ref[...] = jnp.broadcast_to(last[None], last_ref.shape)


def finish(parts, copies):
    vm = pl.BlockSpec(memory_space=pltpu.VMEM)
    return pl.pallas_call(
        finish_body,
        out_shape=jax.ShapeDtypeStruct((copies, 16, 128), bf16),
        in_specs=[vm],
        out_specs=vm,
        name="finish",
    )(parts)


def head_body(last_ref, gain_ref, w_ref, top_ref, rms_ref):
    plane = last_ref.shape[0] // 2
    rows = jnp.swapaxes(last_ref[...].astype(f32), 0, 1)
    halves = []
    for zo in range(2):
        pieces = []
        for part in range(4):
            for core in range(2):
                for sub in range(2):
                    pieces.append(
                        rows[sub * 8 + zo * 4 + part, core * plane : (core + 1) * plane]
                    )
        halves.append(jnp.concatenate(pieces, axis=1))
    tok = jnp.concatenate(halves, axis=0)
    rms = jnp.sqrt(jnp.mean(tok * tok, axis=-1, keepdims=True) + epsilon)
    head_in = (tok / rms * gain_ref[...].astype(f32)).astype(bf16)
    logits = lax.dot_general(
        w_ref[...], head_in, (((1,), (1,)), ((), ())), preferred_element_type=f32
    )
    top_ref[...] = jnp.broadcast_to(jnp.max(logits, axis=0, keepdims=True), top_ref.shape)
    rms_ref[...] = rms


def head(last, gain, w_head):
    vm = pl.BlockSpec(memory_space=pltpu.VMEM)
    rows = last.shape[0]
    return pl.pallas_call(
        head_body,
        out_shape=(
            jax.ShapeDtypeStruct((256, rows), f32),
            jax.ShapeDtypeStruct((rows, 1), f32),
        ),
        in_specs=[vm, vm, vm],
        out_specs=(vm, vm),
        name="head",
    )(last, gain, w_head)


def local(
    hidden,
    attn_gain,
    w_qkv,
    w_out,
    kv_cache,
    holder_slot,
    lengths,
    ffn_gain,
    w_router,
    expert_ids,
    w_exp_in,
    w_exp_down,
    w_sh_in,
    w_sh_down,
    final_gain,
    w_head,
):
    zh = lax.axis_index("zh")
    zl = lax.axis_index("zl")
    core = lax.axis_index("core")
    expert = lax.axis_index(REQ)
    new, feat = hidden.shape
    width = attn_gain.shape[0]
    half = width // 2
    experts_all = w_router.shape[1]
    plane = experts_all // 2
    reqs = holder_slot.shape[0]
    span = new // reqs
    rows = 2 * (SHARE + span)
    slots = plane * rows
    slot_at = holder_slot.reshape(2, plane).T.reshape(reqs)
    order = (slot_at % plane) * 2 + slot_at // plane
    place = jnp.concatenate([jnp.stack([core, expert]).astype(jnp.int32), order])
    barrier = lax.optimization_barrier

    ids_t = expert_ids.T
    sizes = jnp.concatenate(
        [jnp.broadcast_to(lengths // 32, (feat // 2,)), jnp.broadcast_to(lengths % 32, (feat // 2,))]
    )
    meta = jnp.concatenate([ids_t.reshape(TOPK * new // feat, feat), sizes[None]]).astype(bf16)
    meta = jnp.broadcast_to(meta[None], (reqs,) + meta.shape)
    chunks = jnp.concatenate([hidden.reshape(reqs, span, feat), meta], axis=1)
    w_in = w_exp_in[0].swapaxes(1, 2)
    w_down = w_exp_down[0]
    neighbours = [(0, 1), (1, 0), (2, 3), (3, 2)]
    pair_gate = lax.ppermute(w_in[0], "zl", neighbours)
    leg = lax.all_to_all(chunks, REQ, 0, 0, tiled=True)
    ids_there = column_swap(ids_t)


    req_iota = jnp.arange(reqs, dtype=jnp.int32)
    owner_of = jnp.sum(
        jnp.where(holder_slot[None, :] == req_iota[:, None], req_iota[None, :], 0), axis=1
    )
    leg = leg.at[owner_of].get(mode="promise_in_bounds")
    leg, up_w = barrier((leg, w_in[1]))
    pair_up = lax.ppermute(up_w, "zl", neighbours)
    leg = lax.all_to_all(leg, REQ, 0, 0, tiled=True)
    leg, pair_gate, gain, gain_ffn, gain_final, place = barrier(
        (leg, pair_gate, attn_gain[None], ffn_gain[None], final_gain[None], place)
    )
    held = leg[:, :span].reshape(new, feat)
    held_ids = leg[0, span:-1].reshape(TOPK, new).astype(jnp.int32)
    held_len = leg[0, -1, :1].astype(jnp.int32) * 32 + leg[0, -1, feat // 2 :][:1].astype(jnp.int32)

    full = lax.all_gather(held, TP, axis=1, tiled=True)
    parts_mine, parts_theirs = attend(
        held_len,
        place,
        full,
        gain,
        w_qkv,
        rope_tables(held_len, new),
        kv_cache,
        w_out,
    )
    parts_theirs, pair_up = barrier((parts_theirs, pair_up))
    parts = (parts_mine.astype(f32) + swap_core(parts_theirs).astype(f32)).astype(bf16)
    parts, held_ids = barrier((parts, held_ids))
    parts = lax.all_to_all(parts, "zl", 0, 0, tiled=True)
    held_share = (held.astype(f32) + jnp.sum(parts.astype(f32), axis=0)).astype(bf16)

    slot_iota = jnp.arange(slots, dtype=jnp.int32)

    def chosen_of(ids, other):
        both = jnp.where(zh == 0, jnp.stack([ids, other]), jnp.stack([other, ids]))
        picks = both.reshape(2, TOPK * new)
        onehot = (picks[:, :, None] == jnp.arange(experts_all, dtype=jnp.int32)).astype(bf16)
        order = jnp.arange(TOPK * new, dtype=jnp.int32)
        before = (order[:, None] > order[None, :]).astype(bf16)
        earlier = jnp.einsum("pq,rqe->rpe", before, onehot, preferred_element_type=f32)
        rank = jnp.sum(earlier * onehot.astype(f32), axis=2).astype(jnp.int32)
        rank = rank - (zl % 2) * SHARE
        there = picks - zh * plane
        which = jnp.arange(2, dtype=jnp.int32)[:, None]
        slot = there * rows + which * SHARE + rank
        here = (there >= 0) & (there < plane) & (rank >= 0) & (rank < SHARE)
        slot = jnp.where(here, slot, -1).reshape(2, TOPK, new)
        token = jnp.arange(new, dtype=jnp.int32)[None, :]
        chunk = token // span - zh * plane
        common = chunk * rows + 2 * SHARE + which * span + token % span
        common = jnp.where((chunk >= 0) & (chunk < plane), common, -1)
        chosen = (common.reshape(1, 2 * new) == slot_iota[:, None]).astype(bf16)
        for pick in range(TOPK):
            at = slot[:, pick].reshape(1, 2 * new)
            chosen = chosen + (at == slot_iota[:, None]).astype(bf16)
        return chosen

    chosen_held = chosen_of(held_ids, column_swap(held_ids))
    chosen_own = chosen_of(ids_t, ids_there).T

    outgoing = dispatch(chosen_held, spread(held_share, Z, 8))
    down_w, outgoing = barrier((w_down, outgoing))
    rows_mine = lax.all_to_all(
        outgoing.reshape(plane, rows, half), ("x", "y"), 0, 0, tiled=True
    )
    pair_down = lax.ppermute(down_w, "zl", neighbours)

    rows_mine, pair_down = barrier((rows_mine, pair_down))
    rows_theirs = swap_core(rows_mine)
    served_mine, served_theirs = experts(
        place,
        rows_mine,
        rows_theirs,
        gain_ffn,
        w_router.T,
        w_in,
        w_down,
        pair_gate,
        pair_up,
        pair_down,
        w_sh_in.swapaxes(1, 2),
        w_sh_down,
    )
    served = (served_mine.astype(f32) + swap_core(served_theirs).astype(f32)).astype(bf16)
    served, hidden_late = barrier((served, hidden))
    returned = lax.all_to_all(served, ("x", "y"), 0, 0, tiled=True).reshape(slots, half)

    own_full = lax.all_gather(hidden_late, TP, axis=1, tiled=True)
    returned, own_full = barrier((returned, own_full))
    new_cache = new_kv(own_full, gain, w_qkv, rope_tables(lengths[0], new))[:, None]

    keep, send, last = combine(jnp.stack([zh, zl]).astype(jnp.int32), chosen_own, returned)
    last, send = barrier((lax.all_to_all(last, Z, 0, 0, tiled=True), send))
    last = finish(last, reqs)

    def add(mine, theirs):
        return (mine.astype(f32) + theirs.astype(f32)).astype(bf16)

    keep = add(keep, column_swap(send))
    keep = add(keep[:2], lax.ppermute(keep[2:], "zl", [(0, 2), (1, 3), (2, 0), (3, 1)]))
    out_hidden = add(keep[0], lax.ppermute(keep[1], "zl", neighbours))

    last_all = lax.all_to_all(last, ("core", "x", "y"), 0, 0, tiled=True)
    tops, rms = head(last_all, gain_final, w_head)
    last_rms = rms.reshape(reqs)
    top_logit = jnp.max(lax.all_to_all(tops, ALL, 0, 0, tiled=True), axis=0)
    return (out_hidden, new_cache, last_rms, top_logit)


def solution(mesh):
    fine = Mesh(mesh.devices.reshape(SIZES), ALL)
    return jax.shard_map(
        local,
        mesh=fine,
        in_specs=(
            P(REQ, TP),
            P(),
            P(None, None, TP),
            P(TP, None),
            P(None, REQ, None, TP),
            P(),
            P(REQ),
            P(),
            P(),
            P(REQ, None),
            P(REQ, None, None, TP),
            P(REQ, TP, None),
            P(None, None, TP),
            P(TP, None),
            P(),
            P(REQ + TP, None),
        ),
        out_specs=(P(REQ, TP), P(None, REQ, None, TP), P(), P()),
        check_vma=False,
    )
```
